256 devices in a mesh: lon: 32 (over x_lo, z, core), lat: 8 (over y, x_hi).
Axes of the slice: x: 4 (x_hi: 2, x_lo: 2; x = x_hi * 2 + x_lo), y: 4, z: 8, core: 2. Of those that a mesh axis runs over, the one named last changes fastest.
Arguments:
- heat_anomaly: float32 [16, 256, 4096], P(None, 'lat', 'lon'), may hold values from -11 to 11
- saltiness_anomaly: float32 [16, 256, 4096], P(None, 'lat', 'lon'), may hold values from -3 to 3
- zonal_stability_ratio: float32 [16, 256, 4096], P(None, 'lat', 'lon'), may hold values from -0.4 to 0.4
- meridional_stability_ratio: float32 [16, 256, 4096], P(None, 'lat', 'lon'), may hold values from -0.4 to 0.4
- ocean_layer_count: int32 [256, 4096], P('lat', 'lon'), may hold values from 0 to 16
Outputs:
- temperature_next: float32 [16, 256, 4096], P(None, 'lat', 'lon')
- salinity_next: float32 [16, 256, 4096], P(None, 'lat', 'lon')
The draws below stay inside these ranges and needn't reach their ends.
All inputs are finite; a program needn't handle non-finite values.
Results may differ from the reference program's by a relative error of at most 0.0003.
Values sent between devices are 32-bit elements; how exact they have to be, the bound alone decides.
A program may use at most 64 MiB of HBM per device.

```python
import jax
import jax.numpy as jnp
from jax import lax

K = 16
NJ = 256
NI = 4096
N_LAT = 8


def draw_heat_anomaly(key, part):
    level = (jnp.arange(K, dtype=jnp.float32) + 0.5) / K
    profile = (8.0 * (1.0 - 2.0 * level))[:, None, None]
    noise = 0.7 * jnp.clip(jax.random.normal(key, (K, NJ, NI), jnp.float32), -4.0, 4.0)
    return profile + noise


def draw_saltiness_anomaly(key, part):
    level = (jnp.arange(K, dtype=jnp.float32) + 0.5) / K
    profile = (1.6 * (2.0 * level - 1.0))[:, None, None]
    noise = 0.25 * jnp.clip(jax.random.normal(key, (K, NJ, NI), jnp.float32), -4.0, 4.0)
    return profile + noise


def set_ends(entries, own_key, least, largest):
    extent = entries.shape
    spot = [jax.random.randint(jax.random.fold_in(own_key, axis), (), 0, extent[axis]) for axis in range(len(extent))]
    entries = entries.at[tuple(spot)].set(least)
    longest = extent.index(max(extent))
    spot[longest] = (spot[longest] + 1) % extent[longest]
    return entries.at[tuple(spot)].set(largest)


def steps_of(key, extent, shards, least, top_value):
    level, own = 1.0, jax.random.fold_in(key, 6)
    for position, shards_of in shards:
        heights = jnp.exp(jax.random.uniform(jax.random.fold_in(own, position), (shards_of,), jnp.float32, least / len(shards), top_value / len(shards)))
        level = level * jnp.repeat(heights, extent[position] // shards_of).reshape([-1 if axis == position else 1 for axis in range(len(extent))])
    return level


def setup_inputs(seed: int = 0) -> dict:
    arg_keys = jax.random.split(jax.random.key(seed), 6)
    return {
        "heat_anomaly": draw_heat_anomaly(jax.random.fold_in(arg_keys[5], 71), 0),
        "saltiness_anomaly": draw_saltiness_anomaly(jax.random.fold_in(arg_keys[5], 71), 0),
        "zonal_stability_ratio": jnp.clip(jax.random.uniform(arg_keys[2], (K, NJ, NI), jnp.float32, -0.4, 0.4) * steps_of(arg_keys[2], (K, NJ, NI), ((1, 8), (2, 32)), -0.4, 0.0), -0.4, 0.4),
        "meridional_stability_ratio": jnp.clip(jax.random.uniform(arg_keys[3], (K, NJ, NI), jnp.float32, -0.4, 0.4) * steps_of(arg_keys[3], (K, NJ, NI), ((1, 8), (2, 32)), -0.4, 0.0), -0.4, 0.4),
        "ocean_layer_count": set_ends(jax.random.randint(arg_keys[4], (NJ, NI), 0, K + 1), jax.random.fold_in(arg_keys[4], 1), 0, K).astype(jnp.int32),
    }


heat_swelling_alpha = 0.1655
coef_beta = 0.76554
cabbeling_parameter = 0.05952
lambda_salt = 0.00054914
thermobaric_parameter = 0.0001497
press_salt = 0.00001109
cross_coupling_contribution = 0.0024341
total_depth = 5000.0
kappa_iso = 0.1
slope_max = 1.0
strat_min = 0.1


def minmod(former, second):
    return jnp.where(former * second > 0.0, jnp.sign(former) * jnp.minimum(jnp.abs(former), jnp.abs(second)), 0.0)


def seawater_heaviness(heat_anomaly, saltiness_anomaly, seafloor_distances):
    return (-heat_swelling_alpha * (1.0 + 0.5 * cabbeling_parameter * heat_anomaly + thermobaric_parameter * seafloor_distances) * heat_anomaly
            + coef_beta * (1.0 - 0.5 * lambda_salt * saltiness_anomaly - press_salt * seafloor_distances) * saltiness_anomaly
            - cross_coupling_contribution * heat_anomaly * saltiness_anomaly)


def vertical_diff(field):
    along = field.ndim - 3
    layer_stack_sum = field.shape[along]
    top_part = lax.slice_in_dim(field, 1, 2, axis=along) - lax.slice_in_dim(field, 0, 1, axis=along)
    middle = 0.5 * (lax.slice_in_dim(field, 2, layer_stack_sum, axis=along) - lax.slice_in_dim(field, 0, layer_stack_sum - 2, axis=along))
    bottom = lax.slice_in_dim(field, layer_stack_sum - 1, layer_stack_sum, axis=along) - lax.slice_in_dim(field, layer_stack_sum - 2, layer_stack_sum - 1, axis=along)
    return jnp.concatenate([top_part, middle, bottom], axis=along)


def face_flux(tracers, tracer_vert, rho_field, rho_vert, ocean_presence_flags, face_speed, along):
    def window(array, lower, upper):
        axis_pos = array.ndim + along
        return lax.slice_in_dim(array, lower, array.shape[axis_pos] - upper, axis=axis_pos)

    wet_face = window(ocean_presence_flags, 0, 1) * window(ocean_presence_flags, 1, 0)
    masked_step = wet_face * (window(tracers, 1, 0) - window(tracers, 0, 1))
    step_back = window(masked_step, 0, 2)
    step_here = window(masked_step, 1, 1)
    step_ahead = window(masked_step, 2, 0)
    cell_left = window(tracers, 1, 2)
    cell_right = window(tracers, 2, 1)
    face_wet = window(wet_face, 1, 1)
    positive = jnp.maximum(face_speed, 0.0)
    negative = jnp.minimum(face_speed, 0.0)
    advective = face_wet * (positive * (cell_left + 0.5 * (1.0 - face_speed) * minmod(step_back, step_here))
                            + negative * (cell_right - 0.5 * (1.0 + face_speed) * minmod(step_ahead, step_here)))
    rho_step = window(rho_field, 2, 1) - window(rho_field, 1, 2)
    strat_face = jnp.maximum(0.5 * (window(rho_vert, 1, 2) + window(rho_vert, 2, 1)), strat_min)
    slope_face = jnp.clip(-rho_step / strat_face, -slope_max, slope_max)
    vert_face = 0.5 * (window(tracer_vert, 1, 2) + window(tracer_vert, 2, 1))
    isoneutral = -kappa_iso * face_wet * (cell_right - cell_left + slope_face * vert_face)
    flux_total = advective + isoneutral
    return window(flux_total, 0, 1) - window(flux_total, 1, 0)


def stencil(padded, east_cols, north_rows):
    layer_stack_sum = padded.shape[1]
    depth_levels = total_depth * (lax.broadcasted_iota(jnp.float32, (layer_stack_sum, 1, 1), 0) + 0.5) / layer_stack_sum
    tracers = padded[:2]
    ocean_presence_flags = padded[2]
    rho_field = seawater_heaviness(padded[0], padded[1], depth_levels)
    rho_vert = vertical_diff(rho_field)
    tracer_vert = vertical_diff(tracers)
    along_x = face_flux(tracers[:, :, 2:-2, :], tracer_vert[:, :, 2:-2, :], rho_field[:, 2:-2, :],
                        rho_vert[:, 2:-2, :], ocean_presence_flags[:, 2:-2, :], east_cols, -1)
    along_y = face_flux(tracers[:, :, :, 2:-2], tracer_vert[:, :, :, 2:-2], rho_field[:, :, 2:-2],
                        rho_vert[:, :, 2:-2], ocean_presence_flags[:, :, 2:-2], north_rows, -2)
    interior = tracers[:, :, 2:-2, 2:-2]
    return ocean_presence_flags[:, 2:-2, 2:-2] * (interior + along_x + along_y)


def reference(heat_anomaly, saltiness_anomaly, zonal_stability_ratio, meridional_stability_ratio, ocean_layer_count):
    layer_stack_sum, latitude_band_sum, profile_sum = heat_anomaly.shape
    ocean_presence_flags = (lax.broadcasted_iota(jnp.int32, (layer_stack_sum, 1, 1), 0) < ocean_layer_count[None]).astype(jnp.float32)
    scalar_quantities = jnp.stack([heat_anomaly, saltiness_anomaly, ocean_presence_flags])
    lon_padded = jnp.concatenate([scalar_quantities[..., -2:], scalar_quantities, scalar_quantities[..., :2]], axis=-1)
    flipped = jnp.flip(scalar_quantities[:, :, latitude_band_sum - 3:, :], -1)
    ghost_rows = jnp.flip(jnp.roll(flipped, 1, -1)[:, :, 0:2, :], 2)
    ghost_wide = jnp.concatenate([ghost_rows[..., -2:], ghost_rows, ghost_rows[..., :2]], axis=-1)
    south_rows = jnp.zeros((3, layer_stack_sum, 2, profile_sum + 4), jnp.float32)
    padded = jnp.concatenate([south_rows, lon_padded, ghost_wide], axis=2)
    east_all = jnp.concatenate([zonal_stability_ratio[..., -1:], zonal_stability_ratio], axis=-1)
    north_all = jnp.concatenate([jnp.zeros((layer_stack_sum, 1, profile_sum), jnp.float32), meridional_stability_ratio], axis=1)
    block_size = latitude_band_sum // N_LAT

    def one_block(block_index):
        offset = (block_index * block_size).astype(jnp.int32)
        row_block = lax.dynamic_slice_in_dim(padded, offset, block_size + 4, 2)
        east_piece = lax.dynamic_slice_in_dim(east_all, offset, block_size, 1)
        north_piece = lax.dynamic_slice_in_dim(north_all, offset, block_size + 1, 1)
        return stencil(row_block, east_piece, north_piece)

    result = lax.map(one_block, jnp.arange(N_LAT, dtype=jnp.int32))
    result = jnp.moveaxis(result, 0, 2).reshape(2, layer_stack_sum, latitude_band_sum, profile_sum)
    return result[0], result[1]
```

```python
import jax
import jax.numpy as jnp
from jax import lax
from jax.experimental import pallas as pl
from jax.experimental.pallas import tpu as pltpu
from jax.sharding import PartitionSpec as P

ALPHA = 0.1655
BETA = 0.76554
CABBELING = 0.05952
LAMBDA_SALT = 0.00054914
THERMOBARIC = 0.0001497
PRESS_SALT = 1.109e-05
CROSS = 0.0024341
TOTAL_DEPTH = 5000.0
KAPPA = 0.1
SLOPE_MAX = 1.0
STRAT_MIN = 0.1

MESH = pl.DeviceIdType.MESH
F32 = jnp.float32
I32 = jnp.int32

PAD = 8
SLOT = 8
MID = 3


def density(t, s, z):
    lead = -ALPHA - (ALPHA * THERMOBARIC) * z
    salt = BETA - (BETA * PRESS_SALT) * z
    return t * (lead + (-0.5 * ALPHA * CABBELING) * t - CROSS * s) + s * (salt - (0.5 * BETA * LAMBDA_SALT) * s)


def slope_term(rho_diff, rho_zsum, half_scale):
    strat = jnp.maximum(half_scale * rho_zsum, STRAT_MIN)
    slope = jnp.clip(-rho_diff / strat, -SLOPE_MAX, SLOPE_MAX)
    return slope * (KAPPA * half_scale)


def courant_terms(c):
    up = c > 0.0
    coef = jnp.where(up, 0.5, -0.5) - 0.5 * c
    return up, coef


def tracer_flux(face, c, up, coef, sk, qa, qb, d, back, ahead, zsum):
    step = jnp.where(up, back, ahead)
    limited = jnp.minimum(jnp.maximum(step, jnp.minimum(d, 0.0)), jnp.maximum(d, 0.0))
    adv = c * (jnp.where(up, qa, qb) + coef * limited)
    return jnp.where(face, adv - (KAPPA * d + sk * zsum), 0.0)


def lanes(x, shift):
    return pltpu.roll(x, shift % 128, axis=x.ndim - 1)


def rows_by(x, shift):
    return pltpu.roll(x, shift % 8, axis=x.ndim - 2)


def make_kernel(nlon, nlat, levels, rows):
    groups = rows // 8
    per = 16 // groups
    packs = levels // per
    span = SLOT * groups
    top_row = PAD + rows

    def depth(k):
        return TOTAL_DEPTH * (k + 0.5) / levels

    def kernel(
        t_hbm, s_hbm, u_hbm, v_hbm, n_hbm, t_out, s_out,
        q, rho, u, v, n, face_x, keep_x, face_y, keep_y, fy,
        px, from_w, from_e, h, hv, hn, fa, fb, fan, fbn, ex, ey,
        load_sem, send_sem, recv_sem,
    ):
        lon = lax.axis_index("lon")
        lat = lax.axis_index("lat")
        east = lax.rem(lon + 1, nlon)
        west = lax.rem(lon + nlon - 1, nlon)
        has_south = lat > 0
        has_north = lat < nlat - 1
        top = lat == nlat - 1
        mirror = nlon - 1 - lon
        mirror_next = lax.rem(nlon - lon, nlon)
        mirror_far = mirror_next != lon
        top_far = jnp.logical_and(top, mirror_far)
        top_self = jnp.logical_and(top, jnp.logical_not(mirror_far))

        barrier = pltpu.get_barrier_semaphore()

        def greet(device):
            pl.semaphore_signal(barrier, inc=1, device_id=device, device_id_type=MESH)

        @pl.when(has_south)
        def _():
            greet({"lat": lat - 1})

        @pl.when(has_north)
        def _():
            greet({"lat": lat + 1})

        @pl.when(top)
        def _():
            greet({"lon": mirror})

        @pl.when(top_far)
        def _():
            greet({"lon": mirror_next})

        greet({"lon": east})
        greet({"lon": west})

        body_rows = pl.ds(PAD, rows)
        loads = [
            pltpu.make_async_copy(n_hbm, n.at[body_rows], load_sem.at[0]),
            pltpu.make_async_copy(t_hbm, q.at[0, :, body_rows], load_sem.at[1]),
            pltpu.make_async_copy(s_hbm, q.at[1, :, body_rows], load_sem.at[2]),
            pltpu.make_async_copy(u_hbm, u, load_sem.at[3]),
            pltpu.make_async_copy(v_hbm, v.at[:, body_rows], load_sem.at[4]),
        ]
        for load in loads:
            load.start()

        lane = lax.broadcasted_iota(I32, (8, 128), 1)
        row = lax.broadcasted_iota(I32, (8, 128), 0)
        slot_of = lane // SLOT
        sl = lane % SLOT

        loads[0].wait()
        packed_n = jnp.zeros((8, 128), F32)
        for slot in range(16):
            part = n[pl.ds(PAD + 8 * (slot % groups), 8)].astype(F32)
            packed_n = jnp.where(slot_of == slot, lanes(part, SLOT * slot + MID), packed_n)
        px[2 * packs] = packed_n
        loads[1].wait()
        loads[2].wait()
        loads[3].wait()

        @pl.loop(0, packs)
        def _(m):
            for field in range(3):
                packed = jnp.zeros((8, 128), F32)
                for slot in range(16):
                    k = packs * (slot // groups) + m
                    g = slot % groups
                    if field < 2:
                        part = q[field, k, pl.ds(PAD + 8 * g, 8)]
                    else:
                        part = u[k, pl.ds(8 * g, 8)]
                    packed = jnp.where(slot_of == slot, lanes(part, SLOT * slot + MID), packed)
                px[(0, packs, 2 * packs + 1)[field] + m] = packed

        @pl.loop(0, levels)
        def _(k):
            z = depth(k.astype(F32))
            for g in range(groups):
                at = pl.ds(PAD + 8 * g, 8)
                rho[k, at] = density(q[0, k, at], q[1, k, at], z)

        pad_n = jnp.zeros((8, 128), I32)
        n[pl.ds(0, 8)] = pad_n
        n[pl.ds(top_row, 8)] = pad_n
        for g in range(groups):
            at = pl.ds(PAD + 8 * g, 8)
            here = n[at]
            fx = jnp.minimum(here, lanes(here, 1))
            face_x[pl.ds(8 * g, 8)] = fx
            inner = jnp.logical_and(lane > 1, lane < 127)
            keep_x[pl.ds(8 * g, 8)] = jnp.where(inner, fx, 0)
            f = jnp.minimum(here, n[pl.ds(PAD + 8 * g - 1, 8)])
            face_y[at] = f
            if g == 0:
                f = jnp.where(row > 1, f, 0)
            if g == groups - 1:
                f = jnp.where(row < 7, f, 0)
            keep_y[pl.ds(8 * g, 8)] = f
        face_y[pl.ds(0, 8)] = pad_n
        face_y[pl.ds(top_row, 8)] = pad_n

        expected = 2 + has_south.astype(I32) + has_north.astype(I32) + top.astype(I32) + top_far.astype(I32)
        pl.semaphore_wait(barrier, expected)

        def remote(src, dst, index, device, recv=None):
            return pltpu.make_async_remote_copy(
                src_ref=src, dst_ref=dst, send_sem=send_sem.at[index],
                recv_sem=recv_sem.at[index if recv is None else recv],
                device_id=device, device_id_type=MESH,
            )

        first, last = pl.ds(0, 2), pl.ds(rows - 2, 2)
        fold = pl.ds(rows - 3, 2)
        lo, hi = pl.ds(0, 2), pl.ds(6, 2)
        northward = [
            remote(t_hbm.at[:, last], h.at[0, :, lo], 0, {"lat": lat + 1}),
            remote(s_hbm.at[:, last], h.at[1, :, lo], 1, {"lat": lat + 1}),
            remote(v_hbm.at[:, last], hv.at[:, lo], 2, {"lat": lat + 1}),
            remote(n_hbm.at[last], hn.at[lo], 3, {"lat": lat + 1}),
        ]
        southward = [
            remote(t_hbm.at[:, first], h.at[0, :, hi], 4, {"lat": lat - 1}),
            remote(s_hbm.at[:, first], h.at[1, :, hi], 5, {"lat": lat - 1}),
            remote(n_hbm.at[first], hn.at[hi], 6, {"lat": lat - 1}),
        ]
        folded = [
            remote(t_hbm.at[:, fold], fa.at[0, :, hi], 7, {"lon": mirror}),
            remote(s_hbm.at[:, fold], fa.at[1, :, hi], 8, {"lon": mirror}),
            remote(n_hbm.at[fold], fan.at[hi], 9, {"lon": mirror}),
        ]
        folded_next = [
            remote(t_hbm.at[:, fold], fb.at[0, :, hi], 10, {"lon": mirror_next}),
            remote(s_hbm.at[:, fold], fb.at[1, :, hi], 11, {"lon": mirror_next}),
            remote(n_hbm.at[fold], fbn.at[hi], 12, {"lon": mirror_next}),
        ]
        own_next = [
            pltpu.make_async_copy(t_hbm.at[:, fold], fb.at[0, :, hi], load_sem.at[5]),
            pltpu.make_async_copy(s_hbm.at[:, fold], fb.at[1, :, hi], load_sem.at[6]),
            pltpu.make_async_copy(n_hbm.at[fold], fbn.at[hi], load_sem.at[7]),
        ]
        eastward = remote(px, from_w, 13, {"lon": east})
        westward = remote(px.at[pl.ds(0, 2 * packs + 1)], from_e, 14, {"lon": west})

        @pl.when(has_south)
        def _():
            for copy in southward:
                copy.start()

        @pl.when(has_north)
        def _():
            for copy in northward:
                copy.start()

        @pl.when(top)
        def _():
            for copy in folded:
                copy.start()

        @pl.when(top_far)
        def _():
            for copy in folded_next:
                copy.start()

        @pl.when(top_self)
        def _():
            for copy in own_next:
                copy.start()

        eastward.start()
        westward.start()

        outs = (t_out, s_out)
        loads[4].wait()
        fy[0, pl.ds(rows, 8)] = jnp.zeros((8, 128), F32)
        fy[1, pl.ds(rows, 8)] = jnp.zeros((8, 128), F32)

        @pl.loop(0, levels)
        def _(k):
            kp = jnp.minimum(k + 1, levels - 1)
            km = jnp.maximum(k - 1, 0)
            ends = jnp.logical_or(k == 0, k == levels - 1)
            half_scale = jnp.where(ends, 0.5, 0.25).astype(F32)

            for g in reversed(range(groups)):
                r = PAD + 8 * g
                at, dn = pl.ds(r, 8), pl.ds(r - 1, 8)
                t0 = [q[i, k, at] for i in range(2)]
                zd = [q[i, kp, at] - q[i, km, at] for i in range(2)]
                rho0 = rho[k, at]
                rz = rho[kp, at] - rho[km, at]

                wet = k < face_x[pl.ds(8 * g, 8)]
                keep = k < keep_x[pl.ds(8 * g, 8)]
                c = lanes(u[k, pl.ds(8 * g, 8)], 1)
                up, coef = courant_terms(c)
                sk = slope_term(rho0 - lanes(rho0, 1), rz + lanes(rz, 1), half_scale)
                total = []
                for i in range(2):
                    qa = lanes(t0[i], 1)
                    d = jnp.where(wet, t0[i] - qa, 0.0)
                    f = tracer_flux(keep, c, up, coef, sk, qa, t0[i], d, lanes(d, 1), lanes(d, -1), zd[i] + lanes(zd[i], 1))
                    total.append(t0[i] + (f - lanes(f, -1)))

                wet = k < face_y[at]
                wet_back = k < face_y[dn]
                wet_ahead = k < face_y[pl.ds(r + 1, 8)]
                keep = k < keep_y[pl.ds(8 * g, 8)]
                c = v[k, dn]
                up, coef = courant_terms(c)
                sk = slope_term(rho0 - rho[k, dn], rz + (rho[kp, dn] - rho[km, dn]), half_scale)
                here = k < n[at]
                for i in range(2):
                    qa = q[i, k, dn]
                    d = jnp.where(wet, t0[i] - qa, 0.0)
                    back = jnp.where(wet_back, qa - q[i, k, pl.ds(r - 2, 8)], 0.0)
                    ahead = jnp.where(wet_ahead, q[i, k, pl.ds(r + 1, 8)] - t0[i], 0.0)
                    zsum = zd[i] + (q[i, kp, dn] - q[i, km, dn])
                    f = tracer_flux(keep, c, up, coef, sk, qa, t0[i], d, back, ahead, zsum)
                    fy[i, pl.ds(8 * g, 8)] = f
                    f_north = fy[i, pl.ds(8 * g + 1, 8)]
                    outs[i][k, pl.ds(8 * g, 8)] = jnp.where(here, total[i] + (f - f_north), 0.0)

        eastward.wait_recv()
        westward.wait_recv()

        def joined(base, has_east=True):
            own = px[base]
            left = jnp.where(sl < MID, from_w[base], own)
            right = jnp.where(sl < MID, own, from_e[base]) if has_east else own
            a = jnp.where(sl < 4, lanes(left, -1), lanes(right, 4))
            b = jnp.where(sl < 4, lanes(left, -2), lanes(right, 3))
            return a, b

        na, nb = joined(2 * packs)
        face_n = jnp.minimum(na, nb)
        level_of = packs * (lane // span)
        pairs = [[joined(i * packs + m) for m in range(packs)] for i in range(2)]
        rho_pairs = []
        for m in range(packs):
            z = depth((level_of + m).astype(F32))
            rho_pairs.append([density(pairs[0][m][j], pairs[1][m][j], z) for j in range(2)])
        sums = [[a + b for a, b in one] for one in (*pairs, rho_pairs)]

        def zsum_of(one, m):
            if m < packs - 1:
                above = one[m + 1]
            else:
                above = jnp.where(lane < 128 - span, lanes(one[0], -span), one[m])
            if m > 0:
                below = one[m - 1]
            else:
                below = jnp.where(lane < span, one[0], lanes(one[packs - 1], span))
            return above - below

        used = jnp.logical_or(jnp.logical_or(sl == 1, sl == 2), jnp.logical_or(sl == 5, sl == 6))
        for m in range(packs):
            level = level_of + m
            half_scale = jnp.where(jnp.logical_or(level == 0, level == levels - 1), 0.5, 0.25)
            wet = level.astype(F32) < face_n
            keep = jnp.logical_and(wet, used)
            c = joined(2 * packs + 1 + m, False)[0]
            up, coef = courant_terms(c)
            sk = slope_term(rho_pairs[m][1] - rho_pairs[m][0], zsum_of(sums[2], m), half_scale)
            for i in range(2):
                qa, qb = pairs[i][m]
                d = jnp.where(wet, qb - qa, 0.0)
                f = tracer_flux(keep, c, up, coef, sk, qa, qb, d, lanes(d, 1), lanes(d, -1), zsum_of(sums[i], m))
                change = f - lanes(f, -1)
                ex[i, m] = jnp.where(sl < MID, lanes(change, -3), lanes(change, 2))

        ends_x = jnp.logical_or(lane < 2, lane > 125)

        @pl.loop(0, packs)
        def _(m):
            for i in range(2):
                packed = ex[i, m]
                for slot in range(16):
                    k = packs * (slot // groups) + m
                    at = pl.ds(8 * (slot % groups), 8)
                    here = jnp.logical_and(ends_x, k < n[pl.ds(PAD + 8 * (slot % groups), 8)])
                    outs[i][k, at] = outs[i][k, at] + jnp.where(here, lanes(packed, -(SLOT * slot + MID)), 0.0)

        @pl.when(jnp.logical_not(has_south))
        def _():
            hn[lo] = jnp.zeros((2, 128), I32)

            @pl.loop(0, levels)
            def _(k):
                h[0, k, lo] = jnp.zeros((2, 128), F32)
                h[1, k, lo] = jnp.zeros((2, 128), F32)
                hv[k, lo] = jnp.zeros((2, 128), F32)

        @pl.when(has_south)
        def _():
            for copy in northward:
                copy.wait_recv()

        @pl.when(has_north)
        def _():
            for copy in southward:
                copy.wait_recv()

        @pl.when(top)
        def _():
            for copy in folded:
                copy.wait_recv()

        @pl.when(top_far)
        def _():
            for copy in folded_next:
                copy.wait_recv()

        @pl.when(top_self)
        def _():
            for copy in own_next:
                copy.wait()

        @pl.when(top)
        def _():
            order = lax.rem(128 - lane, 128)

            def mirrored(a, b):
                x = jnp.where(lane == 0, b, a)
                x = jnp.where(row == 6, rows_by(x, -1), rows_by(x, 1))
                return jnp.take_along_axis(x, order, axis=1)

            hn[hi] = mirrored(fan[...].astype(F32), fbn[...].astype(F32))[6:8].astype(I32)

            @pl.loop(0, levels)
            def _(k):
                for i in range(2):
                    h[i, k, hi] = mirrored(fa[i, k], fb[i, k])[6:8]

        def edge_pair(halo, load):
            a = jnp.where(
                row < 2, halo, jnp.where(row < 4, load(PAD - 2), jnp.where(row < 7, load(top_row - 7), rows_by(halo, 1)))
            )
            b = jnp.where(
                row < 1, rows_by(halo, -1), jnp.where(row < 4, load(PAD - 1), jnp.where(row < 6, load(top_row - 6), halo))
            )
            return a, b

        na, nb = edge_pair(hn[...], lambda at: n[pl.ds(at, 8)])
        face_n = jnp.minimum(na, nb)
        used_y = jnp.logical_or(jnp.logical_or(row == 1, row == 2), jnp.logical_or(row == 5, row == 6))

        @pl.loop(0, levels)
        def _(k):
            z = depth(k.astype(F32))
            pair = [edge_pair(h[i, k], lambda at, i=i: q[i, k, pl.ds(at, 8)]) for i in range(2)]
            ra, rb = [density(pair[0][j], pair[1][j], z) for j in range(2)]
            for i in range(2):
                ey[2 * i, k] = pair[i][0]
                ey[2 * i + 1, k] = pair[i][1]
                ey[4 + i, k] = pair[i][0] + pair[i][1]
            ey[6, k] = ra + rb
            ey[7, k] = rb - ra

        @pl.loop(0, levels)
        def _(k):
            kp = jnp.minimum(k + 1, levels - 1)
            km = jnp.maximum(k - 1, 0)
            ends = jnp.logical_or(k == 0, k == levels - 1)
            half_scale = jnp.where(ends, 0.5, 0.25).astype(F32)
            wet = k < face_n
            keep = jnp.logical_and(wet, used_y)
            c = jnp.where(row < 2, hv[k], jnp.where(row < 4, v[k, pl.ds(PAD - 2, 8)], v[k, pl.ds(top_row - 7, 8)]))
            up, coef = courant_terms(c)
            sk = slope_term(ey[7, k], ey[6, kp] - ey[6, km], half_scale)
            south, north = pl.ds(0, 8), pl.ds(rows - 8, 8)
            here_s = jnp.logical_and(row < 2, k < n[pl.ds(PAD, 8)])
            here_n = jnp.logical_and(row > 5, k < n[pl.ds(top_row - 8, 8)])
            for i in range(2):
                qa, qb = ey[2 * i, k], ey[2 * i + 1, k]
                d = jnp.where(wet, qb - qa, 0.0)
                zsum = ey[4 + i, kp] - ey[4 + i, km]
                f = tracer_flux(keep, c, up, coef, sk, qa, qb, d, rows_by(d, 1), rows_by(d, -1), zsum)
                change = f - rows_by(f, -1)
                outs[i][k, south] = outs[i][k, south] + jnp.where(here_s, rows_by(change, -1), 0.0)
                outs[i][k, north] = outs[i][k, north] + jnp.where(here_n, rows_by(change, 2), 0.0)

        eastward.wait_send()
        westward.wait_send()

        @pl.when(has_south)
        def _():
            for copy in southward:
                copy.wait_send()

        @pl.when(has_north)
        def _():
            for copy in northward:
                copy.wait_send()

        @pl.when(top)
        def _():
            for copy in folded:
                copy.wait_send()

        @pl.when(top_far)
        def _():
            for copy in folded_next:
                copy.wait_send()

    return kernel


def solution(mesh):
    nlon, nlat = mesh.shape["lon"], mesh.shape["lat"]

    def body(t, s, u, v, n):
        levels, rows, cols = t.shape
        packs = levels // (16 // (rows // 8))
        tall = rows + 2 * PAD
        tile = jax.ShapeDtypeStruct((levels, rows, cols), F32)
        return pl.pallas_call(
            make_kernel(nlon, nlat, levels, rows),
            out_shape=(tile, tile),
            in_specs=[pl.BlockSpec(memory_space=pl.ANY)] * 5,
            out_specs=(pl.BlockSpec(memory_space=pltpu.VMEM),) * 2,
            scratch_shapes=[
                pltpu.VMEM((2, levels, tall, cols), F32),
                pltpu.VMEM((levels, tall, cols), F32),
                pltpu.VMEM((levels, rows, cols), F32),
                pltpu.VMEM((levels, tall, cols), F32),
                pltpu.VMEM((tall, cols), I32),
                pltpu.VMEM((rows, cols), I32),
                pltpu.VMEM((rows, cols), I32),
                pltpu.VMEM((tall, cols), I32),
                pltpu.VMEM((rows, cols), I32),
                pltpu.VMEM((2, rows + 8, cols), F32),
                pltpu.VMEM((3 * packs + 1, 8, cols), F32),
                pltpu.VMEM((3 * packs + 1, 8, cols), F32),
                pltpu.VMEM((2 * packs + 1, 8, cols), F32),
                pltpu.VMEM((2, levels, 8, cols), F32),
                pltpu.VMEM((levels, 8, cols), F32),
                pltpu.VMEM((8, cols), I32),
                pltpu.VMEM((2, levels, 8, cols), F32),
                pltpu.VMEM((2, levels, 8, cols), F32),
                pltpu.VMEM((8, cols), I32),
                pltpu.VMEM((8, cols), I32),
                pltpu.VMEM((2, packs, 8, cols), F32),
                pltpu.VMEM((8, levels, 8, cols), F32),
                pltpu.SemaphoreType.DMA((8,)),
                pltpu.SemaphoreType.DMA((15,)),
                pltpu.SemaphoreType.DMA((15,)),
            ],
            compiler_params=pltpu.CompilerParams(collective_id=0, has_side_effects=True),
            name="tracer_step",
        )(t, s, u, v, n)

    spec = P(None, "lat", "lon")
    return jax.shard_map(
        body, mesh=mesh, in_specs=(spec,) * 4 + (P("lat", "lon"),), out_specs=(spec, spec), check_vma=False
    )
```

```python
import jax
import jax.numpy as jnp
from jax import lax
from jax.experimental import pallas as pl
from jax.experimental.pallas import tpu as pltpu
from jax.sharding import PartitionSpec as P

ALPHA = 0.1655
BETA = 0.76554
CABBELING = 0.05952
LAMBDA_SALT = 0.00054914
THERMOBARIC = 0.0001497
PRESS_SALT = 1.109e-05
CROSS = 0.0024341
TOTAL_DEPTH = 5000.0
KAPPA = 0.1
SLOPE_MAX = 1.0
STRAT_MIN = 0.1

MESH = pl.DeviceIdType.MESH
F32 = jnp.float32
I32 = jnp.int32

PAD = 8
SLOT = 8
MID = 3


def density(t, s, z):
    lead = -ALPHA - (ALPHA * THERMOBARIC) * z
    salt = BETA - (BETA * PRESS_SALT) * z
    return t * (lead + (-0.5 * ALPHA * CABBELING) * t - CROSS * s) + s * (salt - (0.5 * BETA * LAMBDA_SALT) * s)


def slope_term(rho_diff, rho_zsum, half_scale):
    strat = jnp.maximum(half_scale * rho_zsum, STRAT_MIN)
    slope = jnp.clip(-rho_diff / strat, -SLOPE_MAX, SLOPE_MAX)
    return slope * (KAPPA * half_scale)


def courant_terms(c):
    up = c > 0.0
    coef = jnp.where(up, 0.5, -0.5) - 0.5 * c
    return up, coef


def tracer_flux(face, c, up, coef, sk, qa, qb, d, back, ahead, zsum):
    step = jnp.where(up, back, ahead)
    limited = jnp.minimum(jnp.maximum(step, jnp.minimum(d, 0.0)), jnp.maximum(d, 0.0))
    adv = c * (jnp.where(up, qa, qb) + coef * limited)
    return jnp.where(face, adv - (KAPPA * d + sk * zsum), 0.0)


def lanes(x, shift):
    return pltpu.roll(x, shift % 128, axis=x.ndim - 1)


def rows_by(x, shift):
    return pltpu.roll(x, shift % 8, axis=x.ndim - 2)


def make_kernel(nlon, nlat, levels, rows):
    groups = rows // 8
    per = 16 // groups
    packs = levels // per
    span = SLOT * groups
    top_row = PAD + rows

    def depth(k):
        return TOTAL_DEPTH * (k + 0.5) / levels

    def kernel(
        t_hbm, s_hbm, u_hbm, v_hbm, n_hbm,
        t_out, s_out, q, v, n, h, hv, hn,
        rho, u, face_x, keep_x, face_y, keep_y, fy,
        px, to_e, to_w, from_w, from_e, fa, fb, fan, ex,
        load_sem, send_sem, recv_sem,
    ):
        lon = lax.axis_index("lon")
        lat = lax.axis_index("lat")
        east = lax.rem(lon + 1, nlon)
        west = lax.rem(lon + nlon - 1, nlon)
        has_south = lat > 0
        has_north = lat < nlat - 1
        top = lat == nlat - 1
        mirror = nlon - 1 - lon
        mirror_next = lax.rem(nlon - lon, nlon)
        mirror_far = mirror_next != lon
        top_far = jnp.logical_and(top, mirror_far)
        top_self = jnp.logical_and(top, jnp.logical_not(mirror_far))

        barrier = pltpu.get_barrier_semaphore()

        def greet(device):
            pl.semaphore_signal(barrier, inc=1, device_id=device, device_id_type=MESH)

        @pl.when(has_south)
        def _():
            greet({"lat": lat - 1})

        @pl.when(has_north)
        def _():
            greet({"lat": lat + 1})

        @pl.when(top)
        def _():
            greet({"lon": mirror})

        @pl.when(top_far)
        def _():
            greet({"lon": mirror_next})

        greet({"lon": east})
        greet({"lon": west})

        body_rows = pl.ds(PAD, rows)
        loads = [
            pltpu.make_async_copy(n_hbm, n.at[body_rows], load_sem.at[0]),
            pltpu.make_async_copy(t_hbm, q.at[0, :, body_rows], load_sem.at[1]),
            pltpu.make_async_copy(s_hbm, q.at[1, :, body_rows], load_sem.at[2]),
            pltpu.make_async_copy(u_hbm, u, load_sem.at[3]),
            pltpu.make_async_copy(v_hbm, v.at[:, body_rows], load_sem.at[4]),
        ]
        for load in loads:
            load.start()

        lane = lax.broadcasted_iota(I32, (8, 128), 1)
        row = lax.broadcasted_iota(I32, (8, 128), 0)
        slot_of = lane // SLOT
        sl = lane % SLOT

        expected = 2 + has_south.astype(I32) + has_north.astype(I32) + top.astype(I32) + top_far.astype(I32)
        pl.semaphore_wait(barrier, expected)

        def remote(src, dst, index, device):
            return pltpu.make_async_remote_copy(
                src_ref=src, dst_ref=dst, send_sem=send_sem.at[index], recv_sem=recv_sem.at[index],
                device_id=device, device_id_type=MESH,
            )

        first, last = pl.ds(0, 2), pl.ds(rows - 2, 2)
        fold = pl.ds(rows - 3, 2)
        fold_in_group = pl.ds(5, 2)
        lo, hi = pl.ds(0, 2), pl.ds(6, 2)
        northward = [
            remote(t_hbm.at[:, last], h.at[0, :, lo], 0, {"lat": lat + 1}),
            remote(s_hbm.at[:, last], h.at[1, :, lo], 1, {"lat": lat + 1}),
            remote(v_hbm.at[:, pl.ds(rows - 1, 1)], hv.at[:, pl.ds(1, 1)], 2, {"lat": lat + 1}),
            remote(n_hbm.at[last], hn.at[lo], 3, {"lat": lat + 1}),
        ]
        southward = [
            remote(t_hbm.at[:, first], h.at[0, :, hi], 4, {"lat": lat - 1}),
            remote(s_hbm.at[:, first], h.at[1, :, hi], 5, {"lat": lat - 1}),
            remote(n_hbm.at[first], hn.at[hi], 6, {"lat": lat - 1}),
        ]
        folded = [
            remote(t_hbm.at[:, fold], fa.at[0, :, hi], 7, {"lon": mirror}),
            remote(s_hbm.at[:, fold], fa.at[1, :, hi], 8, {"lon": mirror}),
            remote(n_hbm.at[fold], fan.at[hi], 9, {"lon": mirror}),
        ]
        folded_next = remote(to_w.at[:, fold_in_group], fb.at[:, hi], 10, {"lon": mirror_next})
        own_next = pltpu.make_async_copy(to_w.at[:, fold_in_group], fb.at[:, hi], load_sem.at[5])
        eastward = remote(to_e, from_w, 11, {"lon": east})
        westward = remote(to_w, from_e, 12, {"lon": west})

        @pl.when(top)
        def _():
            for copy in folded:
                copy.start()

        @pl.when(has_south)
        def _():
            for copy in southward:
                copy.start()

        @pl.when(has_north)
        def _():
            for copy in northward:
                copy.start()

        for load in loads[:4]:
            load.wait()
        packed_n = jnp.zeros((8, 128), F32)
        for slot in range(16):
            part = n[pl.ds(PAD + 8 * (slot % groups), 8)].astype(F32)
            packed_n = jnp.where(slot_of == slot, lanes(part, SLOT * slot + MID), packed_n)
        px[2 * packs] = packed_n
        n_up, n_down = lanes(packed_n, 5), lanes(packed_n, -2)

        @pl.loop(0, packs)
        def _(m):
            packed = []
            for field in range(3):
                one = jnp.zeros((8, 128), F32)
                for slot in range(16):
                    k = packs * (slot // groups) + m
                    g = slot % groups
                    if field < 2:
                        part = q[field, k, pl.ds(PAD + 8 * g, 8)]
                    else:
                        part = u[k, pl.ds(8 * g, 8)]
                    one = jnp.where(slot_of == slot, lanes(part, SLOT * slot + MID), one)
                px[(0, packs, 2 * packs + 1)[field] + m] = one
                packed.append(one)
            t2, s2, u2 = packed
            s_up = lanes(s2, 2)
            to_e[m] = jnp.where(sl < 3, t2, jnp.where(sl < 5, s_up, jnp.where(sl < 6, lanes(u2, 3), n_up)))
            to_w[m] = jnp.where(sl < 3, n_down, jnp.where(sl < 5, t2, s_up))

        @pl.when(top_far)
        def _():
            folded_next.start()

        @pl.when(top_self)
        def _():
            own_next.start()

        eastward.start()
        westward.start()

        @pl.loop(0, levels)
        def _(k):
            z = depth(k.astype(F32))
            for g in range(groups):
                at = pl.ds(PAD + 8 * g, 8)
                rho[k, at] = density(q[0, k, at], q[1, k, at], z)

        pad_n = jnp.zeros((8, 128), I32)
        n[pl.ds(0, 8)] = pad_n
        n[pl.ds(top_row, 8)] = pad_n
        for g in range(groups):
            at = pl.ds(PAD + 8 * g, 8)
            here = n[at]
            fx = jnp.minimum(here, lanes(here, 1))
            face_x[pl.ds(8 * g, 8)] = fx
            inner = jnp.logical_and(lane > 1, lane < 127)
            keep_x[pl.ds(8 * g, 8)] = jnp.where(inner, fx, 0)
            f = jnp.minimum(here, n[pl.ds(PAD + 8 * g - 1, 8)])
            face_y[at] = f
            if g == 0:
                f = jnp.where(row > 1, f, 0)
            if g == groups - 1:
                f = jnp.where(row < 7, f, 0)
            keep_y[pl.ds(8 * g, 8)] = f
        face_y[pl.ds(0, 8)] = pad_n
        face_y[pl.ds(top_row, 8)] = pad_n

        outs = (t_out, s_out)
        loads[4].wait()
        fy[0, pl.ds(rows, 8)] = jnp.zeros((8, 128), F32)
        fy[1, pl.ds(rows, 8)] = jnp.zeros((8, 128), F32)

        @pl.loop(0, levels)
        def _(k):
            kp = jnp.minimum(k + 1, levels - 1)
            km = jnp.maximum(k - 1, 0)
            ends = jnp.logical_or(k == 0, k == levels - 1)
            half_scale = jnp.where(ends, 0.5, 0.25).astype(F32)

            for g in reversed(range(groups)):
                r = PAD + 8 * g
                at, dn = pl.ds(r, 8), pl.ds(r - 1, 8)
                t0 = [q[i, k, at] for i in range(2)]
                zd = [q[i, kp, at] - q[i, km, at] for i in range(2)]
                rho0 = rho[k, at]
                rz = rho[kp, at] - rho[km, at]

                wet = k < face_x[pl.ds(8 * g, 8)]
                keep = k < keep_x[pl.ds(8 * g, 8)]
                c = lanes(u[k, pl.ds(8 * g, 8)], 1)
                up, coef = courant_terms(c)
                sk = slope_term(rho0 - lanes(rho0, 1), rz + lanes(rz, 1), half_scale)
                total = []
                for i in range(2):
                    qa = lanes(t0[i], 1)
                    d = jnp.where(wet, t0[i] - qa, 0.0)
                    f = tracer_flux(keep, c, up, coef, sk, qa, t0[i], d, lanes(d, 1), lanes(d, -1), zd[i] + lanes(zd[i], 1))
                    total.append(t0[i] + (f - lanes(f, -1)))

                wet = k < face_y[at]
                wet_back = k < face_y[dn]
                wet_ahead = k < face_y[pl.ds(r + 1, 8)]
                keep = k < keep_y[pl.ds(8 * g, 8)]
                c = v[k, dn]
                up, coef = courant_terms(c)
                sk = slope_term(rho0 - rho[k, dn], rz + (rho[kp, dn] - rho[km, dn]), half_scale)
                here = k < n[at]
                for i in range(2):
                    qa = q[i, k, dn]
                    d = jnp.where(wet, t0[i] - qa, 0.0)
                    back = jnp.where(wet_back, qa - q[i, k, pl.ds(r - 2, 8)], 0.0)
                    ahead = jnp.where(wet_ahead, q[i, k, pl.ds(r + 1, 8)] - t0[i], 0.0)
                    zsum = zd[i] + (q[i, kp, dn] - q[i, km, dn])
                    f = tracer_flux(keep, c, up, coef, sk, qa, t0[i], d, back, ahead, zsum)
                    fy[i, pl.ds(8 * g, 8)] = f
                    f_north = fy[i, pl.ds(8 * g + 1, 8)]
                    outs[i][k, pl.ds(8 * g, 8)] = jnp.where(here, total[i] + (f - f_north), 0.0)

        eastward.wait_recv()
        westward.wait_recv()

        def joined(own, before, after):
            left = jnp.where(sl < MID, before, own)
            right = own if after is None else jnp.where(sl < MID, own, after)
            a = jnp.where(sl < 4, lanes(left, -1), lanes(right, 4))
            b = jnp.where(sl < 4, lanes(left, -2), lanes(right, 3))
            return a, b

        na, nb = joined(px[2 * packs], lanes(from_w[0], -5), lanes(from_e[0], 2))
        face_n = jnp.minimum(na, nb)
        level_of = packs * (lane // span)
        pairs = [
            [joined(px[m], from_w[m], from_e[m]) for m in range(packs)],
            [joined(px[packs + m], lanes(from_w[m], -2), lanes(from_e[m], -2)) for m in range(packs)],
        ]
        rho_pairs = []
        for m in range(packs):
            z = depth((level_of + m).astype(F32))
            rho_pairs.append([density(pairs[0][m][j], pairs[1][m][j], z) for j in range(2)])
        sums = [[a + b for a, b in one] for one in (*pairs, rho_pairs)]

        def zsum_of(one, m):
            if m < packs - 1:
                above = one[m + 1]
            else:
                above = jnp.where(lane < 128 - span, lanes(one[0], -span), one[m])
            if m > 0:
                below = one[m - 1]
            else:
                below = jnp.where(lane < span, one[0], lanes(one[packs - 1], span))
            return above - below

        used = jnp.logical_or(jnp.logical_or(sl == 1, sl == 2), jnp.logical_or(sl == 5, sl == 6))
        for m in range(packs):
            level = level_of + m
            half_scale = jnp.where(jnp.logical_or(level == 0, level == levels - 1), 0.5, 0.25)
            wet = level.astype(F32) < face_n
            keep = jnp.logical_and(wet, used)
            c = joined(px[2 * packs + 1 + m], lanes(from_w[m], -3), None)[0]
            up, coef = courant_terms(c)
            sk = slope_term(rho_pairs[m][1] - rho_pairs[m][0], zsum_of(sums[2], m), half_scale)
            for i in range(2):
                qa, qb = pairs[i][m]
                d = jnp.where(wet, qb - qa, 0.0)
                f = tracer_flux(keep, c, up, coef, sk, qa, qb, d, lanes(d, 1), lanes(d, -1), zsum_of(sums[i], m))
                change = f - lanes(f, -1)
                ex[i, m] = jnp.where(sl < MID, lanes(change, -3), lanes(change, 2))

        ends_x = jnp.logical_or(lane < 2, lane > 125)

        @pl.loop(0, packs)
        def _(m):
            for i in range(2):
                packed = ex[i, m]
                for slot in range(16):
                    k = packs * (slot // groups) + m
                    at = pl.ds(8 * (slot % groups), 8)
                    here = jnp.logical_and(ends_x, k < n[pl.ds(PAD + 8 * (slot % groups), 8)])
                    outs[i][k, at] = outs[i][k, at] + jnp.where(here, lanes(packed, -(SLOT * slot + MID)), 0.0)

        @pl.when(jnp.logical_not(has_south))
        def _():
            hn[lo] = jnp.zeros((2, 128), I32)

            @pl.loop(0, levels)
            def _(k):
                h[0, k, lo] = jnp.zeros((2, 128), F32)
                h[1, k, lo] = jnp.zeros((2, 128), F32)
                hv[k, lo] = jnp.zeros((2, 128), F32)

        @pl.when(has_south)
        def _():
            for copy in northward:
                copy.wait_recv()

        @pl.when(has_north)
        def _():
            for copy in southward:
                copy.wait_recv()

        @pl.when(top)
        def _():
            for copy in folded:
                copy.wait_recv()

        @pl.when(top_far)
        def _():
            folded_next.wait_recv()

        @pl.when(top_self)
        def _():
            own_next.wait()

        @pl.when(top)
        def _():
            order = lax.rem(128 - lane, 128)

            def mirrored(x):
                x = jnp.where(row == 6, rows_by(x, -1), rows_by(x, 1))
                return jnp.take_along_axis(x, order, axis=1)

            spot = SLOT * (groups - 1) + MID
            x = jnp.where(lane == 0, lanes(fb[0], -(spot - 2)), fan[...].astype(F32))
            hn[hi] = mirrored(x)[6:8].astype(I32)

            @pl.loop(0, packs)
            def _(m):
                for part in range(16 // groups):
                    k = packs * part + m
                    for i in range(2):
                        x = jnp.where(lane == 0, lanes(fb[m], -(span * part + spot + 2 * i)), fa[i, k])
                        h[i, k, hi] = mirrored(x)[6:8]

        eastward.wait_send()
        westward.wait_send()

        @pl.when(has_south)
        def _():
            for copy in southward:
                copy.wait_send()

        @pl.when(has_north)
        def _():
            for copy in northward:
                copy.wait_send()

        @pl.when(top)
        def _():
            for copy in folded:
                copy.wait_send()

        @pl.when(top_far)
        def _():
            folded_next.wait_send()

    return kernel


def make_edge_kernel(levels, rows):
    top_row = PAD + rows
    unroll = 4

    def kernel(t_part, s_part, q, v, n, h, hv, hn, t_out, s_out, ey, done, sem):
        parts = (t_part, s_part)
        outs = (t_out, s_out)
        row = lax.broadcasted_iota(I32, (8, 128), 0)
        inner = pl.ds(8, rows - 16)
        south, north = pl.ds(0, 8), pl.ds(rows - 8, 8)
        stores = [
            pltpu.make_async_copy(parts[i].at[:, inner], outs[i].at[:, inner], sem.at[i]) for i in range(2)
        ]
        for store in stores:
            store.start()

        def edge_pair(halo, load):
            a = jnp.where(
                row < 2, halo, jnp.where(row < 4, load(PAD - 2), jnp.where(row < 7, load(top_row - 7), rows_by(halo, 1)))
            )
            b = jnp.where(
                row < 1, rows_by(halo, -1), jnp.where(row < 4, load(PAD - 1), jnp.where(row < 6, load(top_row - 6), halo))
            )
            return a, b

        na, nb = edge_pair(hn[...], lambda at: n[pl.ds(at, 8)])
        face_n = jnp.minimum(na, nb)
        used = jnp.logical_or(jnp.logical_or(row == 1, row == 2), jnp.logical_or(row == 5, row == 6))

        @pl.loop(0, levels // unroll)
        def _(block):
            for j in range(unroll):
                k = block * unroll + j
                z = TOTAL_DEPTH * (k.astype(F32) + 0.5) / levels
                pair = [edge_pair(h[i, k], lambda at, i=i: q[i, k, pl.ds(at, 8)]) for i in range(2)]
                ra, rb = [density(pair[0][j], pair[1][j], z) for j in range(2)]
                for i in range(2):
                    ey[2 * i, k] = pair[i][0]
                    ey[2 * i + 1, k] = pair[i][1]
                    ey[4 + i, k] = pair[i][0] + pair[i][1]
                ey[6, k] = ra + rb
                ey[7, k] = rb - ra

        n_south = jnp.where(row < 2, n[pl.ds(PAD, 8)], 0)
        n_north = jnp.where(row > 5, n[pl.ds(top_row - 8, 8)], 0)

        @pl.loop(0, levels // unroll)
        def _(block):
            for j in range(unroll):
                k = block * unroll + j
                kp = jnp.minimum(k + 1, levels - 1)
                km = jnp.maximum(k - 1, 0)
                ends = jnp.logical_or(k == 0, k == levels - 1)
                half_scale = jnp.where(ends, 0.5, 0.25).astype(F32)
                wet = k < face_n
                keep = jnp.logical_and(wet, used)
                c = jnp.where(row < 2, hv[k], jnp.where(row < 4, v[k, pl.ds(PAD - 2, 8)], v[k, pl.ds(top_row - 7, 8)]))
                up, coef = courant_terms(c)
                sk = slope_term(ey[7, k], ey[6, kp] - ey[6, km], half_scale)
                for i in range(2):
                    qa, qb = ey[2 * i, k], ey[2 * i + 1, k]
                    d = jnp.where(wet, qb - qa, 0.0)
                    zsum = ey[4 + i, kp] - ey[4 + i, km]
                    f = tracer_flux(keep, c, up, coef, sk, qa, qb, d, rows_by(d, 1), rows_by(d, -1), zsum)
                    change = f - rows_by(f, -1)
                    done[2 * i, k] = parts[i][k, south] + jnp.where(k < n_south, rows_by(change, -1), 0.0)
                    done[2 * i + 1, k] = parts[i][k, north] + jnp.where(k < n_north, rows_by(change, 2), 0.0)

        for i in range(2):
            stores.append(pltpu.make_async_copy(done.at[2 * i], outs[i].at[:, south], sem.at[2 + 2 * i]))
            stores.append(pltpu.make_async_copy(done.at[2 * i + 1], outs[i].at[:, north], sem.at[3 + 2 * i]))
        for store in stores[2:]:
            store.start()
        for store in stores:
            store.wait()

    return kernel


def solution(mesh):
    nlon, nlat = mesh.shape["lon"], mesh.shape["lat"]

    def body(t, s, u, v, n):
        levels, rows, cols = t.shape
        packs = levels // (16 // (rows // 8))
        tall = rows + 2 * PAD
        plain = jax.ShapeDtypeStruct((levels, rows, cols), F32)
        parts = pl.pallas_call(
            make_kernel(nlon, nlat, levels, rows),
            out_shape=(
                pltpu.VMEM((levels, rows, cols), F32),
                pltpu.VMEM((levels, rows, cols), F32),
                pltpu.VMEM((2, levels, tall, cols), F32),
                pltpu.VMEM((levels, tall, cols), F32),
                pltpu.VMEM((tall, cols), I32),
                pltpu.VMEM((2, levels, 8, cols), F32),
                pltpu.VMEM((levels, 8, cols), F32),
                pltpu.VMEM((8, cols), I32),
            ),
            in_specs=[pl.BlockSpec(memory_space=pl.ANY)] * 5,
            out_specs=(pl.BlockSpec(memory_space=pltpu.VMEM),) * 8,
            scratch_shapes=[
                pltpu.VMEM((levels, tall, cols), F32),
                pltpu.VMEM((levels, rows, cols), F32),
                pltpu.VMEM((rows, cols), I32),
                pltpu.VMEM((rows, cols), I32),
                pltpu.VMEM((tall, cols), I32),
                pltpu.VMEM((rows, cols), I32),
                pltpu.VMEM((2, rows + 8, cols), F32),
                pltpu.VMEM((3 * packs + 1, 8, cols), F32),
                pltpu.VMEM((packs, 8, cols), F32),
                pltpu.VMEM((packs, 8, cols), F32),
                pltpu.VMEM((packs, 8, cols), F32),
                pltpu.VMEM((packs, 8, cols), F32),
                pltpu.VMEM((2, levels, 8, cols), F32),
                pltpu.VMEM((packs, 8, cols), F32),
                pltpu.VMEM((8, cols), I32),
                pltpu.VMEM((2, packs, 8, cols), F32),
                pltpu.SemaphoreType.DMA((6,)),
                pltpu.SemaphoreType.DMA((13,)),
                pltpu.SemaphoreType.DMA((13,)),
            ],
            compiler_params=pltpu.CompilerParams(collective_id=0, has_side_effects=True),
            name="tracer_step",
        )(t, s, u, v, n)
        return pl.pallas_call(
            make_edge_kernel(levels, rows),
            out_shape=(plain, plain),
            in_specs=[pl.BlockSpec(memory_space=pltpu.VMEM)] * 8,
            out_specs=(pl.BlockSpec(memory_space=pl.ANY),) * 2,
            scratch_shapes=[
                pltpu.VMEM((8, levels, 8, cols), F32),
                pltpu.VMEM((4, levels, 8, cols), F32),
                pltpu.SemaphoreType.DMA((6,)),
            ],
            name="edge_rows",
        )(*[pltpu.with_memory_space_constraint(part, pltpu.VMEM) for part in parts])

    spec = P(None, "lat", "lon")
    return jax.shard_map(
        body, mesh=mesh, in_specs=(spec,) * 4 + (P("lat", "lon"),), out_specs=(spec, spec), check_vma=False
    )
```

```python
import jax
import jax.numpy as jnp
from jax import lax
from jax.experimental import pallas as pl
from jax.experimental.pallas import tpu as pltpu
from jax.sharding import PartitionSpec as P

ALPHA = 0.1655
BETA = 0.76554
CABBELING = 0.05952
LAMBDA_SALT = 0.00054914
THERMOBARIC = 0.0001497
PRESS_SALT = 1.109e-05
CROSS = 0.0024341
TOTAL_DEPTH = 5000.0
KAPPA = 0.1
SLOPE_MAX = 1.0
STRAT_MIN = 0.1

MESH = pl.DeviceIdType.MESH
F32 = jnp.float32
I32 = jnp.int32

PAD = 8
SLOT = 8
MID = 3


def density(t, s, z):
    lead = -ALPHA - (ALPHA * THERMOBARIC) * z
    salt = BETA - (BETA * PRESS_SALT) * z
    return t * (lead + (-0.5 * ALPHA * CABBELING) * t - CROSS * s) + s * (salt - (0.5 * BETA * LAMBDA_SALT) * s)


def slope_term(rho_diff, rho_zsum, half_scale):
    strat = jnp.maximum(half_scale * rho_zsum, STRAT_MIN)
    slope = jnp.clip(-rho_diff / strat, -SLOPE_MAX, SLOPE_MAX)
    return slope * (KAPPA * half_scale)


def courant_terms(c):
    up = c > 0.0
    coef = jnp.where(up, 0.5, -0.5) - 0.5 * c
    return up, coef


def tracer_flux(face, c, up, coef, sk, qa, qb, d, back, ahead, zsum):
    step = jnp.where(up, back, ahead)
    limited = jnp.minimum(jnp.maximum(step, jnp.minimum(d, 0.0)), jnp.maximum(d, 0.0))
    adv = c * (jnp.where(up, qa, qb) + coef * limited)
    return jnp.where(face, adv - (KAPPA * d + sk * zsum), 0.0)


def lanes(x, shift):
    return pltpu.roll(x, shift % 128, axis=x.ndim - 1)


def rows_by(x, shift):
    return pltpu.roll(x, shift % 8, axis=x.ndim - 2)


def make_kernel(nlon, nlat, levels, rows):
    groups = rows // 8
    per = 16 // groups
    packs = levels // per
    span = SLOT * groups
    top_row = PAD + rows

    def depth(k):
        return TOTAL_DEPTH * (k + 0.5) / levels

    def kernel(
        t_hbm, s_hbm, u_hbm, v_hbm, n_hbm,
        t_out, s_out, q, v, n, h, hv, hn,
        rho, u, face_x, keep_x, face_y, keep_y, fy,
        px, to_e, to_w, from_w, from_e, fa, fb, fan, ex,
        load_sem, send_sem, recv_sem, late_ready,
    ):
        lon = lax.axis_index("lon")
        lat = lax.axis_index("lat")
        east = lax.rem(lon + 1, nlon)
        west = lax.rem(lon + nlon - 1, nlon)
        has_south = lat > 0
        has_north = lat < nlat - 1
        top = lat == nlat - 1
        mirror = nlon - 1 - lon
        mirror_next = lax.rem(nlon - lon, nlon)
        mirror_far = mirror_next != lon
        top_far = jnp.logical_and(top, mirror_far)
        top_self = jnp.logical_and(top, jnp.logical_not(mirror_far))
        half, quarter = nlon // 2, nlon // 4
        place = lax.rem(lon, half)
        early = place < quarter
        late_west = place == 0
        late_east = place == quarter - 1
        early_west = place == quarter
        early_east = place == half - 1
        mirror_late = jnp.logical_and(top, early)
        mirror_early = jnp.logical_and(top, jnp.logical_not(early))
        next_late = jnp.logical_and(top_far, early)
        next_early = jnp.logical_and(top_far, place > quarter)
        next_same = jnp.logical_and(top_far, place == quarter)

        barrier = pltpu.get_barrier_semaphore()

        def greet(device):
            pl.semaphore_signal(barrier, inc=1, device_id=device, device_id_type=MESH)

        def when(condition, *steps):
            @pl.when(condition)
            def _():
                for step in steps:
                    step()

        def both(a, b):
            return jnp.logical_or(a, b)

        when(has_south, lambda: greet({"lat": lat - 1}))
        when(has_north, lambda: greet({"lat": lat + 1}))
        when(mirror_late, lambda: greet({"lon": mirror}))
        when(both(next_late, next_same), lambda: greet({"lon": mirror_next}))
        when(jnp.logical_not(early_east), lambda: greet({"lon": east}))
        when(jnp.logical_not(early_west), lambda: greet({"lon": west}))

        body_rows = pl.ds(PAD, rows)
        loads = [
            pltpu.make_async_copy(n_hbm, n.at[body_rows], load_sem.at[0]),
            pltpu.make_async_copy(t_hbm, q.at[0, :, body_rows], load_sem.at[1]),
            pltpu.make_async_copy(s_hbm, q.at[1, :, body_rows], load_sem.at[2]),
            pltpu.make_async_copy(u_hbm, u, load_sem.at[3]),
            pltpu.make_async_copy(v_hbm, v.at[:, body_rows], load_sem.at[4]),
        ]
        for load in loads:
            load.start()

        lane = lax.broadcasted_iota(I32, (8, 128), 1)
        row = lax.broadcasted_iota(I32, (8, 128), 0)
        slot_of = lane // SLOT
        sl = lane % SLOT

        greetings = (
            has_south, has_north, mirror_early, both(next_early, next_same),
            jnp.logical_not(late_west), jnp.logical_not(late_east),
        )
        pl.semaphore_wait(barrier, sum(one.astype(I32) for one in greetings))

        def tell(index, device):
            pl.semaphore_signal(late_ready.at[index], inc=1, device_id=device, device_id_type=MESH)

        when(mirror_early, lambda: tell(0, {"lon": mirror}))
        when(next_early, lambda: tell(1, {"lon": mirror_next}))
        when(early_east, lambda: tell(2, {"lon": east}))
        when(early_west, lambda: tell(3, {"lon": west}))

        def remote(src, dst, index, device):
            return pltpu.make_async_remote_copy(
                src_ref=src, dst_ref=dst, send_sem=send_sem.at[index], recv_sem=recv_sem.at[index],
                device_id=device, device_id_type=MESH,
            )

        first, last = pl.ds(0, 2), pl.ds(rows - 2, 2)
        fold = pl.ds(rows - 3, 2)
        fold_in_group = pl.ds(5, 2)
        lo, hi = pl.ds(0, 2), pl.ds(6, 2)
        northward = [
            remote(t_hbm.at[:, last], h.at[0, :, lo], 0, {"lat": lat + 1}),
            remote(s_hbm.at[:, last], h.at[1, :, lo], 1, {"lat": lat + 1}),
            remote(v_hbm.at[:, pl.ds(rows - 1, 1)], hv.at[:, pl.ds(1, 1)], 2, {"lat": lat + 1}),
            remote(n_hbm.at[last], hn.at[lo], 3, {"lat": lat + 1}),
        ]
        southward = [
            remote(t_hbm.at[:, first], h.at[0, :, hi], 4, {"lat": lat - 1}),
            remote(s_hbm.at[:, first], h.at[1, :, hi], 5, {"lat": lat - 1}),
            remote(n_hbm.at[first], hn.at[hi], 6, {"lat": lat - 1}),
        ]
        folded = [
            remote(t_hbm.at[:, fold], fa.at[0, :, hi], 7, {"lon": mirror}),
            remote(s_hbm.at[:, fold], fa.at[1, :, hi], 8, {"lon": mirror}),
            remote(n_hbm.at[fold], fan.at[hi], 9, {"lon": mirror}),
        ]
        folded_next = remote(to_w.at[:, fold_in_group], fb.at[:, hi], 10, {"lon": mirror_next})
        own_next = pltpu.make_async_copy(to_w.at[:, fold_in_group], fb.at[:, hi], load_sem.at[5])
        eastward = remote(to_e, from_w, 11, {"lon": east})
        westward = remote(to_w, from_e, 12, {"lon": west})

        when(mirror_early, *[copy.start for copy in folded])
        when(has_south, *[copy.start for copy in southward])
        when(has_north, *[copy.start for copy in northward])

        for load in loads[:4]:
            load.wait()
        packed_n = jnp.zeros((8, 128), F32)
        for slot in range(16):
            part = n[pl.ds(PAD + 8 * (slot % groups), 8)].astype(F32)
            packed_n = jnp.where(slot_of == slot, lanes(part, SLOT * slot + MID), packed_n)
        px[2 * packs] = packed_n
        n_up, n_down = lanes(packed_n, 5), lanes(packed_n, -2)

        @pl.loop(0, packs)
        def _(m):
            packed = []
            for field in range(3):
                one = jnp.zeros((8, 128), F32)
                for slot in range(16):
                    k = packs * (slot // groups) + m
                    g = slot % groups
                    if field < 2:
                        part = q[field, k, pl.ds(PAD + 8 * g, 8)]
                    else:
                        part = u[k, pl.ds(8 * g, 8)]
                    one = jnp.where(slot_of == slot, lanes(part, SLOT * slot + MID), one)
                px[(0, packs, 2 * packs + 1)[field] + m] = one
                packed.append(one)
            t2, s2, u2 = packed
            s_up = lanes(s2, 2)
            to_e[m] = jnp.where(sl < 3, t2, jnp.where(sl < 5, s_up, jnp.where(sl < 6, lanes(u2, 3), n_up)))
            to_w[m] = jnp.where(sl < 3, n_down, jnp.where(sl < 5, t2, s_up))

        when(top_self, own_next.start)
        when(both(next_early, next_same), folded_next.start)
        when(jnp.logical_not(late_east), eastward.start)
        when(jnp.logical_not(late_west), westward.start)

        @pl.loop(0, levels)
        def _(k):
            z = depth(k.astype(F32))
            for g in range(groups):
                at = pl.ds(PAD + 8 * g, 8)
                rho[k, at] = density(q[0, k, at], q[1, k, at], z)

        pad_n = jnp.zeros((8, 128), I32)
        n[pl.ds(0, 8)] = pad_n
        n[pl.ds(top_row, 8)] = pad_n
        for g in range(groups):
            at = pl.ds(PAD + 8 * g, 8)
            here = n[at]
            fx = jnp.minimum(here, lanes(here, 1))
            face_x[pl.ds(8 * g, 8)] = fx
            inner = jnp.logical_and(lane > 1, lane < 127)
            keep_x[pl.ds(8 * g, 8)] = jnp.where(inner, fx, 0)
            f = jnp.minimum(here, n[pl.ds(PAD + 8 * g - 1, 8)])
            face_y[at] = f
            if g == 0:
                f = jnp.where(row > 1, f, 0)
            if g == groups - 1:
                f = jnp.where(row < 7, f, 0)
            keep_y[pl.ds(8 * g, 8)] = f
        face_y[pl.ds(0, 8)] = pad_n
        face_y[pl.ds(top_row, 8)] = pad_n

        outs = (t_out, s_out)
        loads[4].wait()
        fy[0, pl.ds(rows, 8)] = jnp.zeros((8, 128), F32)
        fy[1, pl.ds(rows, 8)] = jnp.zeros((8, 128), F32)

        def interior(k):
            kp = jnp.minimum(k + 1, levels - 1)
            km = jnp.maximum(k - 1, 0)
            ends = jnp.logical_or(k == 0, k == levels - 1)
            half_scale = jnp.where(ends, 0.5, 0.25).astype(F32)

            for g in reversed(range(groups)):
                r = PAD + 8 * g
                at, dn = pl.ds(r, 8), pl.ds(r - 1, 8)
                t0 = [q[i, k, at] for i in range(2)]
                zd = [q[i, kp, at] - q[i, km, at] for i in range(2)]
                rho0 = rho[k, at]
                rz = rho[kp, at] - rho[km, at]

                wet = k < face_x[pl.ds(8 * g, 8)]
                keep = k < keep_x[pl.ds(8 * g, 8)]
                c = lanes(u[k, pl.ds(8 * g, 8)], 1)
                up, coef = courant_terms(c)
                sk = slope_term(rho0 - lanes(rho0, 1), rz + lanes(rz, 1), half_scale)
                total = []
                for i in range(2):
                    qa = lanes(t0[i], 1)
                    d = jnp.where(wet, t0[i] - qa, 0.0)
                    f = tracer_flux(keep, c, up, coef, sk, qa, t0[i], d, lanes(d, 1), lanes(d, -1), zd[i] + lanes(zd[i], 1))
                    total.append(t0[i] + (f - lanes(f, -1)))

                wet = k < face_y[at]
                wet_back = k < face_y[dn]
                wet_ahead = k < face_y[pl.ds(r + 1, 8)]
                keep = k < keep_y[pl.ds(8 * g, 8)]
                c = v[k, dn]
                up, coef = courant_terms(c)
                sk = slope_term(rho0 - rho[k, dn], rz + (rho[kp, dn] - rho[km, dn]), half_scale)
                here = k < n[at]
                for i in range(2):
                    qa = q[i, k, dn]
                    d = jnp.where(wet, t0[i] - qa, 0.0)
                    back = jnp.where(wet_back, qa - q[i, k, pl.ds(r - 2, 8)], 0.0)
                    ahead = jnp.where(wet_ahead, q[i, k, pl.ds(r + 1, 8)] - t0[i], 0.0)
                    zsum = zd[i] + (q[i, kp, dn] - q[i, km, dn])
                    f = tracer_flux(keep, c, up, coef, sk, qa, t0[i], d, back, ahead, zsum)
                    fy[i, pl.ds(8 * g, 8)] = f
                    f_north = fy[i, pl.ds(8 * g + 1, 8)]
                    outs[i][k, pl.ds(8 * g, 8)] = jnp.where(here, total[i] + (f - f_north), 0.0)

        pl.loop(0, levels)(interior)

        def heard(index):
            return lambda: pl.semaphore_wait(late_ready.at[index], 1)

        when(late_east, heard(3), eastward.start)
        when(late_west, heard(2), westward.start)
        when(mirror_late, heard(0), *[copy.start for copy in folded])
        when(next_late, heard(1), folded_next.start)

        eastward.wait_recv()
        westward.wait_recv()

        def joined(own, before, after):
            left = jnp.where(sl < MID, before, own)
            right = own if after is None else jnp.where(sl < MID, own, after)
            a = jnp.where(sl < 4, lanes(left, -1), lanes(right, 4))
            b = jnp.where(sl < 4, lanes(left, -2), lanes(right, 3))
            return a, b

        na, nb = joined(px[2 * packs], lanes(from_w[0], -5), lanes(from_e[0], 2))
        face_n = jnp.minimum(na, nb)
        level_of = packs * (lane // span)
        pairs = [
            [joined(px[m], from_w[m], from_e[m]) for m in range(packs)],
            [joined(px[packs + m], lanes(from_w[m], -2), lanes(from_e[m], -2)) for m in range(packs)],
        ]
        rho_pairs = []
        for m in range(packs):
            z = depth((level_of + m).astype(F32))
            rho_pairs.append([density(pairs[0][m][j], pairs[1][m][j], z) for j in range(2)])
        sums = [[a + b for a, b in one] for one in (*pairs, rho_pairs)]

        def zsum_of(one, m):
            if m < packs - 1:
                above = one[m + 1]
            else:
                above = jnp.where(lane < 128 - span, lanes(one[0], -span), one[m])
            if m > 0:
                below = one[m - 1]
            else:
                below = jnp.where(lane < span, one[0], lanes(one[packs - 1], span))
            return above - below

        used = jnp.logical_or(jnp.logical_or(sl == 1, sl == 2), jnp.logical_or(sl == 5, sl == 6))
        for m in range(packs):
            level = level_of + m
            half_scale = jnp.where(jnp.logical_or(level == 0, level == levels - 1), 0.5, 0.25)
            wet = level.astype(F32) < face_n
            keep = jnp.logical_and(wet, used)
            c = joined(px[2 * packs + 1 + m], lanes(from_w[m], -3), None)[0]
            up, coef = courant_terms(c)
            sk = slope_term(rho_pairs[m][1] - rho_pairs[m][0], zsum_of(sums[2], m), half_scale)
            for i in range(2):
                qa, qb = pairs[i][m]
                d = jnp.where(wet, qb - qa, 0.0)
                f = tracer_flux(keep, c, up, coef, sk, qa, qb, d, lanes(d, 1), lanes(d, -1), zsum_of(sums[i], m))
                change = f - lanes(f, -1)
                ex[i, m] = jnp.where(sl < MID, lanes(change, -3), lanes(change, 2))

        ends_x = jnp.logical_or(lane < 2, lane > 125)

        @pl.loop(0, packs)
        def _(m):
            for i in range(2):
                packed = ex[i, m]
                for slot in range(16):
                    k = packs * (slot // groups) + m
                    at = pl.ds(8 * (slot % groups), 8)
                    here = jnp.logical_and(ends_x, k < n[pl.ds(PAD + 8 * (slot % groups), 8)])
                    outs[i][k, at] = outs[i][k, at] + jnp.where(here, lanes(packed, -(SLOT * slot + MID)), 0.0)

        @pl.when(jnp.logical_not(has_south))
        def _():
            hn[lo] = jnp.zeros((2, 128), I32)

            @pl.loop(0, levels)
            def _(k):
                h[0, k, lo] = jnp.zeros((2, 128), F32)
                h[1, k, lo] = jnp.zeros((2, 128), F32)
                hv[k, lo] = jnp.zeros((2, 128), F32)

        @pl.when(has_south)
        def _():
            for copy in northward:
                copy.wait_recv()

        @pl.when(has_north)
        def _():
            for copy in southward:
                copy.wait_recv()

        @pl.when(top)
        def _():
            for copy in folded:
                copy.wait_recv()

        @pl.when(top_far)
        def _():
            folded_next.wait_recv()

        @pl.when(top_self)
        def _():
            own_next.wait()

        @pl.when(top)
        def _():
            order = lax.rem(128 - lane, 128)

            def mirrored(x):
                x = jnp.where(row == 6, rows_by(x, -1), rows_by(x, 1))
                return jnp.take_along_axis(x, order, axis=1)

            spot = SLOT * (groups - 1) + MID
            x = jnp.where(lane == 0, lanes(fb[0], -(spot - 2)), fan[...].astype(F32))
            hn[hi] = mirrored(x)[6:8].astype(I32)

            @pl.loop(0, packs)
            def _(m):
                for part in range(16 // groups):
                    k = packs * part + m
                    for i in range(2):
                        x = jnp.where(lane == 0, lanes(fb[m], -(span * part + spot + 2 * i)), fa[i, k])
                        h[i, k, hi] = mirrored(x)[6:8]

        eastward.wait_send()
        westward.wait_send()

        @pl.when(has_south)
        def _():
            for copy in southward:
                copy.wait_send()

        @pl.when(has_north)
        def _():
            for copy in northward:
                copy.wait_send()

        @pl.when(top)
        def _():
            for copy in folded:
                copy.wait_send()

        @pl.when(top_far)
        def _():
            folded_next.wait_send()

    return kernel


def make_edge_kernel(levels, rows):
    top_row = PAD + rows
    unroll = 4

    def kernel(t_part, s_part, q, v, n, h, hv, hn, t_out, s_out, ey, done, sem):
        parts = (t_part, s_part)
        outs = (t_out, s_out)
        row = lax.broadcasted_iota(I32, (8, 128), 0)
        inner = pl.ds(8, rows - 16)
        south, north = pl.ds(0, 8), pl.ds(rows - 8, 8)
        stores = [
            pltpu.make_async_copy(parts[i].at[:, inner], outs[i].at[:, inner], sem.at[i]) for i in range(2)
        ]
        for store in stores:
            store.start()

        def edge_pair(halo, load):
            a = jnp.where(
                row < 2, halo, jnp.where(row < 4, load(PAD - 2), jnp.where(row < 7, load(top_row - 7), rows_by(halo, 1)))
            )
            b = jnp.where(
                row < 1, rows_by(halo, -1), jnp.where(row < 4, load(PAD - 1), jnp.where(row < 6, load(top_row - 6), halo))
            )
            return a, b

        na, nb = edge_pair(hn[...], lambda at: n[pl.ds(at, 8)])
        face_n = jnp.minimum(na, nb)
        used = jnp.logical_or(jnp.logical_or(row == 1, row == 2), jnp.logical_or(row == 5, row == 6))

        @pl.loop(0, levels // unroll)
        def _(block):
            for j in range(unroll):
                k = block * unroll + j
                z = TOTAL_DEPTH * (k.astype(F32) + 0.5) / levels
                pair = [edge_pair(h[i, k], lambda at, i=i: q[i, k, pl.ds(at, 8)]) for i in range(2)]
                ra, rb = [density(pair[0][j], pair[1][j], z) for j in range(2)]
                for i in range(2):
                    ey[2 * i, k] = pair[i][0]
                    ey[2 * i + 1, k] = pair[i][1]
                    ey[4 + i, k] = pair[i][0] + pair[i][1]
                ey[6, k] = ra + rb
                ey[7, k] = rb - ra

        n_south = jnp.where(row < 2, n[pl.ds(PAD, 8)], 0)
        n_north = jnp.where(row > 5, n[pl.ds(top_row - 8, 8)], 0)

        @pl.loop(0, levels // unroll)
        def _(block):
            for j in range(unroll):
                k = block * unroll + j
                kp = jnp.minimum(k + 1, levels - 1)
                km = jnp.maximum(k - 1, 0)
                ends = jnp.logical_or(k == 0, k == levels - 1)
                half_scale = jnp.where(ends, 0.5, 0.25).astype(F32)
                wet = k < face_n
                keep = jnp.logical_and(wet, used)
                c = jnp.where(row < 2, hv[k], jnp.where(row < 4, v[k, pl.ds(PAD - 2, 8)], v[k, pl.ds(top_row - 7, 8)]))
                up, coef = courant_terms(c)
                sk = slope_term(ey[7, k], ey[6, kp] - ey[6, km], half_scale)
                for i in range(2):
                    qa, qb = ey[2 * i, k], ey[2 * i + 1, k]
                    d = jnp.where(wet, qb - qa, 0.0)
                    zsum = ey[4 + i, kp] - ey[4 + i, km]
                    f = tracer_flux(keep, c, up, coef, sk, qa, qb, d, rows_by(d, 1), rows_by(d, -1), zsum)
                    change = f - rows_by(f, -1)
                    done[2 * i, k] = parts[i][k, south] + jnp.where(k < n_south, rows_by(change, -1), 0.0)
                    done[2 * i + 1, k] = parts[i][k, north] + jnp.where(k < n_north, rows_by(change, 2), 0.0)

        for i in range(2):
            stores.append(pltpu.make_async_copy(done.at[2 * i], outs[i].at[:, south], sem.at[2 + 2 * i]))
            stores.append(pltpu.make_async_copy(done.at[2 * i + 1], outs[i].at[:, north], sem.at[3 + 2 * i]))
        for store in stores[2:]:
            store.start()
        for store in stores:
            store.wait()

    return kernel


def solution(mesh):
    nlon, nlat = mesh.shape["lon"], mesh.shape["lat"]

    def body(t, s, u, v, n):
        levels, rows, cols = t.shape
        packs = levels // (16 // (rows // 8))
        tall = rows + 2 * PAD
        plain = jax.ShapeDtypeStruct((levels, rows, cols), F32)
        parts = pl.pallas_call(
            make_kernel(nlon, nlat, levels, rows),
            out_shape=(
                pltpu.VMEM((levels, rows, cols), F32),
                pltpu.VMEM((levels, rows, cols), F32),
                pltpu.VMEM((2, levels, tall, cols), F32),
                pltpu.VMEM((levels, tall, cols), F32),
                pltpu.VMEM((tall, cols), I32),
                pltpu.VMEM((2, levels, 8, cols), F32),
                pltpu.VMEM((levels, 8, cols), F32),
                pltpu.VMEM((8, cols), I32),
            ),
            in_specs=[pl.BlockSpec(memory_space=pl.ANY)] * 5,
            out_specs=(pl.BlockSpec(memory_space=pltpu.VMEM),) * 8,
            scratch_shapes=[
                pltpu.VMEM((levels, tall, cols), F32),
                pltpu.VMEM((levels, rows, cols), F32),
                pltpu.VMEM((rows, cols), I32),
                pltpu.VMEM((rows, cols), I32),
                pltpu.VMEM((tall, cols), I32),
                pltpu.VMEM((rows, cols), I32),
                pltpu.VMEM((2, rows + 8, cols), F32),
                pltpu.VMEM((3 * packs + 1, 8, cols), F32),
                pltpu.VMEM((packs, 8, cols), F32),
                pltpu.VMEM((packs, 8, cols), F32),
                pltpu.VMEM((packs, 8, cols), F32),
                pltpu.VMEM((packs, 8, cols), F32),
                pltpu.VMEM((2, levels, 8, cols), F32),
                pltpu.VMEM((packs, 8, cols), F32),
                pltpu.VMEM((8, cols), I32),
                pltpu.VMEM((2, packs, 8, cols), F32),
                pltpu.SemaphoreType.DMA((6,)),
                pltpu.SemaphoreType.DMA((13,)),
                pltpu.SemaphoreType.DMA((13,)),
                pltpu.SemaphoreType.REGULAR((4,)),
            ],
            compiler_params=pltpu.CompilerParams(collective_id=0, has_side_effects=True),
            name="tracer_step",
        )(t, s, u, v, n)
        return pl.pallas_call(
            make_edge_kernel(levels, rows),
            out_shape=(plain, plain),
            in_specs=[pl.BlockSpec(memory_space=pltpu.VMEM)] * 8,
            out_specs=(pl.BlockSpec(memory_space=pl.ANY),) * 2,
            scratch_shapes=[
                pltpu.VMEM((8, levels, 8, cols), F32),
                pltpu.VMEM((4, levels, 8, cols), F32),
                pltpu.SemaphoreType.DMA((6,)),
            ],
            name="edge_rows",
        )(*[pltpu.with_memory_space_constraint(part, pltpu.VMEM) for part in parts])

    spec = P(None, "lat", "lon")
    return jax.shard_map(
        body, mesh=mesh, in_specs=(spec,) * 4 + (P("lat", "lon"),), out_specs=(spec, spec), check_vma=False
    )
```

```python
import jax
import jax.numpy as jnp
from jax import lax
from jax.experimental import pallas as pl
from jax.experimental.pallas import tpu as pltpu
from jax.sharding import PartitionSpec as P

ALPHA = 0.1655
BETA = 0.76554
CABBELING = 0.05952
LAMBDA_SALT = 0.00054914
THERMOBARIC = 0.0001497
PRESS_SALT = 1.109e-05
CROSS = 0.0024341
TOTAL_DEPTH = 5000.0
KAPPA = 0.1
SLOPE_MAX = 1.0
STRAT_MIN = 0.1

MESH = pl.DeviceIdType.MESH
F32 = jnp.float32
I32 = jnp.int32

PAD = 8
SLOT = 8
MID = 3


def density(t, s, z):
    lead = -ALPHA - (ALPHA * THERMOBARIC) * z
    salt = BETA - (BETA * PRESS_SALT) * z
    return t * (lead + (-0.5 * ALPHA * CABBELING) * t - CROSS * s) + s * (salt - (0.5 * BETA * LAMBDA_SALT) * s)


def slope_term(rho_diff, rho_zsum, half_scale):
    strat = jnp.maximum(half_scale * rho_zsum, STRAT_MIN)
    slope = jnp.clip(-rho_diff / strat, -SLOPE_MAX, SLOPE_MAX)
    return slope * (KAPPA * half_scale)


def courant_terms(c):
    up = c > 0.0
    coef = jnp.where(up, 0.5, -0.5) - 0.5 * c
    return up, coef


def tracer_flux(face, c, up, coef, sk, qa, qb, d, back, ahead, zsum):
    step = jnp.where(up, back, ahead)
    limited = jnp.minimum(jnp.maximum(step, jnp.minimum(d, 0.0)), jnp.maximum(d, 0.0))
    adv = c * (jnp.where(up, qa, qb) + coef * limited)
    return jnp.where(face, adv - (KAPPA * d + sk * zsum), 0.0)


def lanes(x, shift):
    return pltpu.roll(x, shift % 128, axis=x.ndim - 1)


def rows_by(x, shift):
    return pltpu.roll(x, shift % 8, axis=x.ndim - 2)


def make_kernel(nlon, nlat, levels, rows):
    groups = rows // 8
    per = 16 // groups
    packs = levels // per
    span = SLOT * groups
    top_row = PAD + rows

    def depth(k):
        return TOTAL_DEPTH * (k + 0.5) / levels

    def kernel(
        t_hbm, s_hbm, u_hbm, v_hbm, n_hbm,
        t_out, s_out, q, v, n, h, hv, hn,
        rho, u, face_x, keep_x, face_y, keep_y, fy,
        px, to_e, to_w, from_w, from_e, fa, fb, fan, ex,
        load_sem, send_sem, recv_sem, late_ready,
    ):
        lon = lax.axis_index("lon")
        lat = lax.axis_index("lat")
        east = lax.rem(lon + 1, nlon)
        west = lax.rem(lon + nlon - 1, nlon)
        has_south = lat > 0
        has_north = lat < nlat - 1
        top = lat == nlat - 1
        mirror = nlon - 1 - lon
        mirror_next = lax.rem(nlon - lon, nlon)
        mirror_far = mirror_next != lon
        top_far = jnp.logical_and(top, mirror_far)
        top_self = jnp.logical_and(top, jnp.logical_not(mirror_far))
        below_top = lat == nlat - 2
        plain = jnp.logical_not(top)
        half, quarter = nlon // 2, nlon // 4
        place = lax.rem(lon, half)
        early = place < quarter
        late_west = place == 0
        late_east = place == quarter - 1
        early_west = place == quarter
        early_east = place == half - 1
        mirror_late = jnp.logical_and(top, early)
        mirror_early = jnp.logical_and(top, jnp.logical_not(early))
        next_late = jnp.logical_and(top_far, early)
        next_early = jnp.logical_and(top_far, place > quarter)
        next_same = jnp.logical_and(top_far, place == quarter)

        barrier = pltpu.get_barrier_semaphore()

        def greet(device):
            pl.semaphore_signal(barrier, inc=1, device_id=device, device_id_type=MESH)

        def when(condition, *steps):
            @pl.when(condition)
            def _():
                for step in steps:
                    step()

        def both(a, b):
            return jnp.logical_or(a, b)

        when(has_south, lambda: greet({"lat": lat - 1}))
        when(jnp.logical_and(has_north, jnp.logical_not(below_top)), lambda: greet({"lat": lat + 1}))
        when(mirror_late, lambda: greet({"lon": mirror}))
        when(both(next_late, next_same), lambda: greet({"lon": mirror_next}))
        when(jnp.logical_not(early_east), lambda: greet({"lon": east}))
        when(jnp.logical_not(early_west), lambda: greet({"lon": west}))

        body_rows = pl.ds(PAD, rows)
        loads = [
            pltpu.make_async_copy(n_hbm, n.at[body_rows], load_sem.at[0]),
            pltpu.make_async_copy(t_hbm, q.at[0, :, body_rows], load_sem.at[1]),
            pltpu.make_async_copy(s_hbm, q.at[1, :, body_rows], load_sem.at[2]),
            pltpu.make_async_copy(u_hbm, u, load_sem.at[3]),
            pltpu.make_async_copy(v_hbm, v.at[:, body_rows], load_sem.at[4]),
        ]
        for load in loads:
            load.start()

        lane = lax.broadcasted_iota(I32, (8, 128), 1)
        row = lax.broadcasted_iota(I32, (8, 128), 0)
        slot_of = lane // SLOT
        sl = lane % SLOT

        greetings = (
            jnp.logical_and(has_south, plain), has_north, mirror_early, both(next_early, next_same),
            jnp.logical_not(late_west), jnp.logical_not(late_east),
        )

        def meet():
            pl.semaphore_wait(barrier, sum(one.astype(I32) for one in greetings))

        def tell(index, device):
            return lambda: pl.semaphore_signal(
                late_ready.at[index], inc=1, device_id=device, device_id_type=MESH
            )

        def remote(src, dst, index, device):
            return pltpu.make_async_remote_copy(
                src_ref=src, dst_ref=dst, send_sem=send_sem.at[index], recv_sem=recv_sem.at[index],
                device_id=device, device_id_type=MESH,
            )

        first, last = pl.ds(0, 2), pl.ds(rows - 2, 2)
        fold = pl.ds(rows - 3, 2)
        fold_in_group = pl.ds(5, 2)
        lo, hi = pl.ds(0, 2), pl.ds(6, 2)
        northward = [
            remote(t_hbm.at[:, last], h.at[0, :, lo], 0, {"lat": lat + 1}),
            remote(s_hbm.at[:, last], h.at[1, :, lo], 1, {"lat": lat + 1}),
            remote(v_hbm.at[:, pl.ds(rows - 1, 1)], hv.at[:, pl.ds(1, 1)], 2, {"lat": lat + 1}),
            remote(n_hbm.at[last], hn.at[lo], 3, {"lat": lat + 1}),
        ]
        southward = [
            remote(t_hbm.at[:, first], h.at[0, :, hi], 4, {"lat": lat - 1}),
            remote(s_hbm.at[:, first], h.at[1, :, hi], 5, {"lat": lat - 1}),
            remote(n_hbm.at[first], hn.at[hi], 6, {"lat": lat - 1}),
        ]
        folded = [
            remote(t_hbm.at[:, fold], fa.at[0, :, hi], 7, {"lon": mirror}),
            remote(s_hbm.at[:, fold], fa.at[1, :, hi], 8, {"lon": mirror}),
            remote(n_hbm.at[fold], fan.at[hi], 9, {"lon": mirror}),
        ]
        folded_next = remote(to_w.at[:, fold_in_group], fb.at[:, hi], 10, {"lon": mirror_next})
        own_next = pltpu.make_async_copy(to_w.at[:, fold_in_group], fb.at[:, hi], load_sem.at[5])
        eastward = remote(to_e, from_w, 11, {"lon": east})
        westward = remote(to_w, from_e, 12, {"lon": west})

        @pl.when(top)
        def _():
            meet()
            when(mirror_early, *[copy.start for copy in folded], tell(0, {"lon": mirror}))
            when(next_early, tell(1, {"lon": mirror_next}))
            when(early_east, tell(2, {"lon": east}))
            when(early_west, tell(3, {"lon": west}))

        for load in loads[:4]:
            load.wait()
        packed_n = jnp.zeros((8, 128), F32)
        for slot in range(16):
            part = n[pl.ds(PAD + 8 * (slot % groups), 8)].astype(F32)
            packed_n = jnp.where(slot_of == slot, lanes(part, SLOT * slot + MID), packed_n)
        px[2 * packs] = packed_n
        n_up, n_down = lanes(packed_n, 5), lanes(packed_n, -2)

        @pl.loop(0, packs)
        def _(m):
            packed = []
            for field in range(3):
                one = jnp.zeros((8, 128), F32)
                for slot in range(16):
                    k = packs * (slot // groups) + m
                    g = slot % groups
                    if field < 2:
                        part = q[field, k, pl.ds(PAD + 8 * g, 8)]
                    else:
                        part = u[k, pl.ds(8 * g, 8)]
                    one = jnp.where(slot_of == slot, lanes(part, SLOT * slot + MID), one)
                px[(0, packs, 2 * packs + 1)[field] + m] = one
                packed.append(one)
            t2, s2, u2 = packed
            s_up = lanes(s2, 2)
            to_e[m] = jnp.where(sl < 3, t2, jnp.where(sl < 5, s_up, jnp.where(sl < 6, lanes(u2, 3), n_up)))
            to_w[m] = jnp.where(sl < 3, n_down, jnp.where(sl < 5, t2, s_up))

        when(top_self, own_next.start)
        def send_columns():
            when(jnp.logical_not(late_east), eastward.start)
            when(jnp.logical_not(late_west), westward.start)

        @pl.when(top)
        def _():
            when(both(next_early, next_same), folded_next.start)
            send_columns()

        @pl.loop(0, levels)
        def _(k):
            z = depth(k.astype(F32))
            for g in range(groups):
                at = pl.ds(PAD + 8 * g, 8)
                rho[k, at] = density(q[0, k, at], q[1, k, at], z)

        pad_n = jnp.zeros((8, 128), I32)
        n[pl.ds(0, 8)] = pad_n
        n[pl.ds(top_row, 8)] = pad_n
        for g in range(groups):
            at = pl.ds(PAD + 8 * g, 8)
            here = n[at]
            fx = jnp.minimum(here, lanes(here, 1))
            face_x[pl.ds(8 * g, 8)] = fx
            inner = jnp.logical_and(lane > 1, lane < 127)
            keep_x[pl.ds(8 * g, 8)] = jnp.where(inner, fx, 0)
            f = jnp.minimum(here, n[pl.ds(PAD + 8 * g - 1, 8)])
            face_y[at] = f
            if g == 0:
                f = jnp.where(row > 1, f, 0)
            if g == groups - 1:
                f = jnp.where(row < 7, f, 0)
            keep_y[pl.ds(8 * g, 8)] = f
        face_y[pl.ds(0, 8)] = pad_n
        face_y[pl.ds(top_row, 8)] = pad_n

        @pl.when(plain)
        def _():
            meet()
            send_columns()
            when(early_east, tell(2, {"lon": east}))
            when(early_west, tell(3, {"lon": west}))
            when(below_top, tell(4, {"lat": lat + 1}))
            when(has_south, *[copy.start for copy in southward])
            when(has_north, *[copy.start for copy in northward])

        outs = (t_out, s_out)
        loads[4].wait()
        fy[0, pl.ds(rows, 8)] = jnp.zeros((8, 128), F32)
        fy[1, pl.ds(rows, 8)] = jnp.zeros((8, 128), F32)

        def interior(k):
            kp = jnp.minimum(k + 1, levels - 1)
            km = jnp.maximum(k - 1, 0)
            ends = jnp.logical_or(k == 0, k == levels - 1)
            half_scale = jnp.where(ends, 0.5, 0.25).astype(F32)

            for g in reversed(range(groups)):
                r = PAD + 8 * g
                at, dn = pl.ds(r, 8), pl.ds(r - 1, 8)
                t0 = [q[i, k, at] for i in range(2)]
                zd = [q[i, kp, at] - q[i, km, at] for i in range(2)]
                rho0 = rho[k, at]
                rz = rho[kp, at] - rho[km, at]

                wet = k < face_x[pl.ds(8 * g, 8)]
                keep = k < keep_x[pl.ds(8 * g, 8)]
                c = lanes(u[k, pl.ds(8 * g, 8)], 1)
                up, coef = courant_terms(c)
                sk = slope_term(rho0 - lanes(rho0, 1), rz + lanes(rz, 1), half_scale)
                total = []
                for i in range(2):
                    qa = lanes(t0[i], 1)
                    d = jnp.where(wet, t0[i] - qa, 0.0)
                    f = tracer_flux(keep, c, up, coef, sk, qa, t0[i], d, lanes(d, 1), lanes(d, -1), zd[i] + lanes(zd[i], 1))
                    total.append(t0[i] + (f - lanes(f, -1)))

                wet = k < face_y[at]
                wet_back = k < face_y[dn]
                wet_ahead = k < face_y[pl.ds(r + 1, 8)]
                keep = k < keep_y[pl.ds(8 * g, 8)]
                c = v[k, dn]
                up, coef = courant_terms(c)
                sk = slope_term(rho0 - rho[k, dn], rz + (rho[kp, dn] - rho[km, dn]), half_scale)
                here = k < n[at]
                for i in range(2):
                    qa = q[i, k, dn]
                    d = jnp.where(wet, t0[i] - qa, 0.0)
                    back = jnp.where(wet_back, qa - q[i, k, pl.ds(r - 2, 8)], 0.0)
                    ahead = jnp.where(wet_ahead, q[i, k, pl.ds(r + 1, 8)] - t0[i], 0.0)
                    zsum = zd[i] + (q[i, kp, dn] - q[i, km, dn])
                    f = tracer_flux(keep, c, up, coef, sk, qa, t0[i], d, back, ahead, zsum)
                    fy[i, pl.ds(8 * g, 8)] = f
                    f_north = fy[i, pl.ds(8 * g + 1, 8)]
                    outs[i][k, pl.ds(8 * g, 8)] = jnp.where(here, total[i] + (f - f_north), 0.0)

        def heard(index):
            return lambda: pl.semaphore_wait(late_ready.at[index], 1)

        pl.loop(0, levels // 2)(interior)
        when(top, heard(4), *[copy.start for copy in southward])
        pl.loop(levels // 2, levels)(interior)

        when(late_east, heard(3), eastward.start)
        when(late_west, heard(2), westward.start)
        when(mirror_late, heard(0), *[copy.start for copy in folded])
        when(next_late, heard(1), folded_next.start)

        def edge_rows():
            @pl.when(jnp.logical_not(has_south))
            def _():
                hn[lo] = jnp.zeros((2, 128), I32)

                @pl.loop(0, levels)
                def _(k):
                    h[0, k, lo] = jnp.zeros((2, 128), F32)
                    h[1, k, lo] = jnp.zeros((2, 128), F32)
                    hv[k, lo] = jnp.zeros((2, 128), F32)

            @pl.when(has_south)
            def _():
                for copy in northward:
                    copy.wait_recv()

            @pl.when(has_north)
            def _():
                for copy in southward:
                    copy.wait_recv()

            @pl.when(top)
            def _():
                for copy in folded:
                    copy.wait_recv()

            @pl.when(top_far)
            def _():
                folded_next.wait_recv()

            @pl.when(top_self)
            def _():
                own_next.wait()

            @pl.when(top)
            def _():
                order = lax.rem(128 - lane, 128)

                def mirrored(x):
                    x = jnp.where(row == 6, rows_by(x, -1), rows_by(x, 1))
                    return jnp.take_along_axis(x, order, axis=1)

                spot = SLOT * (groups - 1) + MID
                x = jnp.where(lane == 0, lanes(fb[0], -(spot - 2)), fan[...].astype(F32))
                hn[hi] = mirrored(x)[6:8].astype(I32)

                @pl.loop(0, packs)
                def _(m):
                    for part in range(16 // groups):
                        k = packs * part + m
                        for i in range(2):
                            x = jnp.where(lane == 0, lanes(fb[m], -(span * part + spot + 2 * i)), fa[i, k])
                            h[i, k, hi] = mirrored(x)[6:8]

        when(late_west, edge_rows)

        eastward.wait_recv()
        westward.wait_recv()

        def joined(own, before, after):
            left = jnp.where(sl < MID, before, own)
            right = own if after is None else jnp.where(sl < MID, own, after)
            a = jnp.where(sl < 4, lanes(left, -1), lanes(right, 4))
            b = jnp.where(sl < 4, lanes(left, -2), lanes(right, 3))
            return a, b

        na, nb = joined(px[2 * packs], lanes(from_w[0], -5), lanes(from_e[0], 2))
        face_n = jnp.minimum(na, nb)
        level_of = packs * (lane // span)
        pairs = [
            [joined(px[m], from_w[m], from_e[m]) for m in range(packs)],
            [joined(px[packs + m], lanes(from_w[m], -2), lanes(from_e[m], -2)) for m in range(packs)],
        ]
        rho_pairs = []
        for m in range(packs):
            z = depth((level_of + m).astype(F32))
            rho_pairs.append([density(pairs[0][m][j], pairs[1][m][j], z) for j in range(2)])
        sums = [[a + b for a, b in one] for one in (*pairs, rho_pairs)]

        def zsum_of(one, m):
            if m < packs - 1:
                above = one[m + 1]
            else:
                above = jnp.where(lane < 128 - span, lanes(one[0], -span), one[m])
            if m > 0:
                below = one[m - 1]
            else:
                below = jnp.where(lane < span, one[0], lanes(one[packs - 1], span))
            return above - below

        used = jnp.logical_or(jnp.logical_or(sl == 1, sl == 2), jnp.logical_or(sl == 5, sl == 6))
        for m in range(packs):
            level = level_of + m
            half_scale = jnp.where(jnp.logical_or(level == 0, level == levels - 1), 0.5, 0.25)
            wet = level.astype(F32) < face_n
            keep = jnp.logical_and(wet, used)
            c = joined(px[2 * packs + 1 + m], lanes(from_w[m], -3), None)[0]
            up, coef = courant_terms(c)
            sk = slope_term(rho_pairs[m][1] - rho_pairs[m][0], zsum_of(sums[2], m), half_scale)
            for i in range(2):
                qa, qb = pairs[i][m]
                d = jnp.where(wet, qb - qa, 0.0)
                f = tracer_flux(keep, c, up, coef, sk, qa, qb, d, lanes(d, 1), lanes(d, -1), zsum_of(sums[i], m))
                change = f - lanes(f, -1)
                change = jnp.where(sl < MID, lanes(change, -3), lanes(change, 2))
                ex[i, m] = jnp.where(level.astype(F32) < px[2 * packs], change, 0.0)

        ends_x = jnp.logical_or(lane < 2, lane > 125)

        for m in range(packs):
            for i in range(2):
                packed = ex[i, m]
                for slot in range(16):
                    k = packs * (slot // groups) + m
                    at = pl.ds(8 * (slot % groups), 8)
                    outs[i][k, at] = outs[i][k, at] + jnp.where(ends_x, lanes(packed, -(SLOT * slot + MID)), 0.0)

        when(jnp.logical_not(late_west), edge_rows)

        eastward.wait_send()
        westward.wait_send()

        @pl.when(has_south)
        def _():
            for copy in southward:
                copy.wait_send()

        @pl.when(has_north)
        def _():
            for copy in northward:
                copy.wait_send()

        @pl.when(top)
        def _():
            for copy in folded:
                copy.wait_send()

        @pl.when(top_far)
        def _():
            folded_next.wait_send()

    return kernel


def make_edge_kernel(levels, rows):
    top_row = PAD + rows
    pieces = 2

    def kernel(t_part, s_part, q, v, n, h, hv, hn, t_out, s_out, done, sem, end_sem):
        parts = (t_part, s_part)
        outs = (t_out, s_out)
        row = lax.broadcasted_iota(I32, (8, 128), 0)
        inner = pl.ds(8, rows - 16)
        ends = (pl.ds(0, 8), pl.ds(rows - 8, 8))
        stores = [
            pltpu.make_async_copy(parts[i].at[:, inner], outs[i].at[:, inner], sem.at[i]) for i in range(2)
        ]
        for store in stores:
            store.start()

        def edge_pair(halo, load):
            a = jnp.where(
                row < 2, halo, jnp.where(row < 4, load(PAD - 2), jnp.where(row < 7, load(top_row - 7), rows_by(halo, 1)))
            )
            b = jnp.where(
                row < 1, rows_by(halo, -1), jnp.where(row < 4, load(PAD - 1), jnp.where(row < 6, load(top_row - 6), halo))
            )
            return a, b

        na, nb = edge_pair(hn[...], lambda at: n[pl.ds(at, 8)])
        face_n = jnp.minimum(na, nb)
        used = jnp.logical_or(jnp.logical_or(row == 1, row == 2), jnp.logical_or(row == 5, row == 6))
        keep_n = jnp.where(used, face_n, 0)
        cell_n = (jnp.where(row < 2, n[pl.ds(PAD, 8)], 0), jnp.where(row > 5, n[pl.ds(top_row - 8, 8)], 0))

        def level(k):
            pair = [edge_pair(h[i, k], lambda at, i=i: q[i, k, pl.ds(at, 8)]) for i in range(2)]
            ra, rb = [density(pair[0][j], pair[1][j], TOTAL_DEPTH * (k + 0.5) / levels) for j in range(2)]
            return pair, [pair[0][0] + pair[0][1], pair[1][0] + pair[1][1], ra + rb], rb - ra

        held = [level(0), level(1)]
        for k in range(levels):
            below, above = held[max(k - 1, 0)][1], held[min(k + 1, levels - 1)][1]
            pair, _, rho_diff = held[k]
            half_scale = 0.5 if k in (0, levels - 1) else 0.25
            wet, keep = k < face_n, k < keep_n
            c = jnp.where(row < 2, hv[k], jnp.where(row < 4, v[k, pl.ds(PAD - 2, 8)], v[k, pl.ds(top_row - 7, 8)]))
            up, coef = courant_terms(c)
            sk = slope_term(rho_diff, above[2] - below[2], half_scale)
            for i in range(2):
                qa, qb = pair[i]
                d = jnp.where(wet, qb - qa, 0.0)
                f = tracer_flux(keep, c, up, coef, sk, qa, qb, d, rows_by(d, 1), rows_by(d, -1), above[i] - below[i])
                change = f - rows_by(f, -1)
                for e, shift in enumerate((-1, 2)):
                    done[2 * i + e, k] = parts[i][k, ends[e]] + jnp.where(k < cell_n[e], rows_by(change, shift), 0.0)
            if k + 2 < levels:
                held.append(level(k + 2))
            if (k + 1) % (levels // pieces) == 0:
                some = pl.ds(k + 1 - levels // pieces, levels // pieces)
                for i in range(2):
                    for e in range(2):
                        piece = pltpu.make_async_copy(
                            done.at[2 * i + e, some], outs[i].at[some, ends[e]],
                            end_sem.at[2 * i + e, k // (levels // pieces)],
                        )
                        piece.start()
                        stores.append(piece)
        for store in stores:
            store.wait()

    return kernel


def solution(mesh):
    nlon, nlat = mesh.shape["lon"], mesh.shape["lat"]

    def body(t, s, u, v, n):
        levels, rows, cols = t.shape
        packs = levels // (16 // (rows // 8))
        tall = rows + 2 * PAD
        plain = jax.ShapeDtypeStruct((levels, rows, cols), F32)
        parts = pl.pallas_call(
            make_kernel(nlon, nlat, levels, rows),
            out_shape=(
                pltpu.VMEM((levels, rows, cols), F32),
                pltpu.VMEM((levels, rows, cols), F32),
                pltpu.VMEM((2, levels, tall, cols), F32),
                pltpu.VMEM((levels, tall, cols), F32),
                pltpu.VMEM((tall, cols), I32),
                pltpu.VMEM((2, levels, 8, cols), F32),
                pltpu.VMEM((levels, 8, cols), F32),
                pltpu.VMEM((8, cols), I32),
            ),
            in_specs=[pl.BlockSpec(memory_space=pl.ANY)] * 5,
            out_specs=(pl.BlockSpec(memory_space=pltpu.VMEM),) * 8,
            scratch_shapes=[
                pltpu.VMEM((levels, tall, cols), F32),
                pltpu.VMEM((levels, rows, cols), F32),
                pltpu.VMEM((rows, cols), I32),
                pltpu.VMEM((rows, cols), I32),
                pltpu.VMEM((tall, cols), I32),
                pltpu.VMEM((rows, cols), I32),
                pltpu.VMEM((2, rows + 8, cols), F32),
                pltpu.VMEM((3 * packs + 1, 8, cols), F32),
                pltpu.VMEM((packs, 8, cols), F32),
                pltpu.VMEM((packs, 8, cols), F32),
                pltpu.VMEM((packs, 8, cols), F32),
                pltpu.VMEM((packs, 8, cols), F32),
                pltpu.VMEM((2, levels, 8, cols), F32),
                pltpu.VMEM((packs, 8, cols), F32),
                pltpu.VMEM((8, cols), I32),
                pltpu.VMEM((2, packs, 8, cols), F32),
                pltpu.SemaphoreType.DMA((6,)),
                pltpu.SemaphoreType.DMA((13,)),
                pltpu.SemaphoreType.DMA((13,)),
                pltpu.SemaphoreType.REGULAR((5,)),
            ],
            compiler_params=pltpu.CompilerParams(collective_id=0, has_side_effects=True),
            name="tracer_step",
        )(t, s, u, v, n)
        return pl.pallas_call(
            make_edge_kernel(levels, rows),
            out_shape=(plain, plain),
            in_specs=[pl.BlockSpec(memory_space=pltpu.VMEM)] * 8,
            out_specs=(pl.BlockSpec(memory_space=pl.ANY),) * 2,
            scratch_shapes=[
                pltpu.VMEM((4, levels, 8, cols), F32),
                pltpu.SemaphoreType.DMA((2,)),
                pltpu.SemaphoreType.DMA((4, 2)),
            ],
            name="edge_rows",
        )(*[pltpu.with_memory_space_constraint(part, pltpu.VMEM) for part in parts])

    spec = P(None, "lat", "lon")
    return jax.shard_map(
        body, mesh=mesh, in_specs=(spec,) * 4 + (P("lat", "lon"),), out_specs=(spec, spec), check_vma=False
    )
```

```python
import jax
import jax.numpy as jnp
from jax import lax
from jax.experimental import pallas as pl
from jax.experimental.pallas import tpu as pltpu
from jax.sharding import PartitionSpec as P

ALPHA = 0.1655
BETA = 0.76554
CABBELING = 0.05952
LAMBDA_SALT = 0.00054914
THERMOBARIC = 0.0001497
PRESS_SALT = 1.109e-05
CROSS = 0.0024341
TOTAL_DEPTH = 5000.0
KAPPA = 0.1
SLOPE_MAX = 1.0
STRAT_MIN = 0.1

MESH = pl.DeviceIdType.MESH
F32 = jnp.float32
I32 = jnp.int32

PAD = 8
SLOT = 8
MID = 3


def density(t, s, z):
    lead = -ALPHA - (ALPHA * THERMOBARIC) * z
    salt = BETA - (BETA * PRESS_SALT) * z
    return t * (lead + (-0.5 * ALPHA * CABBELING) * t - CROSS * s) + s * (salt - (0.5 * BETA * LAMBDA_SALT) * s)


def slope_term(rho_diff, rho_zsum, half_scale):
    strat = jnp.maximum(half_scale * rho_zsum, STRAT_MIN)
    slope = jnp.clip(-rho_diff / strat, -SLOPE_MAX, SLOPE_MAX)
    return slope * (KAPPA * half_scale)


def courant_terms(c):
    up = c > 0.0
    coef = jnp.where(up, 0.5, -0.5) - 0.5 * c
    return up, coef


def tracer_flux(face, c, up, coef, sk, qa, qb, d, back, ahead, zsum):
    step = jnp.where(up, back, ahead)
    limited = jnp.minimum(jnp.maximum(step, jnp.minimum(d, 0.0)), jnp.maximum(d, 0.0))
    adv = c * (jnp.where(up, qa, qb) + coef * limited)
    return jnp.where(face, adv - (KAPPA * d + sk * zsum), 0.0)


def lanes(x, shift):
    return pltpu.roll(x, shift % 128, axis=x.ndim - 1)


def rows_by(x, shift):
    return pltpu.roll(x, shift % 8, axis=x.ndim - 2)


def edge_rows(north, q, v, n, halo, halo_v, halo_n, levels, rows, emit):
    top_row = PAD + rows
    hop = levels // 2
    row = lax.broadcasted_iota(I32, (8, 128), 0)
    low, place = row < 4, row % 4

    def own(load, m, base):
        return jnp.where(low, load(m, base), load(m + hop, base - 4))

    def pair(halo, load, m):
        if north:
            a = jnp.where(place == 3, rows_by(halo, 1), own(load, m, top_row - 3))
            b = jnp.where(place > 1, halo, own(load, m, top_row - 2))
        else:
            a = jnp.where(place < 2, halo, own(load, m, PAD - 2))
            b = jnp.where(place < 1, rows_by(halo, -1), own(load, m, PAD - 1))
        return a, b

    def load_v(k, base):
        return v[k, pl.ds(base, 8)]

    face_n = jnp.minimum(*pair(halo_n, lambda k, base: n[pl.ds(base, 8)], 0))
    keep_n = jnp.where(jnp.logical_or(place == 1, place == 2), face_n, 0)

    def level(m):
        z = jnp.where(low, TOTAL_DEPTH * (m + 0.5) / levels, TOTAL_DEPTH * (m + hop + 0.5) / levels)
        t, s = [pair(halo(i, m), lambda k, base, i=i: q[i, k, pl.ds(base, 8)], m) for i in range(2)]
        ra, rb = [density(t[j], s[j], z) for j in range(2)]
        return (t, s), (t[0] + t[1], s[0] + s[1], ra + rb), rb - ra

    held = [level(m) for m in range(hop)]
    for m in range(hop):
        tracers, sums, rho_diff = held[m]
        zsums = []
        for j in range(3):
            above = held[m + 1][1][j] if m + 1 < hop else jnp.where(low, rows_by(held[0][1][j], 4), sums[j])
            below = held[m - 1][1][j] if m > 0 else jnp.where(low, sums[j], rows_by(held[hop - 1][1][j], 4))
            zsums.append(above - below)
        half_scale = 0.25
        if m == 0:
            half_scale = jnp.where(low, 0.5, 0.25)
        if m == hop - 1:
            half_scale = jnp.where(low, 0.25, 0.5)
        k = jnp.where(low, m, m + hop)
        wet, keep = k < face_n, k < keep_n
        c = own(load_v, m, top_row - 3) if north else jnp.where(place < 2, halo_v(m), own(load_v, m, PAD - 2))
        up, coef = courant_terms(c)
        sk = slope_term(rho_diff, zsums[2], half_scale)
        for i in range(2):
            qa, qb = tracers[i]
            d = jnp.where(wet, qb - qa, 0.0)
            f = tracer_flux(keep, c, up, coef, sk, qa, qb, d, rows_by(d, 1), rows_by(d, -1), zsums[i])
            change = f - rows_by(f, -1)
            emit(i, m, rows_by(change, 6 if north else -1))
            emit(i, m + hop, rows_by(change, 2 if north else 3))


def make_kernel(nlon, nlat, levels, rows):
    groups = rows // 8
    per = 16 // groups
    packs = levels // per
    span = SLOT * groups
    top_row = PAD + rows

    def depth(k):
        return TOTAL_DEPTH * (k + 0.5) / levels

    def kernel(
        t_hbm, s_hbm, u_hbm, v_hbm, n_hbm,
        t_out, s_out, q, v, n, hp, hn,
        h, hv, hs, h_north, hs_north, rho, u, face_x, keep_x, face_y, keep_y, fy,
        px, to_e, to_w, from_w, from_e, fa, fb, fan, ex,
        load_sem, send_sem, recv_sem, late_ready,
    ):
        lon = lax.axis_index("lon")
        lat = lax.axis_index("lat")
        east = lax.rem(lon + 1, nlon)
        west = lax.rem(lon + nlon - 1, nlon)
        has_south = lat > 0
        has_north = lat < nlat - 1
        top = lat == nlat - 1
        mirror = nlon - 1 - lon
        mirror_next = lax.rem(nlon - lon, nlon)
        mirror_far = mirror_next != lon
        top_far = jnp.logical_and(top, mirror_far)
        top_self = jnp.logical_and(top, jnp.logical_not(mirror_far))
        below_top = lat == nlat - 2
        plain = jnp.logical_not(top)
        half, quarter = nlon // 2, nlon // 4
        place = lax.rem(lon, half)
        early = place < quarter
        late_west = place == 0
        late_east = place == quarter - 1
        early_west = place == quarter
        early_east = place == half - 1
        mirror_late = jnp.logical_and(top, early)
        mirror_early = jnp.logical_and(top, jnp.logical_not(early))
        next_late = jnp.logical_and(top_far, early)
        next_early = jnp.logical_and(top_far, place > quarter)
        next_same = jnp.logical_and(top_far, place == quarter)

        barrier = pltpu.get_barrier_semaphore()

        def greet(device):
            pl.semaphore_signal(barrier, inc=1, device_id=device, device_id_type=MESH)

        def when(condition, *steps):
            @pl.when(condition)
            def _():
                for step in steps:
                    step()

        def both(a, b):
            return jnp.logical_or(a, b)

        when(has_south, lambda: greet({"lat": lat - 1}))
        when(jnp.logical_and(has_north, jnp.logical_not(below_top)), lambda: greet({"lat": lat + 1}))
        when(mirror_late, lambda: greet({"lon": mirror}))
        when(both(next_late, next_same), lambda: greet({"lon": mirror_next}))
        when(jnp.logical_not(early_east), lambda: greet({"lon": east}))
        when(jnp.logical_not(early_west), lambda: greet({"lon": west}))

        body_rows = pl.ds(PAD, rows)
        loads = [
            pltpu.make_async_copy(n_hbm, n.at[body_rows], load_sem.at[0]),
            pltpu.make_async_copy(t_hbm, q.at[0, :, body_rows], load_sem.at[1]),
            pltpu.make_async_copy(s_hbm, q.at[1, :, body_rows], load_sem.at[2]),
            pltpu.make_async_copy(u_hbm, u, load_sem.at[3]),
            pltpu.make_async_copy(v_hbm, v.at[:, body_rows], load_sem.at[4]),
        ]
        for load in loads:
            load.start()

        lane = lax.broadcasted_iota(I32, (8, 128), 1)
        row = lax.broadcasted_iota(I32, (8, 128), 0)
        slot_of = lane // SLOT
        sl = lane % SLOT

        greetings = (
            jnp.logical_and(has_south, plain), has_north, mirror_early, both(next_early, next_same),
            jnp.logical_not(late_west), jnp.logical_not(late_east),
        )

        def meet():
            pl.semaphore_wait(barrier, sum(one.astype(I32) for one in greetings))

        def tell(index, device):
            return lambda: pl.semaphore_signal(
                late_ready.at[index], inc=1, device_id=device, device_id_type=MESH
            )

        def remote(src, dst, index, device):
            return pltpu.make_async_remote_copy(
                src_ref=src, dst_ref=dst, send_sem=send_sem.at[index], recv_sem=recv_sem.at[index],
                device_id=device, device_id_type=MESH,
            )

        first, last = pl.ds(0, 2), pl.ds(rows - 2, 2)
        fold = pl.ds(rows - 3, 2)
        fold_in_group = pl.ds(5, 2)
        lo, hi = pl.ds(0, 2), pl.ds(6, 2)
        northward = [
            remote(t_hbm.at[:, last], h.at[0, :, lo], 0, {"lat": lat + 1}),
            remote(s_hbm.at[:, last], h.at[1, :, lo], 1, {"lat": lat + 1}),
            remote(v_hbm.at[:, pl.ds(rows - 1, 1)], hv.at[:, pl.ds(1, 1)], 2, {"lat": lat + 1}),
            remote(n_hbm.at[last], hs.at[lo], 3, {"lat": lat + 1}),
        ]
        southward = [
            remote(t_hbm.at[:, first], h_north.at[0, :, hi], 4, {"lat": lat - 1}),
            remote(s_hbm.at[:, first], h_north.at[1, :, hi], 5, {"lat": lat - 1}),
            remote(n_hbm.at[first], hs_north.at[hi], 6, {"lat": lat - 1}),
        ]
        folded = [
            remote(t_hbm.at[:, fold], fa.at[0, :, hi], 7, {"lon": mirror}),
            remote(s_hbm.at[:, fold], fa.at[1, :, hi], 8, {"lon": mirror}),
            remote(n_hbm.at[fold], fan.at[hi], 9, {"lon": mirror}),
        ]
        folded_next = remote(to_w.at[:, fold_in_group], fb.at[:, hi], 10, {"lon": mirror_next})
        own_next = pltpu.make_async_copy(to_w.at[:, fold_in_group], fb.at[:, hi], load_sem.at[5])
        eastward = remote(to_e, from_w, 11, {"lon": east})
        westward = remote(to_w, from_e, 12, {"lon": west})

        @pl.when(top)
        def _():
            meet()
            when(mirror_early, *[copy.start for copy in folded], tell(0, {"lon": mirror}))
            when(next_early, tell(1, {"lon": mirror_next}))
            when(early_east, tell(2, {"lon": east}))
            when(early_west, tell(3, {"lon": west}))

        for load in loads[:4]:
            load.wait()
        packed_n = jnp.zeros((8, 128), F32)
        for slot in range(16):
            part = n[pl.ds(PAD + 8 * (slot % groups), 8)].astype(F32)
            packed_n = jnp.where(slot_of == slot, lanes(part, SLOT * slot + MID), packed_n)
        px[2 * packs] = packed_n
        n_up, n_down = lanes(packed_n, 5), lanes(packed_n, -2)

        @pl.loop(0, packs)
        def _(m):
            packed = []
            for field in range(3):
                one = jnp.zeros((8, 128), F32)
                for slot in range(16):
                    k = packs * (slot // groups) + m
                    g = slot % groups
                    if field < 2:
                        part = q[field, k, pl.ds(PAD + 8 * g, 8)]
                    else:
                        part = u[k, pl.ds(8 * g, 8)]
                    one = jnp.where(slot_of == slot, lanes(part, SLOT * slot + MID), one)
                px[(0, packs, 2 * packs + 1)[field] + m] = one
                packed.append(one)
            t2, s2, u2 = packed
            s_up = lanes(s2, 2)
            to_e[m] = jnp.where(sl < 3, t2, jnp.where(sl < 5, s_up, jnp.where(sl < 6, lanes(u2, 3), n_up)))
            to_w[m] = jnp.where(sl < 3, n_down, jnp.where(sl < 5, t2, s_up))

        when(top_self, own_next.start)
        def send_columns():
            when(jnp.logical_not(late_east), eastward.start)
            when(jnp.logical_not(late_west), westward.start)

        @pl.when(top)
        def _():
            when(both(next_early, next_same), folded_next.start)
            send_columns()

        @pl.loop(0, levels)
        def _(k):
            z = depth(k.astype(F32))
            for g in range(groups):
                at = pl.ds(PAD + 8 * g, 8)
                rho[k, at] = density(q[0, k, at], q[1, k, at], z)

        pad_n = jnp.zeros((8, 128), I32)
        n[pl.ds(0, 8)] = pad_n
        n[pl.ds(top_row, 8)] = pad_n
        for g in range(groups):
            at = pl.ds(PAD + 8 * g, 8)
            here = n[at]
            fx = jnp.minimum(here, lanes(here, 1))
            face_x[pl.ds(8 * g, 8)] = fx
            inner = jnp.logical_and(lane > 1, lane < 127)
            keep_x[pl.ds(8 * g, 8)] = jnp.where(inner, fx, 0)
            f = jnp.minimum(here, n[pl.ds(PAD + 8 * g - 1, 8)])
            face_y[at] = f
            if g == 0:
                f = jnp.where(row > 1, f, 0)
            if g == groups - 1:
                f = jnp.where(row < 7, f, 0)
            keep_y[pl.ds(8 * g, 8)] = f
        face_y[pl.ds(0, 8)] = pad_n
        face_y[pl.ds(top_row, 8)] = pad_n

        @pl.when(plain)
        def _():
            meet()
            send_columns()
            when(early_east, tell(2, {"lon": east}))
            when(early_west, tell(3, {"lon": west}))
            when(below_top, tell(4, {"lat": lat + 1}))
            when(has_south, *[copy.start for copy in southward])
            when(has_north, *[copy.start for copy in northward])

        outs = (t_out, s_out)
        loads[4].wait()
        fy[0, pl.ds(rows, 8)] = jnp.zeros((8, 128), F32)
        fy[1, pl.ds(rows, 8)] = jnp.zeros((8, 128), F32)

        def interior(k):
            kp = jnp.minimum(k + 1, levels - 1)
            km = jnp.maximum(k - 1, 0)
            ends = jnp.logical_or(k == 0, k == levels - 1)
            half_scale = jnp.where(ends, 0.5, 0.25).astype(F32)

            for g in reversed(range(groups)):
                r = PAD + 8 * g
                at, dn = pl.ds(r, 8), pl.ds(r - 1, 8)
                t0 = [q[i, k, at] for i in range(2)]
                zd = [q[i, kp, at] - q[i, km, at] for i in range(2)]
                rho0 = rho[k, at]
                rz = rho[kp, at] - rho[km, at]

                wet = k < face_x[pl.ds(8 * g, 8)]
                keep = k < keep_x[pl.ds(8 * g, 8)]
                c = lanes(u[k, pl.ds(8 * g, 8)], 1)
                up, coef = courant_terms(c)
                sk = slope_term(rho0 - lanes(rho0, 1), rz + lanes(rz, 1), half_scale)
                total = []
                for i in range(2):
                    qa = lanes(t0[i], 1)
                    d = jnp.where(wet, t0[i] - qa, 0.0)
                    f = tracer_flux(keep, c, up, coef, sk, qa, t0[i], d, lanes(d, 1), lanes(d, -1), zd[i] + lanes(zd[i], 1))
                    total.append(t0[i] + (f - lanes(f, -1)))

                wet = k < face_y[at]
                wet_back = k < face_y[dn]
                wet_ahead = k < face_y[pl.ds(r + 1, 8)]
                keep = k < keep_y[pl.ds(8 * g, 8)]
                c = v[k, dn]
                up, coef = courant_terms(c)
                sk = slope_term(rho0 - rho[k, dn], rz + (rho[kp, dn] - rho[km, dn]), half_scale)
                here = k < n[at]
                for i in range(2):
                    qa = q[i, k, dn]
                    d = jnp.where(wet, t0[i] - qa, 0.0)
                    back = jnp.where(wet_back, qa - q[i, k, pl.ds(r - 2, 8)], 0.0)
                    ahead = jnp.where(wet_ahead, q[i, k, pl.ds(r + 1, 8)] - t0[i], 0.0)
                    zsum = zd[i] + (q[i, kp, dn] - q[i, km, dn])
                    f = tracer_flux(keep, c, up, coef, sk, qa, t0[i], d, back, ahead, zsum)
                    fy[i, pl.ds(8 * g, 8)] = f
                    f_north = fy[i, pl.ds(8 * g + 1, 8)]
                    outs[i][k, pl.ds(8 * g, 8)] = jnp.where(here, total[i] + (f - f_north), 0.0)

        def heard(index):
            return lambda: pl.semaphore_wait(late_ready.at[index], 1)

        pl.loop(0, levels // 2)(interior)
        when(top, heard(4), *[copy.start for copy in southward])
        pl.loop(levels // 2, levels)(interior)

        when(late_east, heard(3), eastward.start)
        when(late_west, heard(2), westward.start)
        when(mirror_late, heard(0), *[copy.start for copy in folded])
        when(next_late, heard(1), folded_next.start)

        hop = levels // 2
        low = row < 4

        @pl.when(jnp.logical_not(has_south))
        def _():
            hs[lo] = jnp.zeros((2, 128), I32)

            @pl.loop(0, levels)
            def _(k):
                h[0, k, lo] = jnp.zeros((2, 128), F32)
                h[1, k, lo] = jnp.zeros((2, 128), F32)
                hv[k, lo] = jnp.zeros((2, 128), F32)

        when(has_south, *[copy.wait_recv for copy in northward])
        cells = jnp.where(row < 2, n[pl.ds(PAD, 8)], 0)

        def put(i, k, change):
            outs[i][k, pl.ds(0, 8)] = outs[i][k, pl.ds(0, 8)] + jnp.where(k < cells, change, 0.0)

        edge_rows(
            False, q, v, n,
            lambda i, m: jnp.where(low, h[i, m], rows_by(h[i, m + hop], 4)),
            lambda m: jnp.where(low, hv[m], rows_by(hv[m + hop], 4)),
            jnp.where(low, hs[...], rows_by(hs[...], 4)),
            levels, rows, put,
        )

        def north_rows():
            when(has_north, *[copy.wait_recv for copy in southward])
            when(top, *[copy.wait_recv for copy in folded])
            when(top_far, folded_next.wait_recv)
            when(top_self, own_next.wait)

            @pl.when(has_north)
            def _():
                hn[...] = jnp.where(low, rows_by(hs_north[...], -4), hs_north[...])
                for m in range(hop):
                    for i in range(2):
                        hp[i, m] = jnp.where(low, rows_by(h_north[i, m], -4), h_north[i, m + hop])

            @pl.when(top)
            def _():
                order = lax.rem(128 - lane, 128)
                spot = SLOT * (groups - 1) + MID

                def mirrored(x):
                    x = jnp.where(row % 2 == 0, rows_by(x, -1), rows_by(x, 1))
                    return jnp.take_along_axis(x, order, axis=1)

                x = jnp.where(lane == 0, lanes(fb[0], -(spot - 2)), fan[...].astype(F32))
                hn[...] = mirrored(jnp.where(low, rows_by(x, -4), x)).astype(I32)
                for m in range(packs):
                    next_cells = jnp.where(low, rows_by(fb[m], -4), lanes(fb[m], -span * (hop // packs)))
                    for part in range(hop // packs):
                        k = packs * part + m
                        for i in range(2):
                            x = jnp.where(low, rows_by(fa[i, k], -4), fa[i, k + hop])
                            x = jnp.where(lane == 0, lanes(next_cells, -(span * part + spot + 2 * i)), x)
                            hp[i, k] = mirrored(x)

        when(late_west, north_rows)

        eastward.wait_recv()
        westward.wait_recv()

        def joined(own, before, after):
            left = jnp.where(sl < MID, before, own)
            right = own if after is None else jnp.where(sl < MID, own, after)
            a = jnp.where(sl < 4, lanes(left, -1), lanes(right, 4))
            b = jnp.where(sl < 4, lanes(left, -2), lanes(right, 3))
            return a, b

        na, nb = joined(px[2 * packs], lanes(from_w[0], -5), lanes(from_e[0], 2))
        face_n = jnp.minimum(na, nb)
        level_of = packs * (lane // span)
        pairs = [
            [joined(px[m], from_w[m], from_e[m]) for m in range(packs)],
            [joined(px[packs + m], lanes(from_w[m], -2), lanes(from_e[m], -2)) for m in range(packs)],
        ]
        rho_pairs = []
        for m in range(packs):
            z = depth((level_of + m).astype(F32))
            rho_pairs.append([density(pairs[0][m][j], pairs[1][m][j], z) for j in range(2)])
        sums = [[a + b for a, b in one] for one in (*pairs, rho_pairs)]

        def zsum_of(one, m):
            if m < packs - 1:
                above = one[m + 1]
            else:
                above = jnp.where(lane < 128 - span, lanes(one[0], -span), one[m])
            if m > 0:
                below = one[m - 1]
            else:
                below = jnp.where(lane < span, one[0], lanes(one[packs - 1], span))
            return above - below

        used = jnp.logical_or(jnp.logical_or(sl == 1, sl == 2), jnp.logical_or(sl == 5, sl == 6))
        for m in range(packs):
            level = level_of + m
            half_scale = jnp.where(jnp.logical_or(level == 0, level == levels - 1), 0.5, 0.25)
            wet = level.astype(F32) < face_n
            keep = jnp.logical_and(wet, used)
            c = joined(px[2 * packs + 1 + m], lanes(from_w[m], -3), None)[0]
            up, coef = courant_terms(c)
            sk = slope_term(rho_pairs[m][1] - rho_pairs[m][0], zsum_of(sums[2], m), half_scale)
            for i in range(2):
                qa, qb = pairs[i][m]
                d = jnp.where(wet, qb - qa, 0.0)
                f = tracer_flux(keep, c, up, coef, sk, qa, qb, d, lanes(d, 1), lanes(d, -1), zsum_of(sums[i], m))
                change = f - lanes(f, -1)
                change = jnp.where(sl < MID, lanes(change, -3), lanes(change, 2))
                ex[i, m] = jnp.where(level.astype(F32) < px[2 * packs], change, 0.0)

        ends_x = jnp.logical_or(lane < 2, lane > 125)

        for m in range(packs):
            for i in range(2):
                packed = ex[i, m]
                for slot in range(16):
                    k = packs * (slot // groups) + m
                    at = pl.ds(8 * (slot % groups), 8)
                    outs[i][k, at] = outs[i][k, at] + jnp.where(ends_x, lanes(packed, -(SLOT * slot + MID)), 0.0)

        when(jnp.logical_not(late_west), north_rows)

        eastward.wait_send()
        westward.wait_send()

        @pl.when(has_south)
        def _():
            for copy in southward:
                copy.wait_send()

        @pl.when(has_north)
        def _():
            for copy in northward:
                copy.wait_send()

        @pl.when(top)
        def _():
            for copy in folded:
                copy.wait_send()

        @pl.when(top_far)
        def _():
            folded_next.wait_send()

    return kernel


def make_edge_kernel(levels, rows):
    top_row = PAD + rows

    def kernel(t_part, s_part, q, v, n, hp, hn, t_out, s_out, done, sem, end_sem):
        parts = (t_part, s_part)
        outs = (t_out, s_out)
        row = lax.broadcasted_iota(I32, (8, 128), 0)
        rest, end = pl.ds(0, rows - 8), pl.ds(rows - 8, 8)
        stores = [pltpu.make_async_copy(parts[i].at[:, rest], outs[i].at[:, rest], sem.at[i]) for i in range(2)]
        for store in stores:
            store.start()

        cells = jnp.where(row > 5, n[pl.ds(top_row - 8, 8)], 0)

        def put(i, k, change):
            done[i, k] = parts[i][k, end] + jnp.where(k < cells, change, 0.0)

        edge_rows(True, q, v, n, lambda i, m: hp[i, m], None, hn[...], levels, rows, put)

        ends = [pltpu.make_async_copy(done.at[i], outs[i].at[:, end], end_sem.at[i]) for i in range(2)]
        for store in ends:
            store.start()
        for store in stores + ends:
            store.wait()

    return kernel


def solution(mesh):
    nlon, nlat = mesh.shape["lon"], mesh.shape["lat"]

    def body(t, s, u, v, n):
        levels, rows, cols = t.shape
        packs = levels // (16 // (rows // 8))
        tall = rows + 2 * PAD
        plain = jax.ShapeDtypeStruct((levels, rows, cols), F32)
        parts = pl.pallas_call(
            make_kernel(nlon, nlat, levels, rows),
            out_shape=(
                pltpu.VMEM((levels, rows, cols), F32),
                pltpu.VMEM((levels, rows, cols), F32),
                pltpu.VMEM((2, levels, tall, cols), F32),
                pltpu.VMEM((levels, tall, cols), F32),
                pltpu.VMEM((tall, cols), I32),
                pltpu.VMEM((2, levels // 2, 8, cols), F32),
                pltpu.VMEM((8, cols), I32),
            ),
            in_specs=[pl.BlockSpec(memory_space=pl.ANY)] * 5,
            out_specs=(pl.BlockSpec(memory_space=pltpu.VMEM),) * 7,
            scratch_shapes=[
                pltpu.VMEM((2, levels, 8, cols), F32),
                pltpu.VMEM((levels, 8, cols), F32),
                pltpu.VMEM((8, cols), I32),
                pltpu.VMEM((2, levels, 8, cols), F32),
                pltpu.VMEM((8, cols), I32),
                pltpu.VMEM((levels, tall, cols), F32),
                pltpu.VMEM((levels, rows, cols), F32),
                pltpu.VMEM((rows, cols), I32),
                pltpu.VMEM((rows, cols), I32),
                pltpu.VMEM((tall, cols), I32),
                pltpu.VMEM((rows, cols), I32),
                pltpu.VMEM((2, rows + 8, cols), F32),
                pltpu.VMEM((3 * packs + 1, 8, cols), F32),
                pltpu.VMEM((packs, 8, cols), F32),
                pltpu.VMEM((packs, 8, cols), F32),
                pltpu.VMEM((packs, 8, cols), F32),
                pltpu.VMEM((packs, 8, cols), F32),
                pltpu.VMEM((2, levels, 8, cols), F32),
                pltpu.VMEM((packs, 8, cols), F32),
                pltpu.VMEM((8, cols), I32),
                pltpu.VMEM((2, packs, 8, cols), F32),
                pltpu.SemaphoreType.DMA((6,)),
                pltpu.SemaphoreType.DMA((13,)),
                pltpu.SemaphoreType.DMA((13,)),
                pltpu.SemaphoreType.REGULAR((5,)),
            ],
            compiler_params=pltpu.CompilerParams(collective_id=0, has_side_effects=True),
            name="tracer_step",
        )(t, s, u, v, n)
        return pl.pallas_call(
            make_edge_kernel(levels, rows),
            out_shape=(plain, plain),
            in_specs=[pl.BlockSpec(memory_space=pltpu.VMEM)] * 7,
            out_specs=(pl.BlockSpec(memory_space=pl.ANY),) * 2,
            scratch_shapes=[
                pltpu.VMEM((2, levels, 8, cols), F32),
                pltpu.SemaphoreType.DMA((2,)),
                pltpu.SemaphoreType.DMA((2,)),
            ],
            name="edge_rows",
        )(*[pltpu.with_memory_space_constraint(part, pltpu.VMEM) for part in parts])

    spec = P(None, "lat", "lon")
    return jax.shard_map(
        body, mesh=mesh, in_specs=(spec,) * 4 + (P("lat", "lon"),), out_specs=(spec, spec), check_vma=False
    )
```

```python
import jax
import jax.numpy as jnp
from jax import lax
from jax.experimental import pallas as pl
from jax.experimental.pallas import tpu as pltpu
from jax.sharding import PartitionSpec as P

ALPHA = 0.1655
BETA = 0.76554
CABBELING = 0.05952
LAMBDA_SALT = 0.00054914
THERMOBARIC = 0.0001497
PRESS_SALT = 1.109e-05
CROSS = 0.0024341
TOTAL_DEPTH = 5000.0
KAPPA = 0.1
SLOPE_MAX = 1.0
STRAT_MIN = 0.1

MESH = pl.DeviceIdType.MESH
F32 = jnp.float32
I32 = jnp.int32

PAD = 8
SLOT = 8
MID = 3


def density(t, s, z):
    lead = -ALPHA - (ALPHA * THERMOBARIC) * z
    salt = BETA - (BETA * PRESS_SALT) * z
    return t * (lead + (-0.5 * ALPHA * CABBELING) * t - CROSS * s) + s * (salt - (0.5 * BETA * LAMBDA_SALT) * s)


def slope_term(rho_diff, rho_zsum, half_scale):
    strat = jnp.maximum(half_scale * rho_zsum, STRAT_MIN)
    slope = jnp.clip(-rho_diff / strat, -SLOPE_MAX, SLOPE_MAX)
    return slope * (KAPPA * half_scale)


def courant_terms(c):
    up = c > 0.0
    coef = jnp.where(up, 0.5, -0.5) - 0.5 * c
    return up, coef


def tracer_flux(face, c, up, coef, sk, qa, qb, d, back, ahead, zsum):
    step = jnp.where(up, back, ahead)
    limited = jnp.minimum(jnp.maximum(step, jnp.minimum(d, 0.0)), jnp.maximum(d, 0.0))
    adv = c * (jnp.where(up, qa, qb) + coef * limited)
    return jnp.where(face, adv - (KAPPA * d + sk * zsum), 0.0)


def lanes(x, shift):
    return pltpu.roll(x, shift % 128, axis=x.ndim - 1)


def rows_by(x, shift):
    return pltpu.roll(x, shift % 8, axis=x.ndim - 2)


def edge_rows(north, q, v, n, halo, halo_v, halo_n, levels, rows, emit):
    top_row = PAD + rows
    hop = levels // 2
    row = lax.broadcasted_iota(I32, (8, 128), 0)
    low, place = row < 4, row % 4

    def own(load, m, base):
        return jnp.where(low, load(m, base), load(m + hop, base - 4))

    def pair(halo, load, m):
        if north:
            a = jnp.where(place == 3, rows_by(halo, 1), own(load, m, top_row - 3))
            b = jnp.where(place > 1, halo, own(load, m, top_row - 2))
        else:
            a = jnp.where(place < 2, halo, own(load, m, PAD - 2))
            b = jnp.where(place < 1, rows_by(halo, -1), own(load, m, PAD - 1))
        return a, b

    def load_v(k, base):
        return v[k, pl.ds(base, 8)]

    face_n = jnp.minimum(*pair(halo_n, lambda k, base: n[pl.ds(base, 8)], 0))
    keep_n = jnp.where(jnp.logical_or(place == 1, place == 2), face_n, 0)

    def level(m):
        z = jnp.where(low, TOTAL_DEPTH * (m + 0.5) / levels, TOTAL_DEPTH * (m + hop + 0.5) / levels)
        t, s = [pair(halo(i, m), lambda k, base, i=i: q[i, k, pl.ds(base, 8)], m) for i in range(2)]
        ra, rb = [density(t[j], s[j], z) for j in range(2)]
        return (t, s), (t[0] + t[1], s[0] + s[1], ra + rb), rb - ra

    held = [level(m) for m in range(hop)]
    for m in range(hop):
        tracers, sums, rho_diff = held[m]
        zsums = []
        for j in range(3):
            above = held[m + 1][1][j] if m + 1 < hop else jnp.where(low, rows_by(held[0][1][j], 4), sums[j])
            below = held[m - 1][1][j] if m > 0 else jnp.where(low, sums[j], rows_by(held[hop - 1][1][j], 4))
            zsums.append(above - below)
        half_scale = 0.25
        if m == 0:
            half_scale = jnp.where(low, 0.5, 0.25)
        if m == hop - 1:
            half_scale = jnp.where(low, 0.25, 0.5)
        k = jnp.where(low, m, m + hop)
        wet, keep = k < face_n, k < keep_n
        c = own(load_v, m, top_row - 3) if north else jnp.where(place < 2, halo_v(m), own(load_v, m, PAD - 2))
        up, coef = courant_terms(c)
        sk = slope_term(rho_diff, zsums[2], half_scale)
        for i in range(2):
            qa, qb = tracers[i]
            d = jnp.where(wet, qb - qa, 0.0)
            f = tracer_flux(keep, c, up, coef, sk, qa, qb, d, rows_by(d, 1), rows_by(d, -1), zsums[i])
            change = f - rows_by(f, -1)
            emit(i, m, rows_by(change, 6 if north else -1))
            emit(i, m + hop, rows_by(change, 2 if north else 3))


def make_kernel(nlon, nlat, levels, rows):
    groups = rows // 8
    per = 16 // groups
    packs = levels // per
    span = SLOT * groups
    top_row = PAD + rows

    def depth(k):
        return TOTAL_DEPTH * (k + 0.5) / levels

    def kernel(
        t_hbm, s_hbm, u_hbm, v_hbm, n_hbm,
        t_out, s_out, q, v, n, hp, hn,
        h, hv, hs, h_north, hs_north, rho, u, face_x, keep_x, face_y, keep_y, fy,
        px, to_e, to_w, from_w, from_e, fa, fb, fan, ex,
        load_sem, send_sem, recv_sem, late_ready,
    ):
        lon = lax.axis_index("lon")
        lat = lax.axis_index("lat")
        east = lax.rem(lon + 1, nlon)
        west = lax.rem(lon + nlon - 1, nlon)
        has_south = lat > 0
        has_north = lat < nlat - 1
        top = lat == nlat - 1
        mirror = nlon - 1 - lon
        mirror_next = lax.rem(nlon - lon, nlon)
        mirror_far = mirror_next != lon
        top_far = jnp.logical_and(top, mirror_far)
        top_self = jnp.logical_and(top, jnp.logical_not(mirror_far))
        below_top = lat == nlat - 2
        plain = jnp.logical_not(top)
        half, quarter = nlon // 2, nlon // 4
        place = lax.rem(lon, half)
        early = place < quarter
        late_west = place == 0
        late_east = place == quarter - 1
        early_west = place == quarter
        early_east = place == half - 1
        mirror_late = jnp.logical_and(top, early)
        mirror_early = jnp.logical_and(top, jnp.logical_not(early))
        next_late = jnp.logical_and(top_far, early)
        next_early = jnp.logical_and(top_far, place > quarter)
        next_same = jnp.logical_and(top_far, place == quarter)

        barrier = pltpu.get_barrier_semaphore()

        def greet(device):
            pl.semaphore_signal(barrier, inc=1, device_id=device, device_id_type=MESH)

        def when(condition, *steps):
            @pl.when(condition)
            def _():
                for step in steps:
                    step()

        def both(a, b):
            return jnp.logical_or(a, b)

        when(has_south, lambda: greet({"lat": lat - 1}))
        when(jnp.logical_and(has_north, jnp.logical_not(below_top)), lambda: greet({"lat": lat + 1}))
        when(mirror_late, lambda: greet({"lon": mirror}))
        when(both(next_late, next_same), lambda: greet({"lon": mirror_next}))
        when(jnp.logical_not(early_east), lambda: greet({"lon": east}))
        when(jnp.logical_not(early_west), lambda: greet({"lon": west}))

        body_rows = pl.ds(PAD, rows)
        loads = [
            pltpu.make_async_copy(n_hbm, n.at[body_rows], load_sem.at[0]),
            pltpu.make_async_copy(t_hbm, q.at[0, :, body_rows], load_sem.at[1]),
            pltpu.make_async_copy(s_hbm, q.at[1, :, body_rows], load_sem.at[2]),
            pltpu.make_async_copy(u_hbm, u, load_sem.at[3]),
            pltpu.make_async_copy(v_hbm, v.at[:, body_rows], load_sem.at[4]),
        ]
        for load in loads:
            load.start()

        lane = lax.broadcasted_iota(I32, (8, 128), 1)
        row = lax.broadcasted_iota(I32, (8, 128), 0)
        slot_of = lane // SLOT
        sl = lane % SLOT

        greetings = (
            jnp.logical_and(has_south, plain), has_north, mirror_early, both(next_early, next_same),
            jnp.logical_not(late_west), jnp.logical_not(late_east),
        )

        def meet():
            pl.semaphore_wait(barrier, sum(one.astype(I32) for one in greetings))

        def tell(index, device):
            return lambda: pl.semaphore_signal(
                late_ready.at[index], inc=1, device_id=device, device_id_type=MESH
            )

        def remote(src, dst, index, device):
            return pltpu.make_async_remote_copy(
                src_ref=src, dst_ref=dst, send_sem=send_sem.at[index], recv_sem=recv_sem.at[index],
                device_id=device, device_id_type=MESH,
            )

        first, last = pl.ds(0, 2), pl.ds(rows - 2, 2)
        fold = pl.ds(rows - 3, 2)
        fold_in_group = pl.ds(5, 2)
        lo, hi = pl.ds(0, 2), pl.ds(6, 2)
        northward = [
            remote(t_hbm.at[:, last], h.at[0, :, lo], 0, {"lat": lat + 1}),
            remote(s_hbm.at[:, last], h.at[1, :, lo], 1, {"lat": lat + 1}),
            remote(v_hbm.at[:, pl.ds(rows - 1, 1)], hv.at[:, pl.ds(1, 1)], 2, {"lat": lat + 1}),
            remote(n_hbm.at[last], hs.at[lo], 3, {"lat": lat + 1}),
        ]
        southward = [
            remote(t_hbm.at[:, first], h_north.at[0, :, hi], 4, {"lat": lat - 1}),
            remote(s_hbm.at[:, first], h_north.at[1, :, hi], 5, {"lat": lat - 1}),
            remote(n_hbm.at[first], hs_north.at[hi], 6, {"lat": lat - 1}),
        ]
        folded = [
            remote(t_hbm.at[:, fold], fa.at[0, :, hi], 7, {"lon": mirror}),
            remote(s_hbm.at[:, fold], fa.at[1, :, hi], 8, {"lon": mirror}),
            remote(n_hbm.at[fold], fan.at[hi], 9, {"lon": mirror}),
        ]
        folded_next = remote(to_w.at[:, fold_in_group], fb.at[:, hi], 10, {"lon": mirror_next})
        own_next = pltpu.make_async_copy(to_w.at[:, fold_in_group], fb.at[:, hi], load_sem.at[5])
        eastward = remote(to_e, from_w, 11, {"lon": east})
        westward = remote(to_w, from_e, 12, {"lon": west})

        @pl.when(top)
        def _():
            meet()
            when(mirror_early, *[copy.start for copy in folded], tell(0, {"lon": mirror}))
            when(next_early, tell(1, {"lon": mirror_next}))
            when(early_east, tell(2, {"lon": east}))
            when(early_west, tell(3, {"lon": west}))

        for load in loads[:4]:
            load.wait()
        packed_n = jnp.zeros((8, 128), F32)
        for slot in range(16):
            part = n[pl.ds(PAD + 8 * (slot % groups), 8)].astype(F32)
            packed_n = jnp.where(slot_of == slot, lanes(part, SLOT * slot + MID), packed_n)
        px[2 * packs] = packed_n
        n_up, n_down = lanes(packed_n, 5), lanes(packed_n, -2)

        @pl.loop(0, packs)
        def _(m):
            packed = []
            for field in range(3):
                one = jnp.zeros((8, 128), F32)
                for slot in range(16):
                    k = packs * (slot // groups) + m
                    g = slot % groups
                    if field < 2:
                        part = q[field, k, pl.ds(PAD + 8 * g, 8)]
                    else:
                        part = u[k, pl.ds(8 * g, 8)]
                    one = jnp.where(slot_of == slot, lanes(part, SLOT * slot + MID), one)
                px[(0, packs, 2 * packs + 1)[field] + m] = one
                packed.append(one)
            t2, s2, u2 = packed
            s_up = lanes(s2, 2)
            to_e[m] = jnp.where(sl < 3, t2, jnp.where(sl < 5, s_up, jnp.where(sl < 6, lanes(u2, 3), n_up)))
            to_w[m] = jnp.where(sl < 3, n_down, jnp.where(sl < 5, t2, s_up))

        when(top_self, own_next.start)
        def send_columns():
            when(jnp.logical_not(late_east), eastward.start)
            when(jnp.logical_not(late_west), westward.start)

        @pl.when(top)
        def _():
            when(both(next_early, next_same), folded_next.start)
            send_columns()

        @pl.when(plain)
        def _():
            meet()
            send_columns()
            when(early_east, tell(2, {"lon": east}))
            when(early_west, tell(3, {"lon": west}))
            when(below_top, tell(4, {"lat": lat + 1}))
            when(has_south, *[copy.start for copy in southward])
            when(has_north, *[copy.start for copy in northward])

        @pl.loop(0, levels)
        def _(k):
            z = depth(k.astype(F32))
            for g in range(groups):
                at = pl.ds(PAD + 8 * g, 8)
                rho[k, at] = density(q[0, k, at], q[1, k, at], z)

        pad_n = jnp.zeros((8, 128), I32)
        n[pl.ds(0, 8)] = pad_n
        n[pl.ds(top_row, 8)] = pad_n
        for g in range(groups):
            at = pl.ds(PAD + 8 * g, 8)
            here = n[at]
            fx = jnp.minimum(here, lanes(here, 1))
            face_x[pl.ds(8 * g, 8)] = fx
            inner = jnp.logical_and(lane > 1, lane < 127)
            keep_x[pl.ds(8 * g, 8)] = jnp.where(inner, fx, 0)
            f = jnp.minimum(here, n[pl.ds(PAD + 8 * g - 1, 8)])
            face_y[at] = f
            if g == 0:
                f = jnp.where(row > 1, f, 0)
            if g == groups - 1:
                f = jnp.where(row < 7, f, 0)
            keep_y[pl.ds(8 * g, 8)] = f
        face_y[pl.ds(0, 8)] = pad_n
        face_y[pl.ds(top_row, 8)] = pad_n

        outs = (t_out, s_out)
        loads[4].wait()
        fy[0, pl.ds(rows, 8)] = jnp.zeros((8, 128), F32)
        fy[1, pl.ds(rows, 8)] = jnp.zeros((8, 128), F32)

        def interior(k):
            kp = jnp.minimum(k + 1, levels - 1)
            km = jnp.maximum(k - 1, 0)
            ends = jnp.logical_or(k == 0, k == levels - 1)
            half_scale = jnp.where(ends, 0.5, 0.25).astype(F32)

            for g in reversed(range(groups)):
                r = PAD + 8 * g
                at, dn = pl.ds(r, 8), pl.ds(r - 1, 8)
                t0 = [q[i, k, at] for i in range(2)]
                zd = [q[i, kp, at] - q[i, km, at] for i in range(2)]
                rho0 = rho[k, at]
                rz = rho[kp, at] - rho[km, at]

                wet = k < face_x[pl.ds(8 * g, 8)]
                keep = k < keep_x[pl.ds(8 * g, 8)]
                c = lanes(u[k, pl.ds(8 * g, 8)], 1)
                up, coef = courant_terms(c)
                sk = slope_term(rho0 - lanes(rho0, 1), rz + lanes(rz, 1), half_scale)
                total = []
                for i in range(2):
                    qa = lanes(t0[i], 1)
                    d = jnp.where(wet, t0[i] - qa, 0.0)
                    f = tracer_flux(keep, c, up, coef, sk, qa, t0[i], d, lanes(d, 1), lanes(d, -1), zd[i] + lanes(zd[i], 1))
                    total.append(t0[i] + (f - lanes(f, -1)))

                wet = k < face_y[at]
                wet_back = k < face_y[dn]
                wet_ahead = k < face_y[pl.ds(r + 1, 8)]
                keep = k < keep_y[pl.ds(8 * g, 8)]
                c = v[k, dn]
                up, coef = courant_terms(c)
                sk = slope_term(rho0 - rho[k, dn], rz + (rho[kp, dn] - rho[km, dn]), half_scale)
                here = k < n[at]
                for i in range(2):
                    qa = q[i, k, dn]
                    d = jnp.where(wet, t0[i] - qa, 0.0)
                    back = jnp.where(wet_back, qa - q[i, k, pl.ds(r - 2, 8)], 0.0)
                    ahead = jnp.where(wet_ahead, q[i, k, pl.ds(r + 1, 8)] - t0[i], 0.0)
                    zsum = zd[i] + (q[i, kp, dn] - q[i, km, dn])
                    f = tracer_flux(keep, c, up, coef, sk, qa, t0[i], d, back, ahead, zsum)
                    fy[i, pl.ds(8 * g, 8)] = f
                    f_north = fy[i, pl.ds(8 * g + 1, 8)]
                    outs[i][k, pl.ds(8 * g, 8)] = jnp.where(here, total[i] + (f - f_north), 0.0)

        def heard(index):
            return lambda: pl.semaphore_wait(late_ready.at[index], 1)

        pl.loop(0, levels // 2)(interior)
        when(top, heard(4), *[copy.start for copy in southward])
        pl.loop(levels // 2, levels)(interior)

        when(late_east, heard(3), eastward.start)
        when(late_west, heard(2), westward.start)
        when(mirror_late, heard(0), *[copy.start for copy in folded])
        when(next_late, heard(1), folded_next.start)

        hop = levels // 2
        low = row < 4

        @pl.when(jnp.logical_not(has_south))
        def _():
            hs[lo] = jnp.zeros((2, 128), I32)

            @pl.loop(0, levels)
            def _(k):
                h[0, k, lo] = jnp.zeros((2, 128), F32)
                h[1, k, lo] = jnp.zeros((2, 128), F32)
                hv[k, lo] = jnp.zeros((2, 128), F32)

        when(has_south, *[copy.wait_recv for copy in northward])
        cells = jnp.where(row < 2, n[pl.ds(PAD, 8)], 0)

        def put(i, k, change):
            outs[i][k, pl.ds(0, 8)] = outs[i][k, pl.ds(0, 8)] + jnp.where(k < cells, change, 0.0)

        edge_rows(
            False, q, v, n,
            lambda i, m: jnp.where(low, h[i, m], rows_by(h[i, m + hop], 4)),
            lambda m: jnp.where(low, hv[m], rows_by(hv[m + hop], 4)),
            jnp.where(low, hs[...], rows_by(hs[...], 4)),
            levels, rows, put,
        )

        def north_rows():
            when(has_north, *[copy.wait_recv for copy in southward])
            when(top, *[copy.wait_recv for copy in folded])
            when(top_far, folded_next.wait_recv)
            when(top_self, own_next.wait)

            @pl.when(has_north)
            def _():
                hn[...] = jnp.where(low, rows_by(hs_north[...], -4), hs_north[...])
                for m in range(hop):
                    for i in range(2):
                        hp[i, m] = jnp.where(low, rows_by(h_north[i, m], -4), h_north[i, m + hop])

            @pl.when(top)
            def _():
                order = lax.rem(128 - lane, 128)
                spot = SLOT * (groups - 1) + MID

                def mirrored(x):
                    x = jnp.where(row % 2 == 0, rows_by(x, -1), rows_by(x, 1))
                    return jnp.take_along_axis(x, order, axis=1)

                x = jnp.where(lane == 0, lanes(fb[0], -(spot - 2)), fan[...].astype(F32))
                hn[...] = mirrored(jnp.where(low, rows_by(x, -4), x)).astype(I32)
                for m in range(packs):
                    next_cells = jnp.where(low, rows_by(fb[m], -4), lanes(fb[m], -span * (hop // packs)))
                    for part in range(hop // packs):
                        k = packs * part + m
                        for i in range(2):
                            x = jnp.where(low, rows_by(fa[i, k], -4), fa[i, k + hop])
                            x = jnp.where(lane == 0, lanes(next_cells, -(span * part + spot + 2 * i)), x)
                            hp[i, k] = mirrored(x)

        when(late_west, north_rows)

        eastward.wait_recv()
        westward.wait_recv()

        def joined(own, before, after, by_west, by_east):
            a_west = jnp.where(sl < 2, lanes(before, by_west - 1), lanes(own, -1))
            a_east = jnp.where(sl < 7, lanes(own, 4), lanes(after, by_east + 4))
            b_west = jnp.where(sl < 1, lanes(before, by_west - 2), lanes(own, -2))
            b_east = jnp.where(sl < 6, lanes(own, 3), lanes(after, by_east + 3))
            return jnp.where(sl < 4, a_west, a_east), jnp.where(sl < 4, b_west, b_east)

        na, nb = joined(px[2 * packs], from_w[0], from_e[0], -5, 2)
        face_n = jnp.minimum(na, nb)
        level_of = packs * (lane // span)
        pairs = [
            [joined(px[m], from_w[m], from_e[m], 0, 0) for m in range(packs)],
            [joined(px[packs + m], from_w[m], from_e[m], -2, -2) for m in range(packs)],
        ]
        rho_pairs = []
        for m in range(packs):
            z = depth((level_of + m).astype(F32))
            rho_pairs.append([density(pairs[0][m][j], pairs[1][m][j], z) for j in range(2)])
        sums = [[a + b for a, b in one] for one in (*pairs, rho_pairs)]

        def zsum_of(one, m):
            if m < packs - 1:
                above = one[m + 1]
            else:
                above = jnp.where(lane < 128 - span, lanes(one[0], -span), one[m])
            if m > 0:
                below = one[m - 1]
            else:
                below = jnp.where(lane < span, one[0], lanes(one[packs - 1], span))
            return above - below

        used = jnp.logical_or(jnp.logical_or(sl == 1, sl == 2), jnp.logical_or(sl == 5, sl == 6))
        for m in range(packs):
            level = level_of + m
            half_scale = jnp.where(jnp.logical_or(level == 0, level == levels - 1), 0.5, 0.25)
            wet = level.astype(F32) < face_n
            keep = jnp.logical_and(wet, used)
            u2 = px[2 * packs + 1 + m]
            c = jnp.where(sl < 4, jnp.where(sl < 2, lanes(from_w[m], -4), lanes(u2, -1)), lanes(u2, 4))
            up, coef = courant_terms(c)
            sk = slope_term(rho_pairs[m][1] - rho_pairs[m][0], zsum_of(sums[2], m), half_scale)
            for i in range(2):
                qa, qb = pairs[i][m]
                d = jnp.where(wet, qb - qa, 0.0)
                f = tracer_flux(keep, c, up, coef, sk, qa, qb, d, lanes(d, 1), lanes(d, -1), zsum_of(sums[i], m))
                change = jnp.where(sl < MID, lanes(f, -3) - lanes(f, -4), lanes(f, 2) - lanes(f, 1))
                ex[i, m] = jnp.where(level.astype(F32) < px[2 * packs], change, 0.0)

        ends_x = jnp.logical_or(lane < 2, lane > 125)

        packed = [[ex[i, m] for m in range(packs)] for i in range(2)]
        for slot in range(16):
            for m in range(packs):
                for i in range(2):
                    k = packs * (slot // groups) + m
                    at = pl.ds(8 * (slot % groups), 8)
                    change = jnp.where(ends_x, lanes(packed[i][m], -(SLOT * slot + MID)), 0.0)
                    outs[i][k, at] = outs[i][k, at] + change

        when(jnp.logical_not(late_west), north_rows)

        eastward.wait_send()
        westward.wait_send()

        @pl.when(has_south)
        def _():
            for copy in southward:
                copy.wait_send()

        @pl.when(has_north)
        def _():
            for copy in northward:
                copy.wait_send()

        @pl.when(top)
        def _():
            for copy in folded:
                copy.wait_send()

        @pl.when(top_far)
        def _():
            folded_next.wait_send()

    return kernel


def make_edge_kernel(levels, rows):
    top_row = PAD + rows

    def kernel(t_part, s_part, q, v, n, hp, hn, t_out, s_out, done, sem, end_sem):
        parts = (t_part, s_part)
        outs = (t_out, s_out)
        row = lax.broadcasted_iota(I32, (8, 128), 0)
        rest, end = pl.ds(0, rows - 8), pl.ds(rows - 8, 8)
        stores = [pltpu.make_async_copy(parts[i].at[:, rest], outs[i].at[:, rest], sem.at[i]) for i in range(2)]
        for store in stores:
            store.start()

        cells = jnp.where(row > 5, n[pl.ds(top_row - 8, 8)], 0)

        def put(i, k, change):
            done[i, k] = parts[i][k, end] + jnp.where(k < cells, change, 0.0)

        edge_rows(True, q, v, n, lambda i, m: hp[i, m], None, hn[...], levels, rows, put)

        ends = [pltpu.make_async_copy(done.at[i], outs[i].at[:, end], end_sem.at[i]) for i in range(2)]
        for store in ends:
            store.start()
        for store in stores + ends:
            store.wait()

    return kernel


def solution(mesh):
    nlon, nlat = mesh.shape["lon"], mesh.shape["lat"]

    def body(t, s, u, v, n):
        levels, rows, cols = t.shape
        packs = levels // (16 // (rows // 8))
        tall = rows + 2 * PAD
        plain = jax.ShapeDtypeStruct((levels, rows, cols), F32)
        parts = pl.pallas_call(
            make_kernel(nlon, nlat, levels, rows),
            out_shape=(
                pltpu.VMEM((levels, rows, cols), F32),
                pltpu.VMEM((levels, rows, cols), F32),
                pltpu.VMEM((2, levels, tall, cols), F32),
                pltpu.VMEM((levels, tall, cols), F32),
                pltpu.VMEM((tall, cols), I32),
                pltpu.VMEM((2, levels // 2, 8, cols), F32),
                pltpu.VMEM((8, cols), I32),
            ),
            in_specs=[pl.BlockSpec(memory_space=pl.ANY)] * 5,
            out_specs=(pl.BlockSpec(memory_space=pltpu.VMEM),) * 7,
            scratch_shapes=[
                pltpu.VMEM((2, levels, 8, cols), F32),
                pltpu.VMEM((levels, 8, cols), F32),
                pltpu.VMEM((8, cols), I32),
                pltpu.VMEM((2, levels, 8, cols), F32),
                pltpu.VMEM((8, cols), I32),
                pltpu.VMEM((levels, tall, cols), F32),
                pltpu.VMEM((levels, rows, cols), F32),
                pltpu.VMEM((rows, cols), I32),
                pltpu.VMEM((rows, cols), I32),
                pltpu.VMEM((tall, cols), I32),
                pltpu.VMEM((rows, cols), I32),
                pltpu.VMEM((2, rows + 8, cols), F32),
                pltpu.VMEM((3 * packs + 1, 8, cols), F32),
                pltpu.VMEM((packs, 8, cols), F32),
                pltpu.VMEM((packs, 8, cols), F32),
                pltpu.VMEM((packs, 8, cols), F32),
                pltpu.VMEM((packs, 8, cols), F32),
                pltpu.VMEM((2, levels, 8, cols), F32),
                pltpu.VMEM((packs, 8, cols), F32),
                pltpu.VMEM((8, cols), I32),
                pltpu.VMEM((2, packs, 8, cols), F32),
                pltpu.SemaphoreType.DMA((6,)),
                pltpu.SemaphoreType.DMA((13,)),
                pltpu.SemaphoreType.DMA((13,)),
                pltpu.SemaphoreType.REGULAR((5,)),
            ],
            compiler_params=pltpu.CompilerParams(collective_id=0, has_side_effects=True),
            name="tracer_step",
        )(t, s, u, v, n)
        return pl.pallas_call(
            make_edge_kernel(levels, rows),
            out_shape=(plain, plain),
            in_specs=[pl.BlockSpec(memory_space=pltpu.VMEM)] * 7,
            out_specs=(pl.BlockSpec(memory_space=pl.ANY),) * 2,
            scratch_shapes=[
                pltpu.VMEM((2, levels, 8, cols), F32),
                pltpu.SemaphoreType.DMA((2,)),
                pltpu.SemaphoreType.DMA((2,)),
            ],
            name="edge_rows",
        )(*[pltpu.with_memory_space_constraint(part, pltpu.VMEM) for part in parts])

    spec = P(None, "lat", "lon")
    return jax.shard_map(
        body, mesh=mesh, in_specs=(spec,) * 4 + (P("lat", "lon"),), out_specs=(spec, spec), check_vma=False
    )
```

```python
import jax
import jax.numpy as jnp
from jax import lax
from jax.experimental import pallas as pl
from jax.experimental.pallas import tpu as pltpu
from jax.sharding import PartitionSpec as P

ALPHA = 0.1655
BETA = 0.76554
CABBELING = 0.05952
LAMBDA_SALT = 0.00054914
THERMOBARIC = 0.0001497
PRESS_SALT = 1.109e-05
CROSS = 0.0024341
TOTAL_DEPTH = 5000.0
KAPPA = 0.1
SLOPE_MAX = 1.0
STRAT_MIN = 0.1

MESH = pl.DeviceIdType.MESH
F32 = jnp.float32
I32 = jnp.int32

PAD = 8
SLOT = 8
MID = 3


def density(t, s, z):
    lead = -ALPHA - (ALPHA * THERMOBARIC) * z
    salt = BETA - (BETA * PRESS_SALT) * z
    return t * (lead + (-0.5 * ALPHA * CABBELING) * t - CROSS * s) + s * (salt - (0.5 * BETA * LAMBDA_SALT) * s)


def slope_term(rho_diff, rho_zsum, half_scale):
    strat = jnp.maximum(half_scale * rho_zsum, STRAT_MIN)
    slope = jnp.clip(-rho_diff / strat, -SLOPE_MAX, SLOPE_MAX)
    return slope * (KAPPA * half_scale)


def courant_terms(c):
    up = c > 0.0
    coef = jnp.where(up, 0.5, -0.5) - 0.5 * c
    return up, coef


def tracer_flux(face, c, up, coef, sk, qa, qb, d, back, ahead, zsum):
    step = jnp.where(up, back, ahead)
    limited = jnp.minimum(jnp.maximum(step, jnp.minimum(d, 0.0)), jnp.maximum(d, 0.0))
    adv = c * (jnp.where(up, qa, qb) + coef * limited)
    return jnp.where(face, adv - (KAPPA * d + sk * zsum), 0.0)


def lanes(x, shift):
    return pltpu.roll(x, shift % 128, axis=x.ndim - 1)


def rows_by(x, shift):
    return pltpu.roll(x, shift % 8, axis=x.ndim - 2)


def edge_rows(north, q, v, n, halo, halo_v, halo_n, levels, rows, emit):
    top_row = PAD + rows
    hop = levels // 2
    row = lax.broadcasted_iota(I32, (8, 128), 0)
    low, place = row < 4, row % 4

    def own(load, m, base):
        return jnp.where(low, load(m, base), load(m + hop, base - 4))

    def pair(halo, load, m):
        if north:
            a = jnp.where(place == 3, rows_by(halo, 1), own(load, m, top_row - 3))
            b = jnp.where(place > 1, halo, own(load, m, top_row - 2))
        else:
            a = jnp.where(place < 2, halo, own(load, m, PAD - 2))
            b = jnp.where(place < 1, rows_by(halo, -1), own(load, m, PAD - 1))
        return a, b

    def load_v(k, base):
        return v[k, pl.ds(base, 8)]

    face_n = jnp.minimum(*pair(halo_n, lambda k, base: n[pl.ds(base, 8)], 0))
    keep_n = jnp.where(jnp.logical_or(place == 1, place == 2), face_n, 0)

    def level(m):
        z = jnp.where(low, TOTAL_DEPTH * (m + 0.5) / levels, TOTAL_DEPTH * (m + hop + 0.5) / levels)
        t, s = [pair(halo(i, m), lambda k, base, i=i: q[i, k, pl.ds(base, 8)], m) for i in range(2)]
        ra, rb = [density(t[j], s[j], z) for j in range(2)]
        return (t, s), (t[0] + t[1], s[0] + s[1], ra + rb), rb - ra

    held = [level(m) for m in range(hop)]
    for m in range(hop):
        tracers, sums, rho_diff = held[m]
        zsums = []
        for j in range(3):
            above = held[m + 1][1][j] if m + 1 < hop else jnp.where(low, rows_by(held[0][1][j], 4), sums[j])
            below = held[m - 1][1][j] if m > 0 else jnp.where(low, sums[j], rows_by(held[hop - 1][1][j], 4))
            zsums.append(above - below)
        half_scale = 0.25
        if m == 0:
            half_scale = jnp.where(low, 0.5, 0.25)
        if m == hop - 1:
            half_scale = jnp.where(low, 0.25, 0.5)
        k = jnp.where(low, m, m + hop)
        wet, keep = k < face_n, k < keep_n
        c = own(load_v, m, top_row - 3) if north else jnp.where(place < 2, halo_v(m), own(load_v, m, PAD - 2))
        up, coef = courant_terms(c)
        sk = slope_term(rho_diff, zsums[2], half_scale)
        for i in range(2):
            qa, qb = tracers[i]
            d = jnp.where(wet, qb - qa, 0.0)
            f = tracer_flux(keep, c, up, coef, sk, qa, qb, d, rows_by(d, 1), rows_by(d, -1), zsums[i])
            change = f - rows_by(f, -1)
            emit(i, m, rows_by(change, 6 if north else -1))
            emit(i, m + hop, rows_by(change, 2 if north else 3))


def make_kernel(nlon, nlat, levels, rows):
    groups = rows // 8
    per = 16 // groups
    packs = levels // per
    span = SLOT * groups
    top_row = PAD + rows

    def depth(k):
        return TOTAL_DEPTH * (k + 0.5) / levels

    def kernel(
        t_hbm, s_hbm, u_hbm, v_hbm, n_hbm,
        t_out, s_out, q, v, n, hp, hn,
        h, hv, hs, h_north, hs_north, rho, u, face_x, keep_x, face_y, keep_y, fy,
        px, to_e, to_w, from_w, from_e, fa, fb, fan, ex,
        load_sem, send_sem, recv_sem, late_ready,
    ):
        lon = lax.axis_index("lon")
        lat = lax.axis_index("lat")
        east = lax.rem(lon + 1, nlon)
        west = lax.rem(lon + nlon - 1, nlon)
        has_south = lat > 0
        has_north = lat < nlat - 1
        top = lat == nlat - 1
        mirror = nlon - 1 - lon
        mirror_next = lax.rem(nlon - lon, nlon)
        mirror_far = mirror_next != lon
        top_far = jnp.logical_and(top, mirror_far)
        top_self = jnp.logical_and(top, jnp.logical_not(mirror_far))
        below_top = lat == nlat - 2
        plain = jnp.logical_not(top)
        half, quarter = nlon // 2, nlon // 4
        place = lax.rem(lon, half)
        early = place < quarter
        late_west = place == 0
        late_east = place == quarter - 1
        early_west = place == quarter
        early_east = place == half - 1
        mirror_late = jnp.logical_and(top, early)
        mirror_early = jnp.logical_and(top, jnp.logical_not(early))
        next_late = jnp.logical_and(top_far, early)
        next_early = jnp.logical_and(top_far, place > quarter)
        next_same = jnp.logical_and(top_far, place == quarter)

        barrier = pltpu.get_barrier_semaphore()

        def greet(device):
            pl.semaphore_signal(barrier, inc=1, device_id=device, device_id_type=MESH)

        def when(condition, *steps):
            @pl.when(condition)
            def _():
                for step in steps:
                    step()

        def both(a, b):
            return jnp.logical_or(a, b)

        when(has_south, lambda: greet({"lat": lat - 1}))
        when(jnp.logical_and(has_north, jnp.logical_not(below_top)), lambda: greet({"lat": lat + 1}))
        when(mirror_late, lambda: greet({"lon": mirror}))
        when(both(next_late, next_same), lambda: greet({"lon": mirror_next}))
        when(jnp.logical_not(early_east), lambda: greet({"lon": east}))
        when(jnp.logical_not(early_west), lambda: greet({"lon": west}))

        body_rows = pl.ds(PAD, rows)
        loads = [
            pltpu.make_async_copy(n_hbm, n.at[body_rows], load_sem.at[0]),
            pltpu.make_async_copy(t_hbm, q.at[0, :, body_rows], load_sem.at[1]),
            pltpu.make_async_copy(s_hbm, q.at[1, :, body_rows], load_sem.at[2]),
            pltpu.make_async_copy(u_hbm, u, load_sem.at[3]),
            pltpu.make_async_copy(v_hbm, v.at[:, body_rows], load_sem.at[4]),
        ]
        for load in loads:
            load.start()

        lane = lax.broadcasted_iota(I32, (8, 128), 1)
        row = lax.broadcasted_iota(I32, (8, 128), 0)
        slot_of = lane // SLOT
        sl = lane % SLOT

        greetings = (
            jnp.logical_and(has_south, plain), has_north, mirror_early, both(next_early, next_same),
            jnp.logical_not(late_west), jnp.logical_not(late_east),
        )

        def meet():
            pl.semaphore_wait(barrier, sum(one.astype(I32) for one in greetings))

        def tell(index, device):
            return lambda: pl.semaphore_signal(
                late_ready.at[index], inc=1, device_id=device, device_id_type=MESH
            )

        def remote(src, dst, index, device):
            return pltpu.make_async_remote_copy(
                src_ref=src, dst_ref=dst, send_sem=send_sem.at[index], recv_sem=recv_sem.at[index],
                device_id=device, device_id_type=MESH,
            )

        first, last = pl.ds(0, 2), pl.ds(rows - 2, 2)
        fold = pl.ds(rows - 3, 2)
        fold_in_group = pl.ds(5, 2)
        lo, hi = pl.ds(0, 2), pl.ds(6, 2)
        northward = [
            remote(t_hbm.at[:, last], h.at[0, :, lo], 0, {"lat": lat + 1}),
            remote(s_hbm.at[:, last], h.at[1, :, lo], 1, {"lat": lat + 1}),
            remote(v_hbm.at[:, pl.ds(rows - 1, 1)], hv.at[:, pl.ds(1, 1)], 2, {"lat": lat + 1}),
            remote(n_hbm.at[last], hs.at[lo], 3, {"lat": lat + 1}),
        ]
        southward = [
            remote(t_hbm.at[:, first], h_north.at[0, :, hi], 4, {"lat": lat - 1}),
            remote(s_hbm.at[:, first], h_north.at[1, :, hi], 5, {"lat": lat - 1}),
            remote(n_hbm.at[first], hs_north.at[hi], 6, {"lat": lat - 1}),
        ]
        folded = [
            remote(t_hbm.at[:, fold], fa.at[0, :, hi], 7, {"lon": mirror}),
            remote(s_hbm.at[:, fold], fa.at[1, :, hi], 8, {"lon": mirror}),
            remote(n_hbm.at[fold], fan.at[hi], 9, {"lon": mirror}),
        ]
        folded_next = remote(to_w.at[:, fold_in_group], fb.at[:, hi], 10, {"lon": mirror_next})
        own_next = pltpu.make_async_copy(to_w.at[:, fold_in_group], fb.at[:, hi], load_sem.at[5])
        eastward = [remote(to_e.at[m], from_w.at[m], 12 + m, {"lon": east}) for m in range(packs)]
        westward = remote(to_w, from_e, 11, {"lon": west})

        @pl.when(top)
        def _():
            meet()
            when(mirror_early, *[copy.start for copy in folded], tell(0, {"lon": mirror}))
            when(next_early, tell(1, {"lon": mirror_next}))
            when(early_east, tell(2, {"lon": east}))
            when(early_west, tell(3, {"lon": west}))

        loads[0].wait()
        packed_n = jnp.zeros((8, 128), F32)
        for slot in range(16):
            part = n[pl.ds(PAD + 8 * (slot % groups), 8)].astype(F32)
            packed_n = jnp.where(slot_of == slot, lanes(part, SLOT * slot + MID), packed_n)
        px[2 * packs] = packed_n
        n_up, n_down = lanes(packed_n, 5), lanes(packed_n, -2)

        for load in loads[1:4]:
            load.wait()
        top_east = jnp.logical_and(top, jnp.logical_not(late_east))
        for m in range(packs):
            packed = []
            for field in range(3):
                one = jnp.zeros((8, 128), F32)
                for slot in range(16):
                    k = packs * (slot // groups) + m
                    g = slot % groups
                    if field < 2:
                        part = q[field, k, pl.ds(PAD + 8 * g, 8)]
                    else:
                        part = u[k, pl.ds(8 * g, 8)]
                    one = jnp.where(slot_of == slot, lanes(part, SLOT * slot + MID), one)
                px[(0, packs, 2 * packs + 1)[field] + m] = one
                packed.append(one)
            t2, s2, u2 = packed
            s_up = lanes(s2, 2)
            to_e[m] = jnp.where(sl < 3, t2, jnp.where(sl < 5, s_up, jnp.where(sl < 6, lanes(u2, 3), n_up)))
            to_w[m] = jnp.where(sl < 3, n_down, jnp.where(sl < 5, t2, s_up))
            if m > 0:
                when(top_east, eastward[m - 1].start)

        when(top_self, own_next.start)
        @pl.when(top)
        def _():
            when(both(next_early, next_same), folded_next.start)
            when(jnp.logical_not(late_east), eastward[-1].start)
            when(jnp.logical_not(late_west), westward.start)

        @pl.when(plain)
        def _():
            meet()
            when(jnp.logical_not(late_east), *[copy.start for copy in eastward])
            when(jnp.logical_not(late_west), westward.start)
            when(early_east, tell(2, {"lon": east}))
            when(early_west, tell(3, {"lon": west}))
            when(below_top, tell(4, {"lat": lat + 1}))
            when(has_south, *[copy.start for copy in southward])
            when(has_north, *[copy.start for copy in northward])

        @pl.loop(0, levels)
        def _(k):
            z = depth(k.astype(F32))
            for g in range(groups):
                at = pl.ds(PAD + 8 * g, 8)
                rho[k, at] = density(q[0, k, at], q[1, k, at], z)

        pad_n = jnp.zeros((8, 128), I32)
        n[pl.ds(0, 8)] = pad_n
        n[pl.ds(top_row, 8)] = pad_n
        for g in range(groups):
            at = pl.ds(PAD + 8 * g, 8)
            here = n[at]
            fx = jnp.minimum(here, lanes(here, 1))
            face_x[pl.ds(8 * g, 8)] = fx
            inner = jnp.logical_and(lane > 1, lane < 127)
            keep_x[pl.ds(8 * g, 8)] = jnp.where(inner, fx, 0)
            f = jnp.minimum(here, n[pl.ds(PAD + 8 * g - 1, 8)])
            face_y[at] = f
            if g == 0:
                f = jnp.where(row > 1, f, 0)
            if g == groups - 1:
                f = jnp.where(row < 7, f, 0)
            keep_y[pl.ds(8 * g, 8)] = f
        face_y[pl.ds(0, 8)] = pad_n
        face_y[pl.ds(top_row, 8)] = pad_n

        outs = (t_out, s_out)
        loads[4].wait()
        fy[0, pl.ds(rows, 8)] = jnp.zeros((8, 128), F32)
        fy[1, pl.ds(rows, 8)] = jnp.zeros((8, 128), F32)

        def interior(k):
            kp = jnp.minimum(k + 1, levels - 1)
            km = jnp.maximum(k - 1, 0)
            ends = jnp.logical_or(k == 0, k == levels - 1)
            half_scale = jnp.where(ends, 0.5, 0.25).astype(F32)

            for g in reversed(range(groups)):
                r = PAD + 8 * g
                at, dn = pl.ds(r, 8), pl.ds(r - 1, 8)
                t0 = [q[i, k, at] for i in range(2)]
                zd = [q[i, kp, at] - q[i, km, at] for i in range(2)]
                rho0 = rho[k, at]
                rz = rho[kp, at] - rho[km, at]

                wet = k < face_x[pl.ds(8 * g, 8)]
                keep = k < keep_x[pl.ds(8 * g, 8)]
                c = lanes(u[k, pl.ds(8 * g, 8)], 1)
                up, coef = courant_terms(c)
                sk = slope_term(rho0 - lanes(rho0, 1), rz + lanes(rz, 1), half_scale)
                total = []
                for i in range(2):
                    qa = lanes(t0[i], 1)
                    d = jnp.where(wet, t0[i] - qa, 0.0)
                    f = tracer_flux(keep, c, up, coef, sk, qa, t0[i], d, lanes(d, 1), lanes(d, -1), zd[i] + lanes(zd[i], 1))
                    total.append(t0[i] + (f - lanes(f, -1)))

                wet = k < face_y[at]
                wet_back = k < face_y[dn]
                wet_ahead = k < face_y[pl.ds(r + 1, 8)]
                keep = k < keep_y[pl.ds(8 * g, 8)]
                c = v[k, dn]
                up, coef = courant_terms(c)
                sk = slope_term(rho0 - rho[k, dn], rz + (rho[kp, dn] - rho[km, dn]), half_scale)
                here = k < n[at]
                for i in range(2):
                    qa = q[i, k, dn]
                    d = jnp.where(wet, t0[i] - qa, 0.0)
                    back = jnp.where(wet_back, qa - q[i, k, pl.ds(r - 2, 8)], 0.0)
                    ahead = jnp.where(wet_ahead, q[i, k, pl.ds(r + 1, 8)] - t0[i], 0.0)
                    zsum = zd[i] + (q[i, kp, dn] - q[i, km, dn])
                    f = tracer_flux(keep, c, up, coef, sk, qa, t0[i], d, back, ahead, zsum)
                    fy[i, pl.ds(8 * g, 8)] = f
                    f_north = fy[i, pl.ds(8 * g + 1, 8)]
                    outs[i][k, pl.ds(8 * g, 8)] = jnp.where(here, total[i] + (f - f_north), 0.0)

        def heard(index):
            return lambda: pl.semaphore_wait(late_ready.at[index], 1)

        pl.loop(0, levels // 2)(interior)
        when(top, heard(4), *[copy.start for copy in southward])
        pl.loop(levels // 2, levels)(interior)

        when(late_east, heard(3), *[copy.start for copy in eastward])
        when(late_west, heard(2), westward.start)
        when(mirror_late, heard(0), *[copy.start for copy in folded])
        when(next_late, heard(1), folded_next.start)

        hop = levels // 2
        low = row < 4

        @pl.when(jnp.logical_not(has_south))
        def _():
            hs[lo] = jnp.zeros((2, 128), I32)

            @pl.loop(0, levels)
            def _(k):
                h[0, k, lo] = jnp.zeros((2, 128), F32)
                h[1, k, lo] = jnp.zeros((2, 128), F32)
                hv[k, lo] = jnp.zeros((2, 128), F32)

        when(has_south, *[copy.wait_recv for copy in northward])
        cells = jnp.where(row < 2, n[pl.ds(PAD, 8)], 0)

        def put(i, k, change):
            outs[i][k, pl.ds(0, 8)] = outs[i][k, pl.ds(0, 8)] + jnp.where(k < cells, change, 0.0)

        edge_rows(
            False, q, v, n,
            lambda i, m: jnp.where(low, h[i, m], rows_by(h[i, m + hop], 4)),
            lambda m: jnp.where(low, hv[m], rows_by(hv[m + hop], 4)),
            jnp.where(low, hs[...], rows_by(hs[...], 4)),
            levels, rows, put,
        )

        def north_rows():
            when(has_north, *[copy.wait_recv for copy in southward])
            when(top, *[copy.wait_recv for copy in folded])
            when(top_far, folded_next.wait_recv)
            when(top_self, own_next.wait)

            @pl.when(has_north)
            def _():
                hn[...] = jnp.where(low, rows_by(hs_north[...], -4), hs_north[...])
                for m in range(hop):
                    for i in range(2):
                        hp[i, m] = jnp.where(low, rows_by(h_north[i, m], -4), h_north[i, m + hop])

            @pl.when(top)
            def _():
                order = lax.rem(128 - lane, 128)
                spot = SLOT * (groups - 1) + MID

                def mirrored(x):
                    x = jnp.where(row % 2 == 0, rows_by(x, -1), rows_by(x, 1))
                    return jnp.take_along_axis(x, order, axis=1)

                x = jnp.where(lane == 0, lanes(fb[0], -(spot - 2)), fan[...].astype(F32))
                hn[...] = mirrored(jnp.where(low, rows_by(x, -4), x)).astype(I32)
                for m in range(packs):
                    next_cells = jnp.where(low, rows_by(fb[m], -4), lanes(fb[m], -span * (hop // packs)))
                    for part in range(hop // packs):
                        k = packs * part + m
                        for i in range(2):
                            x = jnp.where(low, rows_by(fa[i, k], -4), fa[i, k + hop])
                            x = jnp.where(lane == 0, lanes(next_cells, -(span * part + spot + 2 * i)), x)
                            hp[i, k] = mirrored(x)

        when(late_west, north_rows)

        for copy in eastward:
            copy.wait_recv()
        westward.wait_recv()

        def joined(own, before, after, by_west, by_east):
            a_west = jnp.where(sl < 2, lanes(before, by_west - 1), lanes(own, -1))
            a_east = jnp.where(sl < 7, lanes(own, 4), lanes(after, by_east + 4))
            b_west = jnp.where(sl < 1, lanes(before, by_west - 2), lanes(own, -2))
            b_east = jnp.where(sl < 6, lanes(own, 3), lanes(after, by_east + 3))
            return jnp.where(sl < 4, a_west, a_east), jnp.where(sl < 4, b_west, b_east)

        na, nb = joined(px[2 * packs], from_w[0], from_e[0], -5, 2)
        face_n = jnp.minimum(na, nb)
        level_of = packs * (lane // span)
        pairs = [
            [joined(px[m], from_w[m], from_e[m], 0, 0) for m in range(packs)],
            [joined(px[packs + m], from_w[m], from_e[m], -2, -2) for m in range(packs)],
        ]
        rho_pairs = []
        for m in range(packs):
            z = depth((level_of + m).astype(F32))
            rho_pairs.append([density(pairs[0][m][j], pairs[1][m][j], z) for j in range(2)])
        sums = [[a + b for a, b in one] for one in (*pairs, rho_pairs)]

        def zsum_of(one, m):
            if m < packs - 1:
                above = one[m + 1]
            else:
                above = jnp.where(lane < 128 - span, lanes(one[0], -span), one[m])
            if m > 0:
                below = one[m - 1]
            else:
                below = jnp.where(lane < span, one[0], lanes(one[packs - 1], span))
            return above - below

        used = jnp.logical_or(jnp.logical_or(sl == 1, sl == 2), jnp.logical_or(sl == 5, sl == 6))
        for m in range(packs):
            level = level_of + m
            half_scale = jnp.where(jnp.logical_or(level == 0, level == levels - 1), 0.5, 0.25)
            wet = level.astype(F32) < face_n
            keep = jnp.logical_and(wet, used)
            u2 = px[2 * packs + 1 + m]
            c = jnp.where(sl < 4, jnp.where(sl < 2, lanes(from_w[m], -4), lanes(u2, -1)), lanes(u2, 4))
            up, coef = courant_terms(c)
            sk = slope_term(rho_pairs[m][1] - rho_pairs[m][0], zsum_of(sums[2], m), half_scale)
            for i in range(2):
                qa, qb = pairs[i][m]
                d = jnp.where(wet, qb - qa, 0.0)
                f = tracer_flux(keep, c, up, coef, sk, qa, qb, d, lanes(d, 1), lanes(d, -1), zsum_of(sums[i], m))
                change = jnp.where(sl < MID, lanes(f, -3) - lanes(f, -4), lanes(f, 2) - lanes(f, 1))
                ex[i, m] = jnp.where(level.astype(F32) < px[2 * packs], change, 0.0)

        ends_x = jnp.logical_or(lane < 2, lane > 125)

        packed = [[ex[i, m] for m in range(packs)] for i in range(2)]
        for slot in range(16):
            for m in range(packs):
                for i in range(2):
                    k = packs * (slot // groups) + m
                    at = pl.ds(8 * (slot % groups), 8)
                    change = jnp.where(ends_x, lanes(packed[i][m], -(SLOT * slot + MID)), 0.0)
                    outs[i][k, at] = outs[i][k, at] + change

        when(jnp.logical_not(late_west), north_rows)

        for copy in eastward:
            copy.wait_send()
        westward.wait_send()

        @pl.when(has_south)
        def _():
            for copy in southward:
                copy.wait_send()

        @pl.when(has_north)
        def _():
            for copy in northward:
                copy.wait_send()

        @pl.when(top)
        def _():
            for copy in folded:
                copy.wait_send()

        @pl.when(top_far)
        def _():
            folded_next.wait_send()

    return kernel


def make_edge_kernel(levels, rows):
    top_row = PAD + rows

    def kernel(t_part, s_part, q, v, n, hp, hn, t_out, s_out, done, sem, end_sem):
        parts = (t_part, s_part)
        outs = (t_out, s_out)
        row = lax.broadcasted_iota(I32, (8, 128), 0)
        rest, end = pl.ds(0, rows - 8), pl.ds(rows - 8, 8)
        stores = [pltpu.make_async_copy(parts[i].at[:, rest], outs[i].at[:, rest], sem.at[i]) for i in range(2)]
        for store in stores:
            store.start()

        cells = jnp.where(row > 5, n[pl.ds(top_row - 8, 8)], 0)

        def put(i, k, change):
            done[i, k] = parts[i][k, end] + jnp.where(k < cells, change, 0.0)

        edge_rows(True, q, v, n, lambda i, m: hp[i, m], None, hn[...], levels, rows, put)

        ends = [pltpu.make_async_copy(done.at[i], outs[i].at[:, end], end_sem.at[i]) for i in range(2)]
        for store in ends:
            store.start()
        for store in stores + ends:
            store.wait()

    return kernel


def solution(mesh):
    nlon, nlat = mesh.shape["lon"], mesh.shape["lat"]

    def body(t, s, u, v, n):
        levels, rows, cols = t.shape
        packs = levels // (16 // (rows // 8))
        tall = rows + 2 * PAD
        plain = jax.ShapeDtypeStruct((levels, rows, cols), F32)
        parts = pl.pallas_call(
            make_kernel(nlon, nlat, levels, rows),
            out_shape=(
                pltpu.VMEM((levels, rows, cols), F32),
                pltpu.VMEM((levels, rows, cols), F32),
                pltpu.VMEM((2, levels, tall, cols), F32),
                pltpu.VMEM((levels, tall, cols), F32),
                pltpu.VMEM((tall, cols), I32),
                pltpu.VMEM((2, levels // 2, 8, cols), F32),
                pltpu.VMEM((8, cols), I32),
            ),
            in_specs=[pl.BlockSpec(memory_space=pl.ANY)] * 5,
            out_specs=(pl.BlockSpec(memory_space=pltpu.VMEM),) * 7,
            scratch_shapes=[
                pltpu.VMEM((2, levels, 8, cols), F32),
                pltpu.VMEM((levels, 8, cols), F32),
                pltpu.VMEM((8, cols), I32),
                pltpu.VMEM((2, levels, 8, cols), F32),
                pltpu.VMEM((8, cols), I32),
                pltpu.VMEM((levels, tall, cols), F32),
                pltpu.VMEM((levels, rows, cols), F32),
                pltpu.VMEM((rows, cols), I32),
                pltpu.VMEM((rows, cols), I32),
                pltpu.VMEM((tall, cols), I32),
                pltpu.VMEM((rows, cols), I32),
                pltpu.VMEM((2, rows + 8, cols), F32),
                pltpu.VMEM((3 * packs + 1, 8, cols), F32),
                pltpu.VMEM((packs, 8, cols), F32),
                pltpu.VMEM((packs, 8, cols), F32),
                pltpu.VMEM((packs, 8, cols), F32),
                pltpu.VMEM((packs, 8, cols), F32),
                pltpu.VMEM((2, levels, 8, cols), F32),
                pltpu.VMEM((packs, 8, cols), F32),
                pltpu.VMEM((8, cols), I32),
                pltpu.VMEM((2, packs, 8, cols), F32),
                pltpu.SemaphoreType.DMA((6,)),
                pltpu.SemaphoreType.DMA((12 + packs,)),
                pltpu.SemaphoreType.DMA((12 + packs,)),
                pltpu.SemaphoreType.REGULAR((5,)),
            ],
            compiler_params=pltpu.CompilerParams(collective_id=0, has_side_effects=True),
            name="tracer_step",
        )(t, s, u, v, n)
        return pl.pallas_call(
            make_edge_kernel(levels, rows),
            out_shape=(plain, plain),
            in_specs=[pl.BlockSpec(memory_space=pltpu.VMEM)] * 7,
            out_specs=(pl.BlockSpec(memory_space=pl.ANY),) * 2,
            scratch_shapes=[
                pltpu.VMEM((2, levels, 8, cols), F32),
                pltpu.SemaphoreType.DMA((2,)),
                pltpu.SemaphoreType.DMA((2,)),
            ],
            name="edge_rows",
        )(*[pltpu.with_memory_space_constraint(part, pltpu.VMEM) for part in parts])

    spec = P(None, "lat", "lon")
    return jax.shard_map(
        body, mesh=mesh, in_specs=(spec,) * 4 + (P("lat", "lon"),), out_specs=(spec, spec), check_vma=False
    )
```

```python
import jax
import jax.numpy as jnp
from jax import lax
from jax.experimental import pallas as pl
from jax.experimental.pallas import tpu as pltpu
from jax.sharding import PartitionSpec as P

ALPHA = 0.1655
BETA = 0.76554
CABBELING = 0.05952
LAMBDA_SALT = 0.00054914
THERMOBARIC = 0.0001497
PRESS_SALT = 1.109e-05
CROSS = 0.0024341
TOTAL_DEPTH = 5000.0
KAPPA = 0.1
SLOPE_MAX = 1.0
STRAT_MIN = 0.1

MESH = pl.DeviceIdType.MESH
F32 = jnp.float32
I32 = jnp.int32

PAD = 8
SLOT = 8
MID = 3


def density(t, s, z):
    lead = -ALPHA - (ALPHA * THERMOBARIC) * z
    salt = BETA - (BETA * PRESS_SALT) * z
    return t * (lead + (-0.5 * ALPHA * CABBELING) * t - CROSS * s) + s * (salt - (0.5 * BETA * LAMBDA_SALT) * s)


def slope_term(rho_diff, rho_zsum, half_scale):
    strat = jnp.maximum(half_scale * rho_zsum, STRAT_MIN)
    slope = jnp.clip(-rho_diff / strat, -SLOPE_MAX, SLOPE_MAX)
    return slope * (KAPPA * half_scale)


def courant_terms(c):
    up = c > 0.0
    coef = jnp.where(up, 0.5, -0.5) - 0.5 * c
    return up, coef


def tracer_flux(face, c, up, coef, sk, qa, qb, d, back, ahead, zsum):
    step = jnp.where(up, back, ahead)
    limited = jnp.minimum(jnp.maximum(step, jnp.minimum(d, 0.0)), jnp.maximum(d, 0.0))
    adv = c * (jnp.where(up, qa, qb) + coef * limited)
    return jnp.where(face, adv - (KAPPA * d + sk * zsum), 0.0)


def lanes(x, shift):
    return pltpu.roll(x, shift % 128, axis=x.ndim - 1)


def rows_by(x, shift):
    return pltpu.roll(x, shift % 8, axis=x.ndim - 2)


def edge_rows(north, q, v, n, halo, halo_v, halo_n, levels, rows, emit):
    top_row = PAD + rows
    hop = levels // 2
    row = lax.broadcasted_iota(I32, (8, 128), 0)
    low, place = row < 4, row % 4

    def own(load, m, base):
        return jnp.where(low, load(m, base), load(m + hop, base - 4))

    def pair(halo, load, m):
        if north:
            a = jnp.where(place == 3, rows_by(halo, 1), own(load, m, top_row - 3))
            b = jnp.where(place > 1, halo, own(load, m, top_row - 2))
        else:
            a = jnp.where(place < 2, halo, own(load, m, PAD - 2))
            b = jnp.where(place < 1, rows_by(halo, -1), own(load, m, PAD - 1))
        return a, b

    def load_v(k, base):
        return v[k, pl.ds(base, 8)]

    face_n = jnp.minimum(*pair(halo_n, lambda k, base: n[pl.ds(base, 8)], 0))
    keep_n = jnp.where(jnp.logical_or(place == 1, place == 2), face_n, 0)

    def level(m):
        z = jnp.where(low, TOTAL_DEPTH * (m + 0.5) / levels, TOTAL_DEPTH * (m + hop + 0.5) / levels)
        t, s = [pair(halo(i, m), lambda k, base, i=i: q[i, k, pl.ds(base, 8)], m) for i in range(2)]
        ra, rb = [density(t[j], s[j], z) for j in range(2)]
        return (t, s), (t[0] + t[1], s[0] + s[1], ra + rb), rb - ra

    held = [level(m) for m in range(hop)]
    for m in range(hop):
        tracers, sums, rho_diff = held[m]
        zsums = []
        for j in range(3):
            above = held[m + 1][1][j] if m + 1 < hop else jnp.where(low, rows_by(held[0][1][j], 4), sums[j])
            below = held[m - 1][1][j] if m > 0 else jnp.where(low, sums[j], rows_by(held[hop - 1][1][j], 4))
            zsums.append(above - below)
        half_scale = 0.25
        if m == 0:
            half_scale = jnp.where(low, 0.5, 0.25)
        if m == hop - 1:
            half_scale = jnp.where(low, 0.25, 0.5)
        k = jnp.where(low, m, m + hop)
        wet, keep = k < face_n, k < keep_n
        c = own(load_v, m, top_row - 3) if north else jnp.where(place < 2, halo_v(m), own(load_v, m, PAD - 2))
        up, coef = courant_terms(c)
        sk = slope_term(rho_diff, zsums[2], half_scale)
        for i in range(2):
            qa, qb = tracers[i]
            d = jnp.where(wet, qb - qa, 0.0)
            f = tracer_flux(keep, c, up, coef, sk, qa, qb, d, rows_by(d, 1), rows_by(d, -1), zsums[i])
            change = f - rows_by(f, -1)
            emit(i, m, rows_by(change, 6 if north else -1))
            emit(i, m + hop, rows_by(change, 2 if north else 3))


def make_kernel(nlon, nlat, levels, rows):
    groups = rows // 8
    per = 16 // groups
    packs = levels // per
    span = SLOT * groups
    top_row = PAD + rows

    def depth(k):
        return TOTAL_DEPTH * (k + 0.5) / levels

    def kernel(
        t_hbm, s_hbm, u_hbm, v_hbm, n_hbm,
        t_out, s_out, q, v, n, hp, hn,
        h, hv, hs, h_north, hs_north, rho, u, face_x, keep_x, face_y, keep_y, fy,
        px, to_e, to_w, from_w, from_e, fa, fb, fan,
        load_sem, send_sem, recv_sem, late_ready,
    ):
        lon = lax.axis_index("lon")
        lat = lax.axis_index("lat")
        east = lax.rem(lon + 1, nlon)
        west = lax.rem(lon + nlon - 1, nlon)
        has_south = lat > 0
        has_north = lat < nlat - 1
        top = lat == nlat - 1
        mirror = nlon - 1 - lon
        mirror_next = lax.rem(nlon - lon, nlon)
        mirror_far = mirror_next != lon
        top_far = jnp.logical_and(top, mirror_far)
        top_self = jnp.logical_and(top, jnp.logical_not(mirror_far))
        below_top = lat == nlat - 2
        plain = jnp.logical_not(top)
        half, quarter = nlon // 2, nlon // 4
        place = lax.rem(lon, half)
        early = place < quarter
        late_west = place == 0
        late_east = place == quarter - 1
        early_west = place == quarter
        early_east = place == half - 1
        odd = lax.rem(lat, 2) == 1
        skew_odd = jnp.logical_and(early_east, jnp.logical_and(odd, plain))
        skew_even = jnp.logical_and(early_east, jnp.logical_and(jnp.logical_not(odd), plain))
        level_pair = jnp.logical_not(early_east)
        prompt = jnp.logical_or(top, jnp.logical_and(skew_even, jnp.logical_not(below_top)))
        mirror_late = jnp.logical_and(top, early)
        mirror_early = jnp.logical_and(top, jnp.logical_not(early))
        next_late = jnp.logical_and(top_far, early)
        next_early = jnp.logical_and(top_far, place > quarter)
        next_same = jnp.logical_and(top_far, place == quarter)

        barrier = pltpu.get_barrier_semaphore()

        def greet(device):
            pl.semaphore_signal(barrier, inc=1, device_id=device, device_id_type=MESH)

        def when(condition, *steps):
            @pl.when(condition)
            def _():
                for step in steps:
                    step()

        def both(a, b):
            return jnp.logical_or(a, b)

        def also(a, b):
            return jnp.logical_and(a, b)

        when(also(has_south, jnp.logical_not(skew_odd)), lambda: greet({"lat": lat - 1}))
        northern = jnp.logical_not(both(skew_odd, below_top))
        when(also(has_north, northern), lambda: greet({"lat": lat + 1}))
        when(mirror_late, lambda: greet({"lon": mirror}))
        when(both(next_late, next_same), lambda: greet({"lon": mirror_next}))
        when(jnp.logical_not(early_east), lambda: greet({"lon": east}))
        when(jnp.logical_not(early_west), lambda: greet({"lon": west}))

        body_rows = pl.ds(PAD, rows)
        loads = [
            pltpu.make_async_copy(n_hbm, n.at[body_rows], load_sem.at[0]),
            pltpu.make_async_copy(t_hbm, q.at[0, :, body_rows], load_sem.at[1]),
            pltpu.make_async_copy(s_hbm, q.at[1, :, body_rows], load_sem.at[2]),
            pltpu.make_async_copy(u_hbm, u, load_sem.at[3]),
            pltpu.make_async_copy(v_hbm, v.at[:, body_rows], load_sem.at[4]),
        ]
        for load in loads:
            load.start()

        lane = lax.broadcasted_iota(I32, (8, 128), 1)
        row = lax.broadcasted_iota(I32, (8, 128), 0)
        slot_of = lane // SLOT
        sl = lane % SLOT

        greetings = (
            also(has_south, both(skew_odd, also(level_pair, plain))), also(has_north, both(both(skew_odd, below_top), level_pair)), mirror_early, both(next_early, next_same),
            jnp.logical_not(late_west), jnp.logical_not(late_east),
        )

        def meet():
            pl.semaphore_wait(barrier, sum(one.astype(I32) for one in greetings))

        def tell(index, device):
            return lambda: pl.semaphore_signal(
                late_ready.at[index], inc=1, device_id=device, device_id_type=MESH
            )

        def remote(src, dst, index, device):
            return pltpu.make_async_remote_copy(
                src_ref=src, dst_ref=dst, send_sem=send_sem.at[index], recv_sem=recv_sem.at[index],
                device_id=device, device_id_type=MESH,
            )

        first, last = pl.ds(0, 2), pl.ds(rows - 2, 2)
        fold = pl.ds(rows - 3, 2)
        fold_in_group = pl.ds(5, 2)
        lo, hi = pl.ds(0, 2), pl.ds(6, 2)
        northward = [
            remote(t_hbm.at[:, last], h.at[0, :, lo], 0, {"lat": lat + 1}),
            remote(s_hbm.at[:, last], h.at[1, :, lo], 1, {"lat": lat + 1}),
            remote(v_hbm.at[:, pl.ds(rows - 1, 1)], hv.at[:, pl.ds(1, 1)], 2, {"lat": lat + 1}),
            remote(n_hbm.at[last], hs.at[lo], 3, {"lat": lat + 1}),
        ]
        southward = [
            remote(t_hbm.at[:, first], h_north.at[0, :, hi], 4, {"lat": lat - 1}),
            remote(s_hbm.at[:, first], h_north.at[1, :, hi], 5, {"lat": lat - 1}),
            remote(n_hbm.at[first], hs_north.at[hi], 6, {"lat": lat - 1}),
        ]
        folded = [
            remote(t_hbm.at[:, fold], fa.at[0, :, hi], 7, {"lon": mirror}),
            remote(s_hbm.at[:, fold], fa.at[1, :, hi], 8, {"lon": mirror}),
            remote(n_hbm.at[fold], fan.at[hi], 9, {"lon": mirror}),
        ]
        folded_next = remote(to_w.at[:, fold_in_group], fb.at[:, hi], 10, {"lon": mirror_next})
        own_next = pltpu.make_async_copy(to_w.at[:, fold_in_group], fb.at[:, hi], load_sem.at[5])
        eastward = [remote(to_e.at[m], from_w.at[m], 12 + m, {"lon": east}) for m in range(packs)]
        westward = remote(to_w, from_e, 11, {"lon": west})

        def tell_even():
            when(also(skew_odd, has_north), tell(5, {"lat": lat + 1}))
            when(also(skew_odd, has_south), tell(6, {"lat": lat - 1}))

        @pl.when(prompt)
        def _():
            meet()
            when(mirror_early, *[copy.start for copy in folded], tell(0, {"lon": mirror}))
            when(next_early, tell(1, {"lon": mirror_next}))
            when(early_east, tell(2, {"lon": east}))
            when(also(top, early_west), tell(3, {"lon": west}))

        loads[0].wait()
        packed_n = jnp.zeros((8, 128), F32)
        for slot in range(16):
            part = n[pl.ds(PAD + 8 * (slot % groups), 8)].astype(F32)
            packed_n = jnp.where(slot_of == slot, lanes(part, SLOT * slot + MID), packed_n)
        px[2 * packs] = packed_n
        n_up, n_down = lanes(packed_n, 5), lanes(packed_n, -2)

        for load in loads[1:4]:
            load.wait()
        prompt_east = also(prompt, jnp.logical_not(late_east))
        for m in range(packs):
            packed = []
            for field in range(3):
                one = jnp.zeros((8, 128), F32)
                for slot in range(16):
                    k = packs * (slot // groups) + m
                    g = slot % groups
                    if field < 2:
                        part = q[field, k, pl.ds(PAD + 8 * g, 8)]
                    else:
                        part = u[k, pl.ds(8 * g, 8)]
                    one = jnp.where(slot_of == slot, lanes(part, SLOT * slot + MID), one)
                px[(0, packs, 2 * packs + 1)[field] + m] = one
                packed.append(one)
            t2, s2, u2 = packed
            s_up = lanes(s2, 2)
            to_e[m] = jnp.where(sl < 3, t2, jnp.where(sl < 5, s_up, jnp.where(sl < 6, lanes(u2, 3), n_up)))
            to_w[m] = jnp.where(sl < 3, n_down, jnp.where(sl < 5, t2, s_up))
            if m > 0:
                when(prompt_east, eastward[m - 1].start)

        when(top_self, own_next.start)
        @pl.when(prompt)
        def _():
            when(both(next_early, next_same), folded_next.start)
            when(jnp.logical_not(late_east), eastward[-1].start)
            when(jnp.logical_not(late_west), westward.start)

        @pl.when(jnp.logical_not(prompt))
        def _():
            meet()
            when(jnp.logical_not(late_east), *[copy.start for copy in eastward])
            when(jnp.logical_not(late_west), westward.start)
            when(early_east, tell(2, {"lon": east}))
            when(early_west, tell(3, {"lon": west}))
            tell_even()
            when(below_top, tell(4, {"lat": lat + 1}))
            when(also(has_south, jnp.logical_not(skew_even)), *[copy.start for copy in southward])
            when(has_north, *[copy.start for copy in northward])

        @pl.loop(0, levels)
        def _(k):
            z = depth(k.astype(F32))
            for g in range(groups):
                at = pl.ds(PAD + 8 * g, 8)
                rho[k, at] = density(q[0, k, at], q[1, k, at], z)

        pad_n = jnp.zeros((8, 128), I32)
        n[pl.ds(0, 8)] = pad_n
        n[pl.ds(top_row, 8)] = pad_n
        for g in range(groups):
            at = pl.ds(PAD + 8 * g, 8)
            here = n[at]
            fx = jnp.minimum(here, lanes(here, 1))
            face_x[pl.ds(8 * g, 8)] = fx
            inner = jnp.logical_and(lane > 1, lane < 127)
            keep_x[pl.ds(8 * g, 8)] = jnp.where(inner, fx, 0)
            f = jnp.minimum(here, n[pl.ds(PAD + 8 * g - 1, 8)])
            face_y[at] = f
            if g == 0:
                f = jnp.where(row > 1, f, 0)
            if g == groups - 1:
                f = jnp.where(row < 7, f, 0)
            keep_y[pl.ds(8 * g, 8)] = f
        face_y[pl.ds(0, 8)] = pad_n
        face_y[pl.ds(top_row, 8)] = pad_n

        outs = (t_out, s_out)
        loads[4].wait()
        fy[0, pl.ds(rows, 8)] = jnp.zeros((8, 128), F32)
        fy[1, pl.ds(rows, 8)] = jnp.zeros((8, 128), F32)

        def interior(k):
            kp = jnp.minimum(k + 1, levels - 1)
            km = jnp.maximum(k - 1, 0)
            ends = jnp.logical_or(k == 0, k == levels - 1)
            half_scale = jnp.where(ends, 0.5, 0.25).astype(F32)

            for g in reversed(range(groups)):
                r = PAD + 8 * g
                at, dn = pl.ds(r, 8), pl.ds(r - 1, 8)
                t0 = [q[i, k, at] for i in range(2)]
                zd = [q[i, kp, at] - q[i, km, at] for i in range(2)]
                rho0 = rho[k, at]
                rz = rho[kp, at] - rho[km, at]

                wet = k < face_x[pl.ds(8 * g, 8)]
                keep = k < keep_x[pl.ds(8 * g, 8)]
                c = lanes(u[k, pl.ds(8 * g, 8)], 1)
                up, coef = courant_terms(c)
                sk = slope_term(rho0 - lanes(rho0, 1), rz + lanes(rz, 1), half_scale)
                total = []
                for i in range(2):
                    qa = lanes(t0[i], 1)
                    d = jnp.where(wet, t0[i] - qa, 0.0)
                    f = tracer_flux(keep, c, up, coef, sk, qa, t0[i], d, lanes(d, 1), lanes(d, -1), zd[i] + lanes(zd[i], 1))
                    total.append(t0[i] + (f - lanes(f, -1)))

                wet = k < face_y[at]
                wet_back = k < face_y[dn]
                wet_ahead = k < face_y[pl.ds(r + 1, 8)]
                keep = k < keep_y[pl.ds(8 * g, 8)]
                c = v[k, dn]
                up, coef = courant_terms(c)
                sk = slope_term(rho0 - rho[k, dn], rz + (rho[kp, dn] - rho[km, dn]), half_scale)
                here = k < n[at]
                for i in range(2):
                    qa = q[i, k, dn]
                    d = jnp.where(wet, t0[i] - qa, 0.0)
                    back = jnp.where(wet_back, qa - q[i, k, pl.ds(r - 2, 8)], 0.0)
                    ahead = jnp.where(wet_ahead, q[i, k, pl.ds(r + 1, 8)] - t0[i], 0.0)
                    zsum = zd[i] + (q[i, kp, dn] - q[i, km, dn])
                    f = tracer_flux(keep, c, up, coef, sk, qa, t0[i], d, back, ahead, zsum)
                    fy[i, pl.ds(8 * g, 8)] = f
                    f_north = fy[i, pl.ds(8 * g + 1, 8)]
                    outs[i][k, pl.ds(8 * g, 8)] = jnp.where(here, total[i] + (f - f_north), 0.0)

        def heard(index):
            return lambda: pl.semaphore_wait(late_ready.at[index], 1)

        pl.loop(0, levels // 2)(interior)
        when(top, heard(4), *[copy.start for copy in southward])
        pl.loop(levels // 2, levels)(interior)

        when(also(skew_even, has_south), heard(5), *[copy.start for copy in southward])
        when(also(skew_even, jnp.logical_not(below_top)), heard(6), *[copy.start for copy in northward])
        when(late_east, heard(3), *[copy.start for copy in eastward])
        when(late_west, heard(2), westward.start)
        when(mirror_late, heard(0), *[copy.start for copy in folded])
        when(next_late, heard(1), folded_next.start)

        hop = levels // 2
        low = row < 4

        @pl.when(jnp.logical_not(has_south))
        def _():
            hs[lo] = jnp.zeros((2, 128), I32)

            @pl.loop(0, levels)
            def _(k):
                h[0, k, lo] = jnp.zeros((2, 128), F32)
                h[1, k, lo] = jnp.zeros((2, 128), F32)
                hv[k, lo] = jnp.zeros((2, 128), F32)

        when(has_south, *[copy.wait_recv for copy in northward])
        cells = jnp.where(row < 2, n[pl.ds(PAD, 8)], 0)

        def put(i, k, change):
            outs[i][k, pl.ds(0, 8)] = outs[i][k, pl.ds(0, 8)] + jnp.where(k < cells, change, 0.0)

        edge_rows(
            False, q, v, n,
            lambda i, m: jnp.where(low, h[i, m], rows_by(h[i, m + hop], 4)),
            lambda m: jnp.where(low, hv[m], rows_by(hv[m + hop], 4)),
            jnp.where(low, hs[...], rows_by(hs[...], 4)),
            levels, rows, put,
        )

        def north_rows():
            when(has_north, *[copy.wait_recv for copy in southward])
            when(top, *[copy.wait_recv for copy in folded])
            when(top_far, folded_next.wait_recv)
            when(top_self, own_next.wait)

            @pl.when(has_north)
            def _():
                hn[...] = jnp.where(low, rows_by(hs_north[...], -4), hs_north[...])
                for m in range(hop):
                    for i in range(2):
                        hp[i, m] = jnp.where(low, rows_by(h_north[i, m], -4), h_north[i, m + hop])

            @pl.when(top)
            def _():
                order = lax.rem(128 - lane, 128)
                spot = SLOT * (groups - 1) + MID

                def mirrored(x):
                    x = jnp.where(row % 2 == 0, rows_by(x, -1), rows_by(x, 1))
                    return jnp.take_along_axis(x, order, axis=1)

                x = jnp.where(lane == 0, lanes(fb[0], -(spot - 2)), fan[...].astype(F32))
                hn[...] = mirrored(jnp.where(low, rows_by(x, -4), x)).astype(I32)
                for m in range(packs):
                    next_cells = jnp.where(low, rows_by(fb[m], -4), lanes(fb[m], -span * (hop // packs)))
                    for part in range(hop // packs):
                        k = packs * part + m
                        for i in range(2):
                            x = jnp.where(low, rows_by(fa[i, k], -4), fa[i, k + hop])
                            x = jnp.where(lane == 0, lanes(next_cells, -(span * part + spot + 2 * i)), x)
                            hp[i, k] = mirrored(x)

        when(late_west, north_rows)

        for copy in eastward:
            copy.wait_recv()
        westward.wait_recv()

        def joined(own, before, after, by_west, by_east):
            a_west = jnp.where(sl < 2, lanes(before, by_west - 1), lanes(own, -1))
            a_east = jnp.where(sl < 7, lanes(own, 4), lanes(after, by_east + 4))
            b_west = jnp.where(sl < 1, lanes(before, by_west - 2), lanes(own, -2))
            b_east = jnp.where(sl < 6, lanes(own, 3), lanes(after, by_east + 3))
            return jnp.where(sl < 4, a_west, a_east), jnp.where(sl < 4, b_west, b_east)

        na, nb = joined(px[2 * packs], from_w[0], from_e[0], -5, 2)
        face_n = jnp.minimum(na, nb)
        level_of = packs * (lane // span)
        pairs = [
            [joined(px[m], from_w[m], from_e[m], 0, 0) for m in range(packs)],
            [joined(px[packs + m], from_w[m], from_e[m], -2, -2) for m in range(packs)],
        ]
        rho_pairs = []
        for m in range(packs):
            z = depth((level_of + m).astype(F32))
            rho_pairs.append([density(pairs[0][m][j], pairs[1][m][j], z) for j in range(2)])
        sums = [[a + b for a, b in one] for one in (*pairs, rho_pairs)]

        def zsum_of(one, m):
            if m < packs - 1:
                above = one[m + 1]
            else:
                above = jnp.where(lane < 128 - span, lanes(one[0], -span), one[m])
            if m > 0:
                below = one[m - 1]
            else:
                below = jnp.where(lane < span, one[0], lanes(one[packs - 1], span))
            return above - below

        used = jnp.logical_or(jnp.logical_or(sl == 1, sl == 2), jnp.logical_or(sl == 5, sl == 6))
        changes = [[], []]
        for m in range(packs):
            level = level_of + m
            half_scale = jnp.where(jnp.logical_or(level == 0, level == levels - 1), 0.5, 0.25)
            wet = level.astype(F32) < face_n
            keep = jnp.logical_and(wet, used)
            u2 = px[2 * packs + 1 + m]
            c = jnp.where(sl < 4, jnp.where(sl < 2, lanes(from_w[m], -4), lanes(u2, -1)), lanes(u2, 4))
            up, coef = courant_terms(c)
            sk = slope_term(rho_pairs[m][1] - rho_pairs[m][0], zsum_of(sums[2], m), half_scale)
            for i in range(2):
                qa, qb = pairs[i][m]
                d = jnp.where(wet, qb - qa, 0.0)
                f = tracer_flux(keep, c, up, coef, sk, qa, qb, d, lanes(d, 1), lanes(d, -1), zsum_of(sums[i], m))
                change = jnp.where(sl < MID, lanes(f, -3) - lanes(f, -4), lanes(f, 2) - lanes(f, 1))
                changes[i].append(jnp.where(level.astype(F32) < px[2 * packs], change, 0.0))

        ends_x = jnp.logical_or(lane < 2, lane > 125)

        for slot in range(16):
            for m in range(packs):
                for i in range(2):
                    k = packs * (slot // groups) + m
                    at = pl.ds(8 * (slot % groups), 8)
                    change = jnp.where(ends_x, lanes(changes[i][m], -(SLOT * slot + MID)), 0.0)
                    outs[i][k, at] = outs[i][k, at] + change

        when(jnp.logical_not(late_west), north_rows)

        for copy in eastward:
            copy.wait_send()
        westward.wait_send()

        @pl.when(has_south)
        def _():
            for copy in southward:
                copy.wait_send()

        @pl.when(has_north)
        def _():
            for copy in northward:
                copy.wait_send()

        @pl.when(top)
        def _():
            for copy in folded:
                copy.wait_send()

        @pl.when(top_far)
        def _():
            folded_next.wait_send()

    return kernel


def make_edge_kernel(levels, rows):
    top_row = PAD + rows

    def kernel(t_part, s_part, q, v, n, hp, hn, t_out, s_out, done, sem, end_sem):
        parts = (t_part, s_part)
        outs = (t_out, s_out)
        row = lax.broadcasted_iota(I32, (8, 128), 0)
        rest, end = pl.ds(0, rows - 8), pl.ds(rows - 8, 8)
        stores = [pltpu.make_async_copy(parts[i].at[:, rest], outs[i].at[:, rest], sem.at[i]) for i in range(2)]
        for store in stores:
            store.start()

        cells = jnp.where(row > 5, n[pl.ds(top_row - 8, 8)], 0)

        def put(i, k, change):
            done[i, k] = parts[i][k, end] + jnp.where(k < cells, change, 0.0)

        edge_rows(True, q, v, n, lambda i, m: hp[i, m], None, hn[...], levels, rows, put)

        ends = [pltpu.make_async_copy(done.at[i], outs[i].at[:, end], end_sem.at[i]) for i in range(2)]
        for store in ends:
            store.start()
        for store in stores + ends:
            store.wait()

    return kernel


def solution(mesh):
    nlon, nlat = mesh.shape["lon"], mesh.shape["lat"]

    def body(t, s, u, v, n):
        levels, rows, cols = t.shape
        packs = levels // (16 // (rows // 8))
        tall = rows + 2 * PAD
        plain = jax.ShapeDtypeStruct((levels, rows, cols), F32)
        parts = pl.pallas_call(
            make_kernel(nlon, nlat, levels, rows),
            out_shape=(
                pltpu.VMEM((levels, rows, cols), F32),
                pltpu.VMEM((levels, rows, cols), F32),
                pltpu.VMEM((2, levels, tall, cols), F32),
                pltpu.VMEM((levels, tall, cols), F32),
                pltpu.VMEM((tall, cols), I32),
                pltpu.VMEM((2, levels // 2, 8, cols), F32),
                pltpu.VMEM((8, cols), I32),
            ),
            in_specs=[pl.BlockSpec(memory_space=pl.ANY)] * 5,
            out_specs=(pl.BlockSpec(memory_space=pltpu.VMEM),) * 7,
            scratch_shapes=[
                pltpu.VMEM((2, levels, 8, cols), F32),
                pltpu.VMEM((levels, 8, cols), F32),
                pltpu.VMEM((8, cols), I32),
                pltpu.VMEM((2, levels, 8, cols), F32),
                pltpu.VMEM((8, cols), I32),
                pltpu.VMEM((levels, tall, cols), F32),
                pltpu.VMEM((levels, rows, cols), F32),
                pltpu.VMEM((rows, cols), I32),
                pltpu.VMEM((rows, cols), I32),
                pltpu.VMEM((tall, cols), I32),
                pltpu.VMEM((rows, cols), I32),
                pltpu.VMEM((2, rows + 8, cols), F32),
                pltpu.VMEM((3 * packs + 1, 8, cols), F32),
                pltpu.VMEM((packs, 8, cols), F32),
                pltpu.VMEM((packs, 8, cols), F32),
                pltpu.VMEM((packs, 8, cols), F32),
                pltpu.VMEM((packs, 8, cols), F32),
                pltpu.VMEM((2, levels, 8, cols), F32),
                pltpu.VMEM((packs, 8, cols), F32),
                pltpu.VMEM((8, cols), I32),
                pltpu.SemaphoreType.DMA((6,)),
                pltpu.SemaphoreType.DMA((12 + packs,)),
                pltpu.SemaphoreType.DMA((12 + packs,)),
                pltpu.SemaphoreType.REGULAR((7,)),
            ],
            compiler_params=pltpu.CompilerParams(collective_id=0, has_side_effects=True),
            name="tracer_step",
        )(t, s, u, v, n)
        return pl.pallas_call(
            make_edge_kernel(levels, rows),
            out_shape=(plain, plain),
            in_specs=[pl.BlockSpec(memory_space=pltpu.VMEM)] * 7,
            out_specs=(pl.BlockSpec(memory_space=pl.ANY),) * 2,
            scratch_shapes=[
                pltpu.VMEM((2, levels, 8, cols), F32),
                pltpu.SemaphoreType.DMA((2,)),
                pltpu.SemaphoreType.DMA((2,)),
            ],
            name="edge_rows",
        )(*[pltpu.with_memory_space_constraint(part, pltpu.VMEM) for part in parts])

    spec = P(None, "lat", "lon")
    return jax.shard_map(
        body, mesh=mesh, in_specs=(spec,) * 4 + (P("lat", "lon"),), out_specs=(spec, spec), check_vma=False
    )
```

```python
import jax
import jax.numpy as jnp
from jax import lax
from jax.experimental import pallas as pl
from jax.experimental.pallas import tpu as pltpu
from jax.sharding import PartitionSpec as P

ALPHA = 0.1655
BETA = 0.76554
CABBELING = 0.05952
LAMBDA_SALT = 0.00054914
THERMOBARIC = 0.0001497
PRESS_SALT = 1.109e-05
CROSS = 0.0024341
TOTAL_DEPTH = 5000.0
KAPPA = 0.1
SLOPE_MAX = 1.0
STRAT_MIN = 0.1

MESH = pl.DeviceIdType.MESH
F32 = jnp.float32
I32 = jnp.int32

PAD = 8
SLOT = 8
MID = 3


def density(t, s, z):
    lead = -ALPHA - (ALPHA * THERMOBARIC) * z
    salt = BETA - (BETA * PRESS_SALT) * z
    return t * (lead + (-0.5 * ALPHA * CABBELING) * t - CROSS * s) + s * (salt - (0.5 * BETA * LAMBDA_SALT) * s)


def slope_term(rho_diff, rho_zsum, half_scale):
    strat = jnp.maximum(half_scale * rho_zsum, STRAT_MIN)
    slope = jnp.clip(-rho_diff / strat, -SLOPE_MAX, SLOPE_MAX)
    return slope * (KAPPA * half_scale)


def courant_terms(c):
    up = c > 0.0
    coef = jnp.where(up, 0.5, -0.5) - 0.5 * c
    return up, coef


def tracer_flux(face, c, up, coef, sk, qa, qb, d, back, ahead, zsum):
    step = jnp.where(up, back, ahead)
    limited = jnp.minimum(jnp.maximum(step, jnp.minimum(d, 0.0)), jnp.maximum(d, 0.0))
    adv = c * (jnp.where(up, qa, qb) + coef * limited)
    return jnp.where(face, adv - (KAPPA * d + sk * zsum), 0.0)


def lanes(x, shift):
    return pltpu.roll(x, shift % 128, axis=x.ndim - 1)


def rows_by(x, shift):
    return pltpu.roll(x, shift % 8, axis=x.ndim - 2)


def edge_rows(north, q, v, n, halo, halo_v, halo_n, levels, rows, emit):
    top_row = PAD + rows
    hop = levels // 2
    row = lax.broadcasted_iota(I32, (8, 128), 0)
    low, place = row < 4, row % 4

    def own(load, m, base):
        return jnp.where(low, load(m, base), load(m + hop, base - 4))

    def pair(halo, load, m):
        if north:
            a = jnp.where(place == 3, rows_by(halo, 1), own(load, m, top_row - 3))
            b = jnp.where(place > 1, halo, own(load, m, top_row - 2))
        else:
            a = jnp.where(place < 2, halo, own(load, m, PAD - 2))
            b = jnp.where(place < 1, rows_by(halo, -1), own(load, m, PAD - 1))
        return a, b

    def load_v(k, base):
        return v[k, pl.ds(base, 8)]

    face_n = jnp.minimum(*pair(halo_n, lambda k, base: n[pl.ds(base, 8)], 0))
    keep_n = jnp.where(jnp.logical_or(place == 1, place == 2), face_n, 0)

    def level(m):
        z = jnp.where(low, TOTAL_DEPTH * (m + 0.5) / levels, TOTAL_DEPTH * (m + hop + 0.5) / levels)
        t, s = [pair(halo(i, m), lambda k, base, i=i: q[i, k, pl.ds(base, 8)], m) for i in range(2)]
        ra, rb = [density(t[j], s[j], z) for j in range(2)]
        return (t, s), (t[0] + t[1], s[0] + s[1], ra + rb), rb - ra

    held = [level(m) for m in range(hop)]
    for m in range(hop):
        tracers, sums, rho_diff = held[m]
        zsums = []
        for j in range(3):
            above = held[m + 1][1][j] if m + 1 < hop else jnp.where(low, rows_by(held[0][1][j], 4), sums[j])
            below = held[m - 1][1][j] if m > 0 else jnp.where(low, sums[j], rows_by(held[hop - 1][1][j], 4))
            zsums.append(above - below)
        half_scale = 0.25
        if m == 0:
            half_scale = jnp.where(low, 0.5, 0.25)
        if m == hop - 1:
            half_scale = jnp.where(low, 0.25, 0.5)
        k = jnp.where(low, m, m + hop)
        wet, keep = k < face_n, k < keep_n
        c = own(load_v, m, top_row - 3) if north else jnp.where(place < 2, halo_v(m), own(load_v, m, PAD - 2))
        up, coef = courant_terms(c)
        sk = slope_term(rho_diff, zsums[2], half_scale)
        for i in range(2):
            qa, qb = tracers[i]
            d = jnp.where(wet, qb - qa, 0.0)
            f = tracer_flux(keep, c, up, coef, sk, qa, qb, d, rows_by(d, 1), rows_by(d, -1), zsums[i])
            change = f - rows_by(f, -1)
            emit(i, m, rows_by(change, 6 if north else -1))
            emit(i, m + hop, rows_by(change, 2 if north else 3))


def make_kernel(nlon, nlat, levels, rows):
    groups = rows // 8
    per = 16 // groups
    packs = levels // per
    span = SLOT * groups
    top_row = PAD + rows

    def depth(k):
        return TOTAL_DEPTH * (k + 0.5) / levels

    def kernel(
        t_hbm, s_hbm, u_hbm, v_hbm, n_hbm,
        t_out, s_out, q, v, n, hp, hn,
        h, hv, hs, h_north, hs_north, rho, u, face_x, keep_x, face_y, keep_y, fy,
        px, to_e, to_w, from_w, from_e, fa, fb, fan,
        load_sem, send_sem, recv_sem, late_ready,
    ):
        lon = lax.axis_index("lon")
        lat = lax.axis_index("lat")
        east = lax.rem(lon + 1, nlon)
        west = lax.rem(lon + nlon - 1, nlon)
        has_south = lat > 0
        has_north = lat < nlat - 1
        top = lat == nlat - 1
        mirror = nlon - 1 - lon
        mirror_next = lax.rem(nlon - lon, nlon)
        mirror_far = mirror_next != lon
        top_far = jnp.logical_and(top, mirror_far)
        top_self = jnp.logical_and(top, jnp.logical_not(mirror_far))
        below_top = lat == nlat - 2
        plain = jnp.logical_not(top)
        half, quarter = nlon // 2, nlon // 4
        place = lax.rem(lon, half)
        early = place < quarter
        late_west = place == 0
        late_east = place == quarter - 1
        early_west = place == quarter
        early_east = place == half - 1
        odd = lax.rem(lat, 2) == 1
        skew_odd = jnp.logical_and(early_east, jnp.logical_and(odd, plain))
        skew_even = jnp.logical_and(early_east, jnp.logical_and(jnp.logical_not(odd), plain))
        level_pair = jnp.logical_not(early_east)
        prompt = jnp.logical_or(top, jnp.logical_and(skew_even, jnp.logical_not(below_top)))
        mirror_late = jnp.logical_and(top, early)
        mirror_early = jnp.logical_and(top, jnp.logical_not(early))
        next_late = jnp.logical_and(top_far, early)
        next_early = jnp.logical_and(top_far, place > quarter)
        next_same = jnp.logical_and(top_far, place == quarter)

        barrier = pltpu.get_barrier_semaphore()

        def greet(device):
            pl.semaphore_signal(barrier, inc=1, device_id=device, device_id_type=MESH)

        def when(condition, *steps):
            @pl.when(condition)
            def _():
                for step in steps:
                    step()

        def both(a, b):
            return jnp.logical_or(a, b)

        def also(a, b):
            return jnp.logical_and(a, b)

        when(also(has_south, jnp.logical_not(skew_odd)), lambda: greet({"lat": lat - 1}))
        northern = jnp.logical_not(both(skew_odd, below_top))
        when(also(has_north, northern), lambda: greet({"lat": lat + 1}))
        when(mirror_late, lambda: greet({"lon": mirror}))
        when(both(next_late, next_same), lambda: greet({"lon": mirror_next}))
        when(jnp.logical_not(early_east), lambda: greet({"lon": east}))
        when(jnp.logical_not(early_west), lambda: greet({"lon": west}))

        body_rows = pl.ds(PAD, rows)
        loads = [
            pltpu.make_async_copy(n_hbm, n.at[body_rows], load_sem.at[0]),
            pltpu.make_async_copy(t_hbm, q.at[0, :, body_rows], load_sem.at[1]),
            pltpu.make_async_copy(s_hbm, q.at[1, :, body_rows], load_sem.at[2]),
            pltpu.make_async_copy(u_hbm, u, load_sem.at[3]),
            pltpu.make_async_copy(v_hbm, v.at[:, body_rows], load_sem.at[4]),
        ]
        for load in loads:
            load.start()

        lane = lax.broadcasted_iota(I32, (8, 128), 1)
        row = lax.broadcasted_iota(I32, (8, 128), 0)
        slot_of = lane // SLOT
        sl = lane % SLOT

        greetings = (
            also(has_south, both(skew_odd, also(level_pair, plain))), also(has_north, both(both(skew_odd, below_top), level_pair)), mirror_early, both(next_early, next_same),
            jnp.logical_not(late_west), jnp.logical_not(late_east),
        )

        def meet():
            pl.semaphore_wait(barrier, sum(one.astype(I32) for one in greetings))

        def tell(index, device):
            return lambda: pl.semaphore_signal(
                late_ready.at[index], inc=1, device_id=device, device_id_type=MESH
            )

        def remote(src, dst, index, device):
            return pltpu.make_async_remote_copy(
                src_ref=src, dst_ref=dst, send_sem=send_sem.at[index], recv_sem=recv_sem.at[index],
                device_id=device, device_id_type=MESH,
            )

        first, last = pl.ds(0, 2), pl.ds(rows - 2, 2)
        fold = pl.ds(rows - 3, 2)
        lower, upper = pl.ds(0, levels // 2), pl.ds(levels // 2, levels // 2)
        fold_in_group = pl.ds(5, 2)
        lo, hi = pl.ds(0, 2), pl.ds(6, 2)
        northward = [
            remote(t_hbm.at[:, last], h.at[0, :, lo], 0, {"lat": lat + 1}),
            remote(s_hbm.at[:, last], h.at[1, :, lo], 1, {"lat": lat + 1}),
            remote(v_hbm.at[:, pl.ds(rows - 1, 1)], hv.at[:, pl.ds(1, 1)], 2, {"lat": lat + 1}),
            remote(n_hbm.at[last], hs.at[lo], 3, {"lat": lat + 1}),
        ]
        southward = [
            remote(t_hbm.at[:, first], h_north.at[0, :, hi], 4, {"lat": lat - 1}),
            remote(s_hbm.at[:, first], h_north.at[1, :, hi], 5, {"lat": lat - 1}),
            remote(n_hbm.at[first], hs_north.at[hi], 6, {"lat": lat - 1}),
        ]
        folded = [
            remote(n_hbm.at[fold], fan.at[hi], 9, {"lon": mirror}),
            remote(t_hbm.at[lower, fold], fa.at[0, lower, hi], 7, {"lon": mirror}),
            remote(s_hbm.at[lower, fold], fa.at[1, lower, hi], 8, {"lon": mirror}),
            remote(t_hbm.at[upper, fold], fa.at[0, upper, hi], 12 + packs, {"lon": mirror}),
            remote(s_hbm.at[upper, fold], fa.at[1, upper, hi], 13 + packs, {"lon": mirror}),
        ]
        folded_next = remote(to_w.at[:, fold_in_group], fb.at[:, hi], 10, {"lon": mirror_next})
        own_next = pltpu.make_async_copy(to_w.at[:, fold_in_group], fb.at[:, hi], load_sem.at[5])
        eastward = [remote(to_e.at[m], from_w.at[m], 12 + m, {"lon": east}) for m in range(packs)]
        westward = remote(to_w, from_e, 11, {"lon": west})

        def tell_even():
            when(also(skew_odd, has_north), tell(5, {"lat": lat + 1}))
            when(also(skew_odd, has_south), tell(6, {"lat": lat - 1}))

        @pl.when(prompt)
        def _():
            meet()
            when(mirror_early, *[copy.start for copy in folded], tell(0, {"lon": mirror}))
            when(next_early, tell(1, {"lon": mirror_next}))
            when(early_east, tell(2, {"lon": east}))
            when(also(top, early_west), tell(3, {"lon": west}))

        loads[0].wait()
        packed_n = jnp.zeros((8, 128), F32)
        for slot in range(16):
            part = n[pl.ds(PAD + 8 * (slot % groups), 8)].astype(F32)
            packed_n = jnp.where(slot_of == slot, lanes(part, SLOT * slot + MID), packed_n)
        px[2 * packs] = packed_n
        n_up, n_down = lanes(packed_n, 5), lanes(packed_n, -2)

        for load in loads[1:4]:
            load.wait()
        prompt_east = also(prompt, jnp.logical_not(late_east))
        for m in range(packs):
            packed = []
            for field in range(3):
                one = jnp.zeros((8, 128), F32)
                for slot in range(16):
                    k = packs * (slot // groups) + m
                    g = slot % groups
                    if field < 2:
                        part = q[field, k, pl.ds(PAD + 8 * g, 8)]
                    else:
                        part = u[k, pl.ds(8 * g, 8)]
                    one = jnp.where(slot_of == slot, lanes(part, SLOT * slot + MID), one)
                px[(0, packs, 2 * packs + 1)[field] + m] = one
                packed.append(one)
            t2, s2, u2 = packed
            s_up = lanes(s2, 2)
            to_e[m] = jnp.where(sl < 3, t2, jnp.where(sl < 5, s_up, jnp.where(sl < 6, lanes(u2, 3), n_up)))
            to_w[m] = jnp.where(sl < 3, n_down, jnp.where(sl < 5, t2, s_up))
            if m > 0:
                when(prompt_east, eastward[m - 1].start)

        when(top_self, own_next.start)
        @pl.when(prompt)
        def _():
            when(both(next_early, next_same), folded_next.start)
            when(jnp.logical_not(late_east), eastward[-1].start)
            when(jnp.logical_not(late_west), westward.start)

        @pl.when(jnp.logical_not(prompt))
        def _():
            meet()
            when(jnp.logical_not(late_east), *[copy.start for copy in eastward])
            when(jnp.logical_not(late_west), westward.start)
            when(early_east, tell(2, {"lon": east}))
            when(early_west, tell(3, {"lon": west}))
            tell_even()
            when(below_top, tell(4, {"lat": lat + 1}))
            when(also(has_south, jnp.logical_not(skew_even)), *[copy.start for copy in southward])
            when(has_north, *[copy.start for copy in northward])

        @pl.loop(0, levels)
        def _(k):
            z = depth(k.astype(F32))
            for g in range(groups):
                at = pl.ds(PAD + 8 * g, 8)
                rho[k, at] = density(q[0, k, at], q[1, k, at], z)

        pad_n = jnp.zeros((8, 128), I32)
        n[pl.ds(0, 8)] = pad_n
        n[pl.ds(top_row, 8)] = pad_n
        for g in range(groups):
            at = pl.ds(PAD + 8 * g, 8)
            here = n[at]
            fx = jnp.minimum(here, lanes(here, 1))
            face_x[pl.ds(8 * g, 8)] = fx
            inner = jnp.logical_and(lane > 1, lane < 127)
            keep_x[pl.ds(8 * g, 8)] = jnp.where(inner, fx, 0)
            f = jnp.minimum(here, n[pl.ds(PAD + 8 * g - 1, 8)])
            face_y[at] = f
            if g == 0:
                f = jnp.where(row > 1, f, 0)
            if g == groups - 1:
                f = jnp.where(row < 7, f, 0)
            keep_y[pl.ds(8 * g, 8)] = f
        face_y[pl.ds(0, 8)] = pad_n
        face_y[pl.ds(top_row, 8)] = pad_n

        outs = (t_out, s_out)
        loads[4].wait()
        fy[0, pl.ds(rows, 8)] = jnp.zeros((8, 128), F32)
        fy[1, pl.ds(rows, 8)] = jnp.zeros((8, 128), F32)

        def interior(k):
            kp = jnp.minimum(k + 1, levels - 1)
            km = jnp.maximum(k - 1, 0)
            ends = jnp.logical_or(k == 0, k == levels - 1)
            half_scale = jnp.where(ends, 0.5, 0.25).astype(F32)

            for g in reversed(range(groups)):
                r = PAD + 8 * g
                at, dn = pl.ds(r, 8), pl.ds(r - 1, 8)
                t0 = [q[i, k, at] for i in range(2)]
                zd = [q[i, kp, at] - q[i, km, at] for i in range(2)]
                rho0 = rho[k, at]
                rz = rho[kp, at] - rho[km, at]

                wet = k < face_x[pl.ds(8 * g, 8)]
                keep = k < keep_x[pl.ds(8 * g, 8)]
                c = lanes(u[k, pl.ds(8 * g, 8)], 1)
                up, coef = courant_terms(c)
                sk = slope_term(rho0 - lanes(rho0, 1), rz + lanes(rz, 1), half_scale)
                total = []
                for i in range(2):
                    qa = lanes(t0[i], 1)
                    d = jnp.where(wet, t0[i] - qa, 0.0)
                    f = tracer_flux(keep, c, up, coef, sk, qa, t0[i], d, lanes(d, 1), lanes(d, -1), zd[i] + lanes(zd[i], 1))
                    total.append(t0[i] + (f - lanes(f, -1)))

                wet = k < face_y[at]
                wet_back = k < face_y[dn]
                wet_ahead = k < face_y[pl.ds(r + 1, 8)]
                keep = k < keep_y[pl.ds(8 * g, 8)]
                c = v[k, dn]
                up, coef = courant_terms(c)
                sk = slope_term(rho0 - rho[k, dn], rz + (rho[kp, dn] - rho[km, dn]), half_scale)
                here = k < n[at]
                for i in range(2):
                    qa = q[i, k, dn]
                    d = jnp.where(wet, t0[i] - qa, 0.0)
                    back = jnp.where(wet_back, qa - q[i, k, pl.ds(r - 2, 8)], 0.0)
                    ahead = jnp.where(wet_ahead, q[i, k, pl.ds(r + 1, 8)] - t0[i], 0.0)
                    zsum = zd[i] + (q[i, kp, dn] - q[i, km, dn])
                    f = tracer_flux(keep, c, up, coef, sk, qa, t0[i], d, back, ahead, zsum)
                    fy[i, pl.ds(8 * g, 8)] = f
                    f_north = fy[i, pl.ds(8 * g + 1, 8)]
                    outs[i][k, pl.ds(8 * g, 8)] = jnp.where(here, total[i] + (f - f_north), 0.0)

        def heard(index):
            return lambda: pl.semaphore_wait(late_ready.at[index], 1)

        pl.loop(0, levels // 2)(interior)
        when(top, heard(4), *[copy.start for copy in southward])
        pl.loop(levels // 2, levels)(interior)

        when(also(skew_even, has_south), heard(5), *[copy.start for copy in southward])
        when(also(skew_even, jnp.logical_not(below_top)), heard(6), *[copy.start for copy in northward])
        when(late_east, heard(3), *[copy.start for copy in eastward])
        when(late_west, heard(2), westward.start)
        when(mirror_late, heard(0), *[copy.start for copy in folded])
        when(next_late, heard(1), folded_next.start)

        hop = levels // 2
        low = row < 4

        @pl.when(jnp.logical_not(has_south))
        def _():
            hs[lo] = jnp.zeros((2, 128), I32)

            @pl.loop(0, levels)
            def _(k):
                h[0, k, lo] = jnp.zeros((2, 128), F32)
                h[1, k, lo] = jnp.zeros((2, 128), F32)
                hv[k, lo] = jnp.zeros((2, 128), F32)

        when(has_south, *[copy.wait_recv for copy in northward])
        cells = jnp.where(row < 2, n[pl.ds(PAD, 8)], 0)

        def put(i, k, change):
            outs[i][k, pl.ds(0, 8)] = outs[i][k, pl.ds(0, 8)] + jnp.where(k < cells, change, 0.0)

        edge_rows(
            False, q, v, n,
            lambda i, m: jnp.where(low, h[i, m], rows_by(h[i, m + hop], 4)),
            lambda m: jnp.where(low, hv[m], rows_by(hv[m + hop], 4)),
            jnp.where(low, hs[...], rows_by(hs[...], 4)),
            levels, rows, put,
        )

        def north_rows():
            when(has_north, *[copy.wait_recv for copy in southward])
            when(top, *[copy.wait_recv for copy in folded])
            when(top_far, folded_next.wait_recv)
            when(top_self, own_next.wait)

            @pl.when(has_north)
            def _():
                hn[...] = jnp.where(low, rows_by(hs_north[...], -4), hs_north[...])
                for m in range(hop):
                    for i in range(2):
                        hp[i, m] = jnp.where(low, rows_by(h_north[i, m], -4), h_north[i, m + hop])

            @pl.when(top)
            def _():
                order = lax.rem(128 - lane, 128)
                spot = SLOT * (groups - 1) + MID

                def mirrored(x):
                    x = jnp.where(row % 2 == 0, rows_by(x, -1), rows_by(x, 1))
                    return jnp.take_along_axis(x, order, axis=1)

                x = jnp.where(lane == 0, lanes(fb[0], -(spot - 2)), fan[...].astype(F32))
                hn[...] = mirrored(jnp.where(low, rows_by(x, -4), x)).astype(I32)
                for m in range(packs):
                    next_cells = jnp.where(low, rows_by(fb[m], -4), lanes(fb[m], -span * (hop // packs)))
                    for part in range(hop // packs):
                        k = packs * part + m
                        for i in range(2):
                            x = jnp.where(low, rows_by(fa[i, k], -4), fa[i, k + hop])
                            x = jnp.where(lane == 0, lanes(next_cells, -(span * part + spot + 2 * i)), x)
                            hp[i, k] = mirrored(x)

        when(late_west, north_rows)

        for copy in eastward:
            copy.wait_recv()
        westward.wait_recv()

        def joined(own, before, after, by_west, by_east):
            a_west = jnp.where(sl < 2, lanes(before, by_west - 1), lanes(own, -1))
            a_east = jnp.where(sl < 7, lanes(own, 4), lanes(after, by_east + 4))
            b_west = jnp.where(sl < 1, lanes(before, by_west - 2), lanes(own, -2))
            b_east = jnp.where(sl < 6, lanes(own, 3), lanes(after, by_east + 3))
            return jnp.where(sl < 4, a_west, a_east), jnp.where(sl < 4, b_west, b_east)

        na, nb = joined(px[2 * packs], from_w[0], from_e[0], -5, 2)
        face_n = jnp.minimum(na, nb)
        level_of = packs * (lane // span)
        pairs = [
            [joined(px[m], from_w[m], from_e[m], 0, 0) for m in range(packs)],
            [joined(px[packs + m], from_w[m], from_e[m], -2, -2) for m in range(packs)],
        ]
        rho_pairs = []
        for m in range(packs):
            z = depth((level_of + m).astype(F32))
            rho_pairs.append([density(pairs[0][m][j], pairs[1][m][j], z) for j in range(2)])
        sums = [[a + b for a, b in one] for one in (*pairs, rho_pairs)]

        def zsum_of(one, m):
            if m < packs - 1:
                above = one[m + 1]
            else:
                above = jnp.where(lane < 128 - span, lanes(one[0], -span), one[m])
            if m > 0:
                below = one[m - 1]
            else:
                below = jnp.where(lane < span, one[0], lanes(one[packs - 1], span))
            return above - below

        used = jnp.logical_or(jnp.logical_or(sl == 1, sl == 2), jnp.logical_or(sl == 5, sl == 6))
        changes = [[], []]
        for m in range(packs):
            level = level_of + m
            half_scale = jnp.where(jnp.logical_or(level == 0, level == levels - 1), 0.5, 0.25)
            wet = level.astype(F32) < face_n
            keep = jnp.logical_and(wet, used)
            u2 = px[2 * packs + 1 + m]
            c = jnp.where(sl < 4, jnp.where(sl < 2, lanes(from_w[m], -4), lanes(u2, -1)), lanes(u2, 4))
            up, coef = courant_terms(c)
            sk = slope_term(rho_pairs[m][1] - rho_pairs[m][0], zsum_of(sums[2], m), half_scale)
            for i in range(2):
                qa, qb = pairs[i][m]
                d = jnp.where(wet, qb - qa, 0.0)
                f = tracer_flux(keep, c, up, coef, sk, qa, qb, d, lanes(d, 1), lanes(d, -1), zsum_of(sums[i], m))
                change = jnp.where(sl < MID, lanes(f, -3) - lanes(f, -4), lanes(f, 2) - lanes(f, 1))
                changes[i].append(jnp.where(level.astype(F32) < px[2 * packs], change, 0.0))

        ends_x = jnp.logical_or(lane < 2, lane > 125)

        for slot in range(16):
            for m in range(packs):
                for i in range(2):
                    k = packs * (slot // groups) + m
                    at = pl.ds(8 * (slot % groups), 8)
                    change = jnp.where(ends_x, lanes(changes[i][m], -(SLOT * slot + MID)), 0.0)
                    outs[i][k, at] = outs[i][k, at] + change

        when(jnp.logical_not(late_west), north_rows)

        for copy in eastward:
            copy.wait_send()
        westward.wait_send()

        @pl.when(has_south)
        def _():
            for copy in southward:
                copy.wait_send()

        @pl.when(has_north)
        def _():
            for copy in northward:
                copy.wait_send()

        @pl.when(top)
        def _():
            for copy in folded:
                copy.wait_send()

        @pl.when(top_far)
        def _():
            folded_next.wait_send()

    return kernel


def make_edge_kernel(levels, rows):
    top_row = PAD + rows

    def kernel(t_part, s_part, q, v, n, hp, hn, t_out, s_out, done, sem, end_sem):
        parts = (t_part, s_part)
        outs = (t_out, s_out)
        row = lax.broadcasted_iota(I32, (8, 128), 0)
        rest, end = pl.ds(0, rows - 8), pl.ds(rows - 8, 8)
        stores = [pltpu.make_async_copy(parts[i].at[:, rest], outs[i].at[:, rest], sem.at[i]) for i in range(2)]
        for store in stores:
            store.start()

        cells = jnp.where(row > 5, n[pl.ds(top_row - 8, 8)], 0)

        def put(i, k, change):
            done[i, k] = parts[i][k, end] + jnp.where(k < cells, change, 0.0)

        edge_rows(True, q, v, n, lambda i, m: hp[i, m], None, hn[...], levels, rows, put)

        ends = [pltpu.make_async_copy(done.at[i], outs[i].at[:, end], end_sem.at[i]) for i in range(2)]
        for store in ends:
            store.start()
        for store in stores + ends:
            store.wait()

    return kernel


def solution(mesh):
    nlon, nlat = mesh.shape["lon"], mesh.shape["lat"]

    def body(t, s, u, v, n):
        levels, rows, cols = t.shape
        packs = levels // (16 // (rows // 8))
        tall = rows + 2 * PAD
        plain = jax.ShapeDtypeStruct((levels, rows, cols), F32)
        parts = pl.pallas_call(
            make_kernel(nlon, nlat, levels, rows),
            out_shape=(
                pltpu.VMEM((levels, rows, cols), F32),
                pltpu.VMEM((levels, rows, cols), F32),
                pltpu.VMEM((2, levels, tall, cols), F32),
                pltpu.VMEM((levels, tall, cols), F32),
                pltpu.VMEM((tall, cols), I32),
                pltpu.VMEM((2, levels // 2, 8, cols), F32),
                pltpu.VMEM((8, cols), I32),
            ),
            in_specs=[pl.BlockSpec(memory_space=pl.ANY)] * 5,
            out_specs=(pl.BlockSpec(memory_space=pltpu.VMEM),) * 7,
            scratch_shapes=[
                pltpu.VMEM((2, levels, 8, cols), F32),
                pltpu.VMEM((levels, 8, cols), F32),
                pltpu.VMEM((8, cols), I32),
                pltpu.VMEM((2, levels, 8, cols), F32),
                pltpu.VMEM((8, cols), I32),
                pltpu.VMEM((levels, tall, cols), F32),
                pltpu.VMEM((levels, rows, cols), F32),
                pltpu.VMEM((rows, cols), I32),
                pltpu.VMEM((rows, cols), I32),
                pltpu.VMEM((tall, cols), I32),
                pltpu.VMEM((rows, cols), I32),
                pltpu.VMEM((2, rows + 8, cols), F32),
                pltpu.VMEM((3 * packs + 1, 8, cols), F32),
                pltpu.VMEM((packs, 8, cols), F32),
                pltpu.VMEM((packs, 8, cols), F32),
                pltpu.VMEM((packs, 8, cols), F32),
                pltpu.VMEM((packs, 8, cols), F32),
                pltpu.VMEM((2, levels, 8, cols), F32),
                pltpu.VMEM((packs, 8, cols), F32),
                pltpu.VMEM((8, cols), I32),
                pltpu.SemaphoreType.DMA((6,)),
                pltpu.SemaphoreType.DMA((14 + packs,)),
                pltpu.SemaphoreType.DMA((14 + packs,)),
                pltpu.SemaphoreType.REGULAR((7,)),
            ],
            compiler_params=pltpu.CompilerParams(collective_id=0, has_side_effects=True),
            name="tracer_step",
        )(t, s, u, v, n)
        return pl.pallas_call(
            make_edge_kernel(levels, rows),
            out_shape=(plain, plain),
            in_specs=[pl.BlockSpec(memory_space=pltpu.VMEM)] * 7,
            out_specs=(pl.BlockSpec(memory_space=pl.ANY),) * 2,
            scratch_shapes=[
                pltpu.VMEM((2, levels, 8, cols), F32),
                pltpu.SemaphoreType.DMA((2,)),
                pltpu.SemaphoreType.DMA((2,)),
            ],
            name="edge_rows",
        )(*[pltpu.with_memory_space_constraint(part, pltpu.VMEM) for part in parts])

    spec = P(None, "lat", "lon")
    return jax.shard_map(
        body, mesh=mesh, in_specs=(spec,) * 4 + (P("lat", "lon"),), out_specs=(spec, spec), check_vma=False
    )
```

```python
import jax
import jax.numpy as jnp
from jax import lax
from jax.experimental import pallas as pl
from jax.experimental.pallas import tpu as pltpu
from jax.sharding import PartitionSpec as P

ALPHA = 0.1655
BETA = 0.76554
CABBELING = 0.05952
LAMBDA_SALT = 0.00054914
THERMOBARIC = 0.0001497
PRESS_SALT = 1.109e-05
CROSS = 0.0024341
TOTAL_DEPTH = 5000.0
KAPPA = 0.1
SLOPE_MAX = 1.0
STRAT_MIN = 0.1

MESH = pl.DeviceIdType.MESH
F32 = jnp.float32
I32 = jnp.int32

PAD = 8
SLOT = 8
MID = 3


def density(t, s, z):
    lead = -ALPHA - (ALPHA * THERMOBARIC) * z
    salt = BETA - (BETA * PRESS_SALT) * z
    return t * (lead + (-0.5 * ALPHA * CABBELING) * t - CROSS * s) + s * (salt - (0.5 * BETA * LAMBDA_SALT) * s)


def slope_term(rho_diff, rho_zsum, half_scale):
    strat = jnp.maximum(half_scale * rho_zsum, STRAT_MIN)
    slope = jnp.clip(-rho_diff / strat, -SLOPE_MAX, SLOPE_MAX)
    return slope * (KAPPA * half_scale)


def courant_terms(c):
    up = c > 0.0
    coef = jnp.where(up, 0.5, -0.5) - 0.5 * c
    return up, coef


def tracer_flux(face, c, up, coef, sk, qa, qb, d, back, ahead, zsum):
    step = jnp.where(up, back, ahead)
    limited = jnp.minimum(jnp.maximum(step, jnp.minimum(d, 0.0)), jnp.maximum(d, 0.0))
    adv = c * (jnp.where(up, qa, qb) + coef * limited)
    return jnp.where(face, adv - (KAPPA * d + sk * zsum), 0.0)


def lanes(x, shift):
    return pltpu.roll(x, shift % 128, axis=x.ndim - 1)


def rows_by(x, shift):
    return pltpu.roll(x, shift % 8, axis=x.ndim - 2)


def edge_rows(north, q, v, n, halo, halo_v, halo_n, levels, rows, emit):
    top_row = PAD + rows
    hop = levels // 2
    row = lax.broadcasted_iota(I32, (8, 128), 0)
    low, place = row < 4, row % 4

    def own(load, m, base):
        return jnp.where(low, load(m, base), load(m + hop, base - 4))

    def pair(halo, load, m):
        if north:
            a = jnp.where(place == 3, rows_by(halo, 1), own(load, m, top_row - 3))
            b = jnp.where(place > 1, halo, own(load, m, top_row - 2))
        else:
            a = jnp.where(place < 2, halo, own(load, m, PAD - 2))
            b = jnp.where(place < 1, rows_by(halo, -1), own(load, m, PAD - 1))
        return a, b

    def load_v(k, base):
        return v[k, pl.ds(base, 8)]

    face_n = jnp.minimum(*pair(halo_n, lambda k, base: n[pl.ds(base, 8)], 0))
    keep_n = jnp.where(jnp.logical_or(place == 1, place == 2), face_n, 0)

    def level(m):
        z = jnp.where(low, TOTAL_DEPTH * (m + 0.5) / levels, TOTAL_DEPTH * (m + hop + 0.5) / levels)
        t, s = [pair(halo(i, m), lambda k, base, i=i: q[i, k, pl.ds(base, 8)], m) for i in range(2)]
        ra, rb = [density(t[j], s[j], z) for j in range(2)]
        return (t, s), (t[0] + t[1], s[0] + s[1], ra + rb), rb - ra

    held = [level(m) for m in range(hop)]
    for m in range(hop):
        tracers, sums, rho_diff = held[m]
        zsums = []
        for j in range(3):
            above = held[m + 1][1][j] if m + 1 < hop else jnp.where(low, rows_by(held[0][1][j], 4), sums[j])
            below = held[m - 1][1][j] if m > 0 else jnp.where(low, sums[j], rows_by(held[hop - 1][1][j], 4))
            zsums.append(above - below)
        half_scale = 0.25
        if m == 0:
            half_scale = jnp.where(low, 0.5, 0.25)
        if m == hop - 1:
            half_scale = jnp.where(low, 0.25, 0.5)
        k = jnp.where(low, m, m + hop)
        wet, keep = k < face_n, k < keep_n
        c = own(load_v, m, top_row - 3) if north else jnp.where(place < 2, halo_v(m), own(load_v, m, PAD - 2))
        up, coef = courant_terms(c)
        sk = slope_term(rho_diff, zsums[2], half_scale)
        for i in range(2):
            qa, qb = tracers[i]
            d = jnp.where(wet, qb - qa, 0.0)
            f = tracer_flux(keep, c, up, coef, sk, qa, qb, d, rows_by(d, 1), rows_by(d, -1), zsums[i])
            change = f - rows_by(f, -1)
            emit(i, m, rows_by(change, 6 if north else -1))
            emit(i, m + hop, rows_by(change, 2 if north else 3))


def make_kernel(nlon, nlat, levels, rows):
    groups = rows // 8
    per = 16 // groups
    packs = levels // per
    span = SLOT * groups
    top_row = PAD + rows

    def depth(k):
        return TOTAL_DEPTH * (k + 0.5) / levels

    def kernel(
        t_hbm, s_hbm, u_hbm, v_hbm, n_hbm,
        t_out, s_out, q, v, n, hp, hn,
        h, hv, hs, h_north, hs_north, rho, u, face_x, keep_x, face_y, keep_y, fy,
        px, to_e, to_w, from_w, from_e, fa, fb, fan,
        load_sem, send_sem, recv_sem, late_ready,
    ):
        lon = lax.axis_index("lon")
        lat = lax.axis_index("lat")
        east = lax.rem(lon + 1, nlon)
        west = lax.rem(lon + nlon - 1, nlon)
        has_south = lat > 0
        has_north = lat < nlat - 1
        top = lat == nlat - 1
        mirror = nlon - 1 - lon
        mirror_next = lax.rem(nlon - lon, nlon)
        mirror_far = mirror_next != lon
        top_far = jnp.logical_and(top, mirror_far)
        top_self = jnp.logical_and(top, jnp.logical_not(mirror_far))
        below_top = lat == nlat - 2
        plain = jnp.logical_not(top)
        half, quarter = nlon // 2, nlon // 4
        place = lax.rem(lon, half)
        early = place < quarter
        late_west = place == 0
        late_east = place == quarter - 1
        early_west = place == quarter
        early_east = place == half - 1
        odd = lax.rem(lat, 2) == 1
        skew_odd = jnp.logical_and(early_east, jnp.logical_and(odd, plain))
        skew_even = jnp.logical_and(early_east, jnp.logical_and(jnp.logical_not(odd), plain))
        level_pair = jnp.logical_not(early_east)
        prompt = jnp.logical_or(top, jnp.logical_and(skew_even, jnp.logical_not(below_top)))
        mirror_late = jnp.logical_and(top, early)
        mirror_early = jnp.logical_and(top, jnp.logical_not(early))
        next_late = jnp.logical_and(top_far, early)
        next_early = jnp.logical_and(top_far, place > quarter)
        next_same = jnp.logical_and(top_far, place == quarter)

        barrier = pltpu.get_barrier_semaphore()

        def greet(device):
            pl.semaphore_signal(barrier, inc=1, device_id=device, device_id_type=MESH)

        def when(condition, *steps):
            @pl.when(condition)
            def _():
                for step in steps:
                    step()

        def both(a, b):
            return jnp.logical_or(a, b)

        def also(a, b):
            return jnp.logical_and(a, b)

        body_rows = pl.ds(PAD, rows)
        loads = [
            pltpu.make_async_copy(n_hbm, n.at[body_rows], load_sem.at[0]),
            pltpu.make_async_copy(t_hbm, q.at[0, :, body_rows], load_sem.at[1]),
            pltpu.make_async_copy(s_hbm, q.at[1, :, body_rows], load_sem.at[2]),
            pltpu.make_async_copy(u_hbm, u, load_sem.at[3]),
            pltpu.make_async_copy(v_hbm, v.at[:, body_rows], load_sem.at[4]),
        ]
        for load in loads[:4]:
            load.start()

        when(also(has_south, jnp.logical_not(skew_odd)), lambda: greet({"lat": lat - 1}))
        northern = jnp.logical_not(both(skew_odd, below_top))
        when(also(has_north, northern), lambda: greet({"lat": lat + 1}))
        when(mirror_late, lambda: greet({"lon": mirror}))
        when(both(next_late, next_same), lambda: greet({"lon": mirror_next}))
        when(jnp.logical_not(early_east), lambda: greet({"lon": east}))
        when(jnp.logical_not(early_west), lambda: greet({"lon": west}))

        loads[4].start()

        lane = lax.broadcasted_iota(I32, (8, 128), 1)
        row = lax.broadcasted_iota(I32, (8, 128), 0)
        slot_of = lane // SLOT
        sl = lane % SLOT

        greetings = (
            also(has_south, both(skew_odd, also(level_pair, plain))), also(has_north, both(both(skew_odd, below_top), level_pair)), mirror_early, both(next_early, next_same),
            jnp.logical_not(late_west), jnp.logical_not(late_east),
        )

        def meet():
            pl.semaphore_wait(barrier, sum(one.astype(I32) for one in greetings))

        def tell(index, device):
            return lambda: pl.semaphore_signal(
                late_ready.at[index], inc=1, device_id=device, device_id_type=MESH
            )

        def remote(src, dst, index, device):
            return pltpu.make_async_remote_copy(
                src_ref=src, dst_ref=dst, send_sem=send_sem.at[index], recv_sem=recv_sem.at[index],
                device_id=device, device_id_type=MESH,
            )

        first, last = pl.ds(0, 2), pl.ds(rows - 2, 2)
        fold = pl.ds(rows - 3, 2)
        fold_in_group = pl.ds(5, 2)
        lo, hi = pl.ds(0, 2), pl.ds(6, 2)
        northward = [
            remote(t_hbm.at[:, last], h.at[0, :, lo], 0, {"lat": lat + 1}),
            remote(s_hbm.at[:, last], h.at[1, :, lo], 1, {"lat": lat + 1}),
            remote(v_hbm.at[:, pl.ds(rows - 1, 1)], hv.at[:, pl.ds(1, 1)], 2, {"lat": lat + 1}),
            remote(n_hbm.at[last], hs.at[lo], 3, {"lat": lat + 1}),
        ]
        southward = [
            remote(t_hbm.at[:, first], h_north.at[0, :, hi], 4, {"lat": lat - 1}),
            remote(s_hbm.at[:, first], h_north.at[1, :, hi], 5, {"lat": lat - 1}),
            remote(n_hbm.at[first], hs_north.at[hi], 6, {"lat": lat - 1}),
        ]
        folded = [
            remote(t_hbm.at[:, fold], fa.at[0, :, hi], 7, {"lon": mirror}),
            remote(s_hbm.at[:, fold], fa.at[1, :, hi], 8, {"lon": mirror}),
            remote(n_hbm.at[fold], fan.at[hi], 9, {"lon": mirror}),
        ]
        folded_next = remote(to_w.at[:, fold_in_group], fb.at[:, hi], 10, {"lon": mirror_next})
        own_next = pltpu.make_async_copy(to_w.at[:, fold_in_group], fb.at[:, hi], load_sem.at[5])
        eastward = [remote(to_e.at[m], from_w.at[m], 12 + m, {"lon": east}) for m in range(packs)]
        westward = remote(to_w, from_e, 11, {"lon": west})

        def tell_even():
            when(also(skew_odd, has_north), tell(5, {"lat": lat + 1}))
            when(also(skew_odd, has_south), tell(6, {"lat": lat - 1}))

        @pl.when(prompt)
        def _():
            meet()
            when(mirror_early, *[copy.start for copy in folded], tell(0, {"lon": mirror}))
            when(next_early, tell(1, {"lon": mirror_next}))
            when(early_east, tell(2, {"lon": east}))
            when(also(top, early_west), tell(3, {"lon": west}))

        loads[0].wait()
        packed_n = jnp.zeros((8, 128), F32)
        for slot in range(16):
            part = n[pl.ds(PAD + 8 * (slot % groups), 8)].astype(F32)
            packed_n = jnp.where(slot_of == slot, lanes(part, SLOT * slot + MID), packed_n)
        px[2 * packs] = packed_n
        n_up, n_down = lanes(packed_n, 5), lanes(packed_n, -2)

        for load in loads[1:4]:
            load.wait()
        prompt_east = also(prompt, jnp.logical_not(late_east))
        for m in range(packs):
            packed = []
            for field in range(3):
                one = jnp.zeros((8, 128), F32)
                for slot in range(16):
                    k = packs * (slot // groups) + m
                    g = slot % groups
                    if field < 2:
                        part = q[field, k, pl.ds(PAD + 8 * g, 8)]
                    else:
                        part = u[k, pl.ds(8 * g, 8)]
                    one = jnp.where(slot_of == slot, lanes(part, SLOT * slot + MID), one)
                px[(0, packs, 2 * packs + 1)[field] + m] = one
                packed.append(one)
            t2, s2, u2 = packed
            s_up = lanes(s2, 2)
            to_e[m] = jnp.where(sl < 3, t2, jnp.where(sl < 5, s_up, jnp.where(sl < 6, lanes(u2, 3), n_up)))
            to_w[m] = jnp.where(sl < 3, n_down, jnp.where(sl < 5, t2, s_up))
            if m > 0:
                when(prompt_east, eastward[m - 1].start)

        when(top_self, own_next.start)
        @pl.when(prompt)
        def _():
            when(both(next_early, next_same), folded_next.start)
            when(jnp.logical_not(late_east), eastward[-1].start)
            when(jnp.logical_not(late_west), westward.start)

        @pl.when(jnp.logical_not(prompt))
        def _():
            meet()
            when(jnp.logical_not(late_east), *[copy.start for copy in eastward])
            when(jnp.logical_not(late_west), westward.start)
            when(early_east, tell(2, {"lon": east}))
            when(early_west, tell(3, {"lon": west}))
            tell_even()
            when(below_top, tell(4, {"lat": lat + 1}))
            when(also(has_south, jnp.logical_not(skew_even)), *[copy.start for copy in southward])
            when(has_north, *[copy.start for copy in northward])

        @pl.loop(0, levels)
        def _(k):
            z = depth(k.astype(F32))
            for g in range(groups):
                at = pl.ds(PAD + 8 * g, 8)
                rho[k, at] = density(q[0, k, at], q[1, k, at], z)

        pad_n = jnp.zeros((8, 128), I32)
        n[pl.ds(0, 8)] = pad_n
        n[pl.ds(top_row, 8)] = pad_n
        for g in range(groups):
            at = pl.ds(PAD + 8 * g, 8)
            here = n[at]
            fx = jnp.minimum(here, lanes(here, 1))
            face_x[pl.ds(8 * g, 8)] = fx
            inner = jnp.logical_and(lane > 1, lane < 127)
            keep_x[pl.ds(8 * g, 8)] = jnp.where(inner, fx, 0)
            f = jnp.minimum(here, n[pl.ds(PAD + 8 * g - 1, 8)])
            face_y[at] = f
            if g == 0:
                f = jnp.where(row > 1, f, 0)
            if g == groups - 1:
                f = jnp.where(row < 7, f, 0)
            keep_y[pl.ds(8 * g, 8)] = f
        face_y[pl.ds(0, 8)] = pad_n
        face_y[pl.ds(top_row, 8)] = pad_n

        outs = (t_out, s_out)
        loads[4].wait()
        fy[0, pl.ds(rows, 8)] = jnp.zeros((8, 128), F32)
        fy[1, pl.ds(rows, 8)] = jnp.zeros((8, 128), F32)

        def interior(k):
            kp = jnp.minimum(k + 1, levels - 1)
            km = jnp.maximum(k - 1, 0)
            ends = jnp.logical_or(k == 0, k == levels - 1)
            half_scale = jnp.where(ends, 0.5, 0.25).astype(F32)

            for g in reversed(range(groups)):
                r = PAD + 8 * g
                at, dn = pl.ds(r, 8), pl.ds(r - 1, 8)
                t0 = [q[i, k, at] for i in range(2)]
                zd = [q[i, kp, at] - q[i, km, at] for i in range(2)]
                rho0 = rho[k, at]
                rz = rho[kp, at] - rho[km, at]

                wet = k < face_x[pl.ds(8 * g, 8)]
                keep = k < keep_x[pl.ds(8 * g, 8)]
                c = lanes(u[k, pl.ds(8 * g, 8)], 1)
                up, coef = courant_terms(c)
                sk = slope_term(rho0 - lanes(rho0, 1), rz + lanes(rz, 1), half_scale)
                total = []
                for i in range(2):
                    qa = lanes(t0[i], 1)
                    d = jnp.where(wet, t0[i] - qa, 0.0)
                    f = tracer_flux(keep, c, up, coef, sk, qa, t0[i], d, lanes(d, 1), lanes(d, -1), zd[i] + lanes(zd[i], 1))
                    total.append(t0[i] + (f - lanes(f, -1)))

                wet = k < face_y[at]
                wet_back = k < face_y[dn]
                wet_ahead = k < face_y[pl.ds(r + 1, 8)]
                keep = k < keep_y[pl.ds(8 * g, 8)]
                c = v[k, dn]
                up, coef = courant_terms(c)
                sk = slope_term(rho0 - rho[k, dn], rz + (rho[kp, dn] - rho[km, dn]), half_scale)
                here = k < n[at]
                for i in range(2):
                    qa = q[i, k, dn]
                    d = jnp.where(wet, t0[i] - qa, 0.0)
                    back = jnp.where(wet_back, qa - q[i, k, pl.ds(r - 2, 8)], 0.0)
                    ahead = jnp.where(wet_ahead, q[i, k, pl.ds(r + 1, 8)] - t0[i], 0.0)
                    zsum = zd[i] + (q[i, kp, dn] - q[i, km, dn])
                    f = tracer_flux(keep, c, up, coef, sk, qa, t0[i], d, back, ahead, zsum)
                    fy[i, pl.ds(8 * g, 8)] = f
                    f_north = fy[i, pl.ds(8 * g + 1, 8)]
                    outs[i][k, pl.ds(8 * g, 8)] = jnp.where(here, total[i] + (f - f_north), 0.0)

        def heard(index):
            return lambda: pl.semaphore_wait(late_ready.at[index], 1)

        pl.loop(0, levels // 2)(interior)
        when(top, heard(4), *[copy.start for copy in southward])
        pl.loop(levels // 2, levels)(interior)

        when(also(skew_even, has_south), heard(5), *[copy.start for copy in southward])
        when(also(skew_even, jnp.logical_not(below_top)), heard(6), *[copy.start for copy in northward])
        when(late_east, heard(3), *[copy.start for copy in eastward])
        when(late_west, heard(2), westward.start)
        when(mirror_late, heard(0), *[copy.start for copy in folded])
        when(next_late, heard(1), folded_next.start)

        hop = levels // 2
        low = row < 4

        @pl.when(jnp.logical_not(has_south))
        def _():
            hs[lo] = jnp.zeros((2, 128), I32)

            @pl.loop(0, levels)
            def _(k):
                h[0, k, lo] = jnp.zeros((2, 128), F32)
                h[1, k, lo] = jnp.zeros((2, 128), F32)
                hv[k, lo] = jnp.zeros((2, 128), F32)

        when(has_south, *[copy.wait_recv for copy in northward])
        cells = jnp.where(row < 2, n[pl.ds(PAD, 8)], 0)

        def put(i, k, change):
            outs[i][k, pl.ds(0, 8)] = outs[i][k, pl.ds(0, 8)] + jnp.where(k < cells, change, 0.0)

        edge_rows(
            False, q, v, n,
            lambda i, m: jnp.where(low, h[i, m], rows_by(h[i, m + hop], 4)),
            lambda m: jnp.where(low, hv[m], rows_by(hv[m + hop], 4)),
            jnp.where(low, hs[...], rows_by(hs[...], 4)),
            levels, rows, put,
        )

        def north_rows():
            when(has_north, *[copy.wait_recv for copy in southward])
            when(top, *[copy.wait_recv for copy in folded])
            when(top_far, folded_next.wait_recv)
            when(top_self, own_next.wait)

            @pl.when(has_north)
            def _():
                hn[...] = jnp.where(low, rows_by(hs_north[...], -4), hs_north[...])
                for m in range(hop):
                    for i in range(2):
                        hp[i, m] = jnp.where(low, rows_by(h_north[i, m], -4), h_north[i, m + hop])

            @pl.when(top)
            def _():
                order = lax.rem(128 - lane, 128)
                spot = SLOT * (groups - 1) + MID

                def mirrored(x):
                    x = jnp.where(row % 2 == 0, rows_by(x, -1), rows_by(x, 1))
                    return jnp.take_along_axis(x, order, axis=1)

                x = jnp.where(lane == 0, lanes(fb[0], -(spot - 2)), fan[...].astype(F32))
                hn[...] = mirrored(jnp.where(low, rows_by(x, -4), x)).astype(I32)
                for m in range(packs):
                    next_cells = jnp.where(low, rows_by(fb[m], -4), lanes(fb[m], -span * (hop // packs)))
                    for part in range(hop // packs):
                        k = packs * part + m
                        for i in range(2):
                            x = jnp.where(low, rows_by(fa[i, k], -4), fa[i, k + hop])
                            x = jnp.where(lane == 0, lanes(next_cells, -(span * part + spot + 2 * i)), x)
                            hp[i, k] = mirrored(x)

        when(late_west, north_rows)

        for copy in eastward:
            copy.wait_recv()
        westward.wait_recv()

        def joined(own, before, after, by_west, by_east):
            a_west = jnp.where(sl < 2, lanes(before, by_west - 1), lanes(own, -1))
            a_east = jnp.where(sl < 7, lanes(own, 4), lanes(after, by_east + 4))
            b_west = jnp.where(sl < 1, lanes(before, by_west - 2), lanes(own, -2))
            b_east = jnp.where(sl < 6, lanes(own, 3), lanes(after, by_east + 3))
            return jnp.where(sl < 4, a_west, a_east), jnp.where(sl < 4, b_west, b_east)

        na, nb = joined(px[2 * packs], from_w[0], from_e[0], -5, 2)
        face_n = jnp.minimum(na, nb)
        level_of = packs * (lane // span)
        pairs = [
            [joined(px[m], from_w[m], from_e[m], 0, 0) for m in range(packs)],
            [joined(px[packs + m], from_w[m], from_e[m], -2, -2) for m in range(packs)],
        ]
        rho_pairs = []
        for m in range(packs):
            z = depth((level_of + m).astype(F32))
            rho_pairs.append([density(pairs[0][m][j], pairs[1][m][j], z) for j in range(2)])
        sums = [[a + b for a, b in one] for one in (*pairs, rho_pairs)]

        def zsum_of(one, m):
            if m < packs - 1:
                above = one[m + 1]
            else:
                above = jnp.where(lane < 128 - span, lanes(one[0], -span), one[m])
            if m > 0:
                below = one[m - 1]
            else:
                below = jnp.where(lane < span, one[0], lanes(one[packs - 1], span))
            return above - below

        used = jnp.logical_or(jnp.logical_or(sl == 1, sl == 2), jnp.logical_or(sl == 5, sl == 6))
        changes = [[], []]
        for m in range(packs):
            level = level_of + m
            half_scale = jnp.where(jnp.logical_or(level == 0, level == levels - 1), 0.5, 0.25)
            wet = level.astype(F32) < face_n
            keep = jnp.logical_and(wet, used)
            u2 = px[2 * packs + 1 + m]
            c = jnp.where(sl < 4, jnp.where(sl < 2, lanes(from_w[m], -4), lanes(u2, -1)), lanes(u2, 4))
            up, coef = courant_terms(c)
            sk = slope_term(rho_pairs[m][1] - rho_pairs[m][0], zsum_of(sums[2], m), half_scale)
            for i in range(2):
                qa, qb = pairs[i][m]
                d = jnp.where(wet, qb - qa, 0.0)
                f = tracer_flux(keep, c, up, coef, sk, qa, qb, d, lanes(d, 1), lanes(d, -1), zsum_of(sums[i], m))
                change = jnp.where(sl < MID, lanes(f, -3) - lanes(f, -4), lanes(f, 2) - lanes(f, 1))
                changes[i].append(jnp.where(level.astype(F32) < px[2 * packs], change, 0.0))

        ends_x = jnp.logical_or(lane < 2, lane > 125)

        for slot in range(16):
            for m in range(packs):
                for i in range(2):
                    k = packs * (slot // groups) + m
                    at = pl.ds(8 * (slot % groups), 8)
                    change = jnp.where(ends_x, lanes(changes[i][m], -(SLOT * slot + MID)), 0.0)
                    outs[i][k, at] = outs[i][k, at] + change

        when(jnp.logical_not(late_west), north_rows)

        for copy in eastward:
            copy.wait_send()
        westward.wait_send()

        @pl.when(has_south)
        def _():
            for copy in southward:
                copy.wait_send()

        @pl.when(has_north)
        def _():
            for copy in northward:
                copy.wait_send()

        @pl.when(top)
        def _():
            for copy in folded:
                copy.wait_send()

        @pl.when(top_far)
        def _():
            folded_next.wait_send()

    return kernel


def make_edge_kernel(levels, rows):
    top_row = PAD + rows

    def kernel(t_part, s_part, q, v, n, hp, hn, t_out, s_out, done, sem, end_sem):
        parts = (t_part, s_part)
        outs = (t_out, s_out)
        row = lax.broadcasted_iota(I32, (8, 128), 0)
        rest, end = pl.ds(0, rows - 8), pl.ds(rows - 8, 8)
        stores = [pltpu.make_async_copy(parts[i].at[:, rest], outs[i].at[:, rest], sem.at[i]) for i in range(2)]
        for store in stores:
            store.start()

        cells = jnp.where(row > 5, n[pl.ds(top_row - 8, 8)], 0)

        def put(i, k, change):
            done[i, k] = parts[i][k, end] + jnp.where(k < cells, change, 0.0)

        edge_rows(True, q, v, n, lambda i, m: hp[i, m], None, hn[...], levels, rows, put)

        ends = [pltpu.make_async_copy(done.at[i], outs[i].at[:, end], end_sem.at[i]) for i in range(2)]
        for store in ends:
            store.start()
        for store in stores + ends:
            store.wait()

    return kernel


def solution(mesh):
    nlon, nlat = mesh.shape["lon"], mesh.shape["lat"]

    def body(t, s, u, v, n):
        levels, rows, cols = t.shape
        packs = levels // (16 // (rows // 8))
        tall = rows + 2 * PAD
        plain = jax.ShapeDtypeStruct((levels, rows, cols), F32)
        parts = pl.pallas_call(
            make_kernel(nlon, nlat, levels, rows),
            out_shape=(
                pltpu.VMEM((levels, rows, cols), F32),
                pltpu.VMEM((levels, rows, cols), F32),
                pltpu.VMEM((2, levels, tall, cols), F32),
                pltpu.VMEM((levels, tall, cols), F32),
                pltpu.VMEM((tall, cols), I32),
                pltpu.VMEM((2, levels // 2, 8, cols), F32),
                pltpu.VMEM((8, cols), I32),
            ),
            in_specs=[pl.BlockSpec(memory_space=pl.ANY)] * 5,
            out_specs=(pl.BlockSpec(memory_space=pltpu.VMEM),) * 7,
            scratch_shapes=[
                pltpu.VMEM((2, levels, 8, cols), F32),
                pltpu.VMEM((levels, 8, cols), F32),
                pltpu.VMEM((8, cols), I32),
                pltpu.VMEM((2, levels, 8, cols), F32),
                pltpu.VMEM((8, cols), I32),
                pltpu.VMEM((levels, tall, cols), F32),
                pltpu.VMEM((levels, rows, cols), F32),
                pltpu.VMEM((rows, cols), I32),
                pltpu.VMEM((rows, cols), I32),
                pltpu.VMEM((tall, cols), I32),
                pltpu.VMEM((rows, cols), I32),
                pltpu.VMEM((2, rows + 8, cols), F32),
                pltpu.VMEM((3 * packs + 1, 8, cols), F32),
                pltpu.VMEM((packs, 8, cols), F32),
                pltpu.VMEM((packs, 8, cols), F32),
                pltpu.VMEM((packs, 8, cols), F32),
                pltpu.VMEM((packs, 8, cols), F32),
                pltpu.VMEM((2, levels, 8, cols), F32),
                pltpu.VMEM((packs, 8, cols), F32),
                pltpu.VMEM((8, cols), I32),
                pltpu.SemaphoreType.DMA((6,)),
                pltpu.SemaphoreType.DMA((12 + packs,)),
                pltpu.SemaphoreType.DMA((12 + packs,)),
                pltpu.SemaphoreType.REGULAR((7,)),
            ],
            compiler_params=pltpu.CompilerParams(collective_id=0, has_side_effects=True),
            name="tracer_step",
        )(t, s, u, v, n)
        return pl.pallas_call(
            make_edge_kernel(levels, rows),
            out_shape=(plain, plain),
            in_specs=[pl.BlockSpec(memory_space=pltpu.VMEM)] * 7,
            out_specs=(pl.BlockSpec(memory_space=pl.ANY),) * 2,
            scratch_shapes=[
                pltpu.VMEM((2, levels, 8, cols), F32),
                pltpu.SemaphoreType.DMA((2,)),
                pltpu.SemaphoreType.DMA((2,)),
            ],
            name="edge_rows",
        )(*[pltpu.with_memory_space_constraint(part, pltpu.VMEM) for part in parts])

    spec = P(None, "lat", "lon")
    return jax.shard_map(
        body, mesh=mesh, in_specs=(spec,) * 4 + (P("lat", "lon"),), out_specs=(spec, spec), check_vma=False
    )
```
